32 devices in a mesh: grp: 2 (over x), hor: 8 (over z, y), dep: 2 (over core).
Axes of the slice: x: 2, y: 2, z: 4, core: 2. Of those that a mesh axis runs over, the one named last changes fastest.
Arguments:
- residual: float32 [64, 64, 1024], P(('grp', 'dep'), 'hor'), parts along dimension 0, may hold values from -6 to 6
- focus_bins: int32 [64, 64, 1024], P(('grp', 'dep'), 'hor'), parts along dimension 0, may hold values from 0 to 15
- layer_class: int32 [64], P('grp'), parts along dimension 0, may hold values from 0 to 7
Outputs:
- preconditioned: float32 [64, 64, 1024], P(('grp', 'dep'), 'hor'), parts along dimension 0
The draws below stay inside these ranges and needn't reach their ends.
There are 2 independent parts, one for each index of `grp`. The reference program is written for one: setup_inputs(seed, part) draws one part's arguments, and reference() takes and returns one part's arrays. A program takes and returns all parts, laid end to end along the dimension named above; each array names one. Nothing has to cross between parts.
All inputs are finite; a program needn't handle non-finite values.
Results may differ from the reference program's by a relative error of at most 0.0003.
Values sent between devices are 32-bit elements; how exact they have to be, the bound alone decides.
No kernel may reach another device: no remote copies, remote signals or barrier semaphores. Data moves between devices by JAX's collectives and lax.ppermute only.
A program may use at most 128 MiB of HBM per device.

```python
import math
import jax
import jax.numpy as jnp
from jax import lax

NZ = 32
NX = 1024
NY = 64
NCLASS = 8
NBINS = 16


def place_ends(drawn, stream_key, least, largest):
    spot = [jax.random.randint(jax.random.fold_in(stream_key, axis), (), 0, length) for axis, length in enumerate(drawn.shape)]
    main_axis = drawn.shape.index(max(drawn.shape))
    next_to = spot[:main_axis] + [(spot[main_axis] + 1) % drawn.shape[main_axis]] + spot[main_axis + 1:]
    return drawn.at[tuple(spot)].set(least).at[tuple(next_to)].set(largest)


def steps_of(key, dims, cuts, least, largest):
    gain, own = 1.0, jax.random.fold_in(key, 6)
    for axis_at, blocks in cuts:
        draws = jnp.exp(jax.random.uniform(jax.random.fold_in(own, axis_at), (blocks,), jnp.float32, least / len(cuts), largest / len(cuts)))
        gain = gain * jnp.repeat(draws, dims[axis_at] // blocks).reshape([-1 if axis == axis_at else 1 for axis in range(len(dims))])
    return gain


def bell_draw(rng, dims, width, reach, split=(), kind=jnp.bfloat16):
    factor_of = steps_of(rng, dims, split, -0.22, 0.18) if split else 1.0
    entries = jax.random.normal(rng, dims, jnp.float32) * width * factor_of
    return jnp.minimum(jnp.maximum(entries, -reach), reach).astype(kind)


def setup_inputs(seed: int = 0, part: int = 0) -> dict:
    streams_of = jax.random.split(jax.random.key(seed), 4)
    own_keys = jax.random.split(jax.random.fold_in(streams_of[3], part), 4)
    return {
        "residual": bell_draw(own_keys[0], (NZ, NY, NX), 1.0, 6.0, ((0, 2), (1, 8)), jnp.float32),
        "focus_bins": place_ends(jax.random.randint(own_keys[1], (NZ, NY, NX), 0, NBINS), jax.random.fold_in(own_keys[1], 1), 0, NBINS - 1).astype(jnp.int32),
        "layer_class": place_ends(jax.random.randint(own_keys[2], (NZ,), 0, NCLASS), jax.random.fold_in(own_keys[2], 1), 0, NCLASS - 1).astype(jnp.int32),
    }


damping = 0.01
smoothing = 1.0
coupling_scale = 1.0
weight_base = 0.5
weight_step = 0.2
focus_base = 0.5
focus_step = 0.09242


def depth_weights(layer_class):
    return weight_base * jnp.exp(weight_step * layer_class.astype(jnp.float32))


def focusing(focus_bins):
    return focus_base * jnp.exp(focus_step * focus_bins.astype(jnp.float32))


def couplings(weights):
    inner = coupling_scale * weights[:-1] * weights[1:]
    zero_end = jnp.zeros((1,), jnp.float32)
    return jnp.concatenate([zero_end, inner]), jnp.concatenate([inner, zero_end])


def symbol(frequency, length):
    return 2.0 - 2.0 * jnp.cos(frequency * (2.0 * math.pi / length))


def hartley(values, axis):
    spectrum = jnp.fft.fft(values, axis=axis)
    return jnp.real(spectrum) - jnp.imag(spectrum)


def reference(residual, focus_bins, layer_class):
    focus_map = focusing(focus_bins)
    scaled = focus_map * residual
    spectrum = hartley(hartley(scaled, 2), 1)
    weights = depth_weights(layer_class)
    couple_prev, couple_next = couplings(weights)
    symbol_x = symbol(jnp.arange(NX, dtype=jnp.float32), NX)
    symbol_y = symbol(jnp.arange(NY, dtype=jnp.float32), NY)
    wave_term = damping + smoothing * (symbol_y[:, None] + symbol_x[None, :])

    def forward(carried, inputs):
        prev_upper, prev_source = carried
        layer_plane, weight, lower, upper = inputs
        middle = weight * wave_term + (lower + upper)
        pivots = middle + lower * prev_upper
        now_upper = -upper / pivots
        now_source = (layer_plane + lower * prev_source) / pivots
        return (now_upper, now_source), (now_upper, now_source)

    zero_plane = jnp.zeros((NY, NX), jnp.float32)
    _, (uppers, sources) = lax.scan(forward, (zero_plane, zero_plane), (spectrum, weights, couple_prev, couple_next))

    def backward(following, inputs):
        upper, source = inputs
        result = source - upper * following
        return result, result

    _, solved = lax.scan(backward, zero_plane, (uppers, sources), reverse=True)
    restored = hartley(hartley(solved, 2), 1)
    return focus_map * restored / (NX * NY)
```

```python
import functools
import math

import jax
import jax.numpy as jnp
import ml_dtypes
import numpy as np
from jax import lax
from jax.experimental import pallas as pl
from jax.experimental.pallas import tpu as pltpu
from jax.sharding import PartitionSpec as P

damping = 0.01
smoothing = 1.0
coupling_scale = 1.0
weight_base = 0.5
weight_step = 0.2
focus_base = 0.5
focus_step = 0.09242
lanes = 128
f32 = jnp.float32
bf16 = jnp.bfloat16


def cas(angle):
    return np.cos(angle) + np.sin(angle)


def split_table(table):
    table = table.astype(np.float32)
    high = table.astype(ml_dtypes.bfloat16)
    low = (table - high.astype(np.float32)).astype(ml_dtypes.bfloat16)
    return high, low


def fold_tables(length):
    half = length // 2
    cell = np.arange(half)[:, None]
    tables = []
    for parity in range(2):
        wave = 2 * np.arange(half)[None, :] + parity
        tables.append(cas(2.0 * np.pi * (cell * wave % length) / length))
    return split_table(np.stack(tables))


def sine_matrix(rows):
    index = np.arange(1, rows)
    matrix = np.zeros((rows, rows))
    matrix[0, 0] = 1.0
    matrix[1:, 1:] = np.sqrt(2.0 / rows) * np.sin(np.pi * np.outer(index, index) / rows)
    return matrix


def symbol_of(angle):
    return 2.0 - 2.0 * np.cos(angle)


def split(values):
    high = values.astype(bf16)
    low = (values - high.astype(f32)).astype(bf16)
    return high, low


def dot3(left, right, dims=(((1,), (0,)), ((), ()))):
    dot = functools.partial(lax.dot_general, dimension_numbers=dims, preferred_element_type=f32)
    left_high, left_low = left
    right_high, right_low = right
    return dot(left_high, right_high) + (dot(left_low, right_high) + dot(left_high, right_low))


def focusing(focus_bins):
    return focus_base * jnp.exp(focus_step * focus_bins.astype(f32))


def layer_terms(class_ref, layers, plane_tiles, axis):
    weights = []
    for layer in range(layers):
        level = jnp.full((8, lanes), class_ref[layer], jnp.int32).astype(f32)
        weights.append(weight_base * jnp.exp(weight_step * level))
    couple = [coupling_scale * weights[k] * weights[k + 1] for k in range(layers - 1)]

    def spread(values):
        return [jnp.concatenate([value] * plane_tiles, axis=axis) for value in values]

    return spread(weights), spread(couple)


def diagonal(layer, weights, couple, wave):
    total = weights[layer] * wave
    if layer > 0:
        total = total + couple[layer - 1]
    if layer < len(couple):
        total = total + couple[layer]
    return total


def factor(weights, couple, wave, inverse_ref):
    layers = len(weights)
    half = layers // 2
    top = 1.0 / diagonal(0, weights, couple, wave)
    bottom = 1.0 / diagonal(layers - 1, weights, couple, wave)
    inverse_ref[0] = top
    inverse_ref[layers - 1] = bottom
    for step in range(1, half):
        low = step
        link = couple[low - 1]
        top = 1.0 / (diagonal(low, weights, couple, wave) - link * link * top)
        inverse_ref[low] = top
        high = layers - 1 - step
        link = couple[high]
        pivot = diagonal(high, weights, couple, wave) - link * link * bottom
        if step == half - 1:
            link = couple[half - 1]
            pivot = pivot - link * link * top
        bottom = 1.0 / pivot
        inverse_ref[high] = bottom


def substitute(couple, inverse_ref, partial_ref, source, emit):
    layers = len(couple) + 1
    half = layers // 2
    top = source(0)
    bottom = source(layers - 1)
    partial_ref[0] = top
    partial_ref[layers - 1] = bottom
    for step in range(1, half):
        low = step
        top = source(low) + couple[low - 1] * inverse_ref[low - 1] * top
        partial_ref[low] = top
        high = layers - 1 - step
        bottom = source(high) + couple[high] * inverse_ref[high + 1] * bottom
        partial_ref[high] = bottom
    link = couple[half - 1]
    bottom = (bottom + link * inverse_ref[half - 1] * top) * inverse_ref[half]
    top = (top + link * bottom) * inverse_ref[half - 1]
    emit(half, bottom)
    emit(half - 1, top)
    for step in range(1, half):
        low = half - 1 - step
        top = (partial_ref[low] + couple[low] * top) * inverse_ref[low]
        emit(low, top)
        high = half + step
        bottom = (partial_ref[high] + couple[high - 1] * bottom) * inverse_ref[high]
        emit(high, bottom)


def turn(values, shift):
    shift = shift % lanes
    return values if shift == 0 else pltpu.roll(values, shift, values.ndim - 1)


def fold_kernel(dep_ref, residual_ref, bins_ref, own_ref, send_ref):
    half = own_ref.shape[-1]
    sign = jnp.where(dep_ref[0] == 0, 1.0, -1.0).astype(f32)
    scaled = focusing(bins_ref[...]) * residual_ref[...]
    left = scaled[..., :half]
    right = sign * scaled[..., half:]
    own_ref[...] = left + right
    send_ref[...] = left - right


def interior_kernel(
    dep_ref,
    class_ref,
    own_ref,
    recv_ref,
    table_high,
    table_low,
    sine_high,
    sine_low,
    edge_high,
    edge_low,
    wave_ref,
    packed_ref,
    source_ref,
    inverse_ref,
    stage_ref,
    partial_ref,
):
    depth, rows, half = own_ref.shape
    layers = 2 * depth
    hor_count = packed_ref.shape[0]
    chunk = half // hor_count
    place = dep_ref[0] * depth
    stage_ref[pl.ds(place, depth)] = own_ref[...]
    stage_ref[pl.ds(depth - place, depth)] = recv_ref[...]
    weights, couple = layer_terms(class_ref, layers, half // lanes, 1)
    factor(weights, couple, wave_ref[0], inverse_ref)
    cells = stage_ref[...].reshape(layers * rows, half)
    waves = dot3(split(cells), (table_high[0], table_low[0]))
    block = depth * rows
    sine = (sine_high[...], sine_low[...])
    for part in range(2):
        piece = waves[part * block : (part + 1) * block]
        source_ref[part * depth : (part + 1) * depth] = dot3(sine, split(piece)).reshape(
            depth, rows, half
        )
    edge_row = lax.broadcasted_iota(jnp.int32, (rows, half), 0) == 0

    def emit(layer, values):
        stage_ref[layer] = jnp.where(edge_row, source_ref[layer], weights[layer] * values)

    substitute(couple, inverse_ref, partial_ref, lambda layer: source_ref[layer], emit)
    edge = (edge_high[...], edge_low[...])
    lower = []
    upper = []
    for part in range(2):
        piece = stage_ref[part * depth : (part + 1) * depth].reshape(block, half)
        both = dot3(edge, split(piece))
        lower.append(both[:depth])
        upper.append(both[depth:])
    lower = jnp.concatenate(lower, axis=0)
    upper = jnp.concatenate(upper, axis=0)
    lane = lax.broadcasted_iota(jnp.int32, (layers, lanes), 1)
    for index in range(hor_count):
        tile = index * chunk // lanes * lanes
        offset = index * chunk % lanes
        packed_ref[index] = jnp.where(
            lane < chunk,
            turn(lower[:, tile : tile + lanes], -offset),
            turn(upper[:, tile : tile + lanes], chunk - offset),
        )


def small_hartley(count, read, write, shape):
    if count <= 8:
        table = cas(2.0 * np.pi * (np.outer(np.arange(count), np.arange(count)) % count) / count)
        parts = [read(index) for index in range(count)]
        for wave in range(count):
            total = None
            for index in range(count):
                value = float(table[wave, index])
                if abs(value) < 1e-12:
                    continue
                if abs(value - 1.0) < 1e-12:
                    term = parts[index]
                elif abs(value + 1.0) < 1e-12:
                    term = -parts[index]
                else:
                    term = parts[index] * value
                total = term if total is None else total + term
            write(wave, total)
        return

    def outer(wave, carry):
        def inner(index, total):
            angle = jnp.full(shape, wave * index % count, jnp.int32).astype(f32)
            angle = angle * (2.0 * math.pi / count)
            return total + read(index) * (jnp.cos(angle) + jnp.sin(angle))

        write(wave, lax.fori_loop(0, count, inner, jnp.zeros(shape, f32)))
        return carry

    lax.fori_loop(0, count, outer, 0)


def interface_kernel(
    spot_ref,
    class_ref,
    packed_ref,
    wave_y_ref,
    wave_x_ref,
    back_ref,
    sum_ref,
    wave_ref,
    answer_ref,
    inverse_ref,
    partial_ref,
    *,
    chunk,
):
    hor_count, layers, _ = packed_ref.shape
    rows = wave_y_ref.shape[0]
    subsets = lanes // chunk
    classes = max(1, hor_count // rows)
    repeats = max(1, rows // hor_count)
    lane = lax.broadcasted_iota(jnp.int32, (layers, lanes), 1)
    first = lane % (2 * chunk) < chunk

    def halves(index):
        values = packed_ref[index]
        width = 2 * chunk
        while width < lanes:
            values = jnp.where(lane < width, values, turn(values, width))
            width = width * 2
        return values

    def joined(index):
        here = halves(index)
        before = halves((index + hor_count - 1) % hor_count)
        return jnp.where(first, here, turn(here, chunk)) + jnp.where(
            first, turn(before, -chunk), before
        )

    def put_sum(index, values):
        sum_ref[index] = values

    if hor_count <= 8:
        small_hartley(hor_count, joined, lambda k, v: wave_ref.__setitem__(k, v), (layers, lanes))
    else:
        lax.fori_loop(0, hor_count, lambda k, c: (put_sum(k, joined(k)), c)[1], 0)
        small_hartley(
            hor_count,
            lambda k: sum_ref[k],
            lambda k, v: wave_ref.__setitem__(k, v),
            (layers, lanes),
        )
    weights, couple = layer_terms(class_ref, layers, rows // 8, 0)
    wave = damping + smoothing * (wave_y_ref[...] + wave_x_ref[pl.ds(spot_ref[0], 1), :])
    factor(weights, couple, wave, inverse_ref)
    plane_lane = lax.broadcasted_iota(jnp.int32, (rows, lanes), 1)
    group = plane_lane // chunk % classes

    def source(layer):
        if classes == 1:
            return jnp.concatenate([wave_ref[:, layer, :]] * repeats, axis=0)
        total = wave_ref[0:rows, layer, :]
        for part in range(1, classes):
            piece = wave_ref[part * rows : (part + 1) * rows, layer, :]
            total = jnp.where(group == part, piece, total)
        return total

    def emit(layer, values):
        if classes == 1:
            total = values[0:hor_count]
            for part in range(1, repeats):
                total = total + values[part * hor_count : (part + 1) * hor_count]
            answer_ref[:, layer, :] = total
            return
        for part in range(classes):
            answer_ref[part * rows : (part + 1) * rows, layer, :] = jnp.where(
                group == part, values, 0.0
            )

    substitute(couple, inverse_ref, partial_ref, source, emit)

    def gathered(index):
        values = answer_ref[index]
        shift = chunk
        while shift < lanes:
            values = values + turn(values, shift)
            shift = shift * 2
        return values

    scale = 1.0 / (rows * subsets)

    def put_scaled(index, values):
        sum_ref[index] = values * scale

    if hor_count <= 8:
        small_hartley(hor_count, gathered, put_scaled, (layers, lanes))
    else:
        lax.fori_loop(
            0, hor_count, lambda k, c: (wave_ref.__setitem__(k, gathered(k)), c)[1], 0
        )
        small_hartley(hor_count, lambda k: wave_ref[k], put_scaled, (layers, lanes))
    for index in range(hor_count):
        back_ref[index] = jnp.where(first, sum_ref[index], sum_ref[(index + 1) % hor_count])


def finish_kernel(
    dep_ref,
    class_ref,
    back_ref,
    source_ref,
    inverse_ref,
    table_high,
    table_low,
    sine_high,
    sine_low,
    near_ref,
    far_ref,
    own_ref,
    send_ref,
    left_ref,
    right_ref,
    stage_ref,
    partial_ref,
):
    layers, rows, half = source_ref.shape
    depth = layers // 2
    hor_count = back_ref.shape[0]
    chunk = half // hor_count
    lane = lax.broadcasted_iota(jnp.int32, (layers, lanes), 1)
    for tile in range(half // lanes):
        left = None
        right = None
        for index in range(tile * lanes // chunk, (tile + 1) * lanes // chunk):
            offset = index * chunk % lanes
            values = back_ref[index]
            left_part = turn(values, offset)
            right_part = turn(values, offset - chunk)
            inside = lane >= offset
            left = left_part if left is None else jnp.where(inside, left_part, left)
            right = right_part if right is None else jnp.where(inside, right_part, right)
        left_ref[:, tile * lanes : (tile + 1) * lanes] = left
        right_ref[:, tile * lanes : (tile + 1) * lanes] = right
    weights, couple = layer_terms(class_ref, layers, half // lanes, 1)
    near = near_ref[...]
    far = far_ref[...]
    edge_row = lax.broadcasted_iota(jnp.int32, (rows, half), 0) == 0

    def row_of(ref, layer):
        return jnp.broadcast_to(ref[pl.ds(layer, 1), :], (rows, half))

    def source(layer):
        pull = near * row_of(left_ref, layer) + far * row_of(right_ref, layer)
        return source_ref[layer] + weights[layer] * pull

    def emit(layer, values):
        stage_ref[layer] = jnp.where(edge_row, row_of(left_ref, layer), values)

    substitute(couple, inverse_ref, partial_ref, source, emit)
    block = depth * rows
    sine = (sine_high[...], sine_low[...])
    parts = []
    for part in range(2):
        piece = stage_ref[part * depth : (part + 1) * depth].reshape(block, half)
        parts.append(dot3(sine, split(piece)))
    waves = jnp.concatenate(parts, axis=0)
    cells = dot3(split(waves), (table_high[0], table_low[0]), (((1,), (1,)), ((), ())))
    stage_ref[...] = cells.reshape(layers, rows, half)
    place = dep_ref[0] * depth
    own_ref[...] = stage_ref[pl.ds(place, depth)]
    send_ref[...] = stage_ref[pl.ds(depth - place, depth)]


def unfold_kernel(dep_ref, own_ref, recv_ref, bins_ref, out_ref, *, scale):
    half = own_ref.shape[-1]
    sign = jnp.where(dep_ref[0] == 0, scale, -scale).astype(f32)
    focus_map = focusing(bins_ref[...])
    own = own_ref[...]
    recv = recv_ref[...]
    out_ref[..., :half] = focus_map[..., :half] * ((own + recv) * scale)
    out_ref[..., half:] = focus_map[..., half:] * ((own - recv) * sign)


def whole(shape):
    return pl.BlockSpec(shape, lambda i, *_: (0,) * len(shape))


def call(kernel, scalars, in_specs, out_specs, out_shape, scratch=(), grid=(1,)):
    return pl.pallas_call(
        kernel,
        grid_spec=pltpu.PrefetchScalarGridSpec(
            num_scalar_prefetch=scalars,
            grid=grid,
            in_specs=in_specs,
            out_specs=out_specs,
            scratch_shapes=list(scratch),
        ),
        out_shape=out_shape,
        compiler_params=pltpu.CompilerParams(vmem_limit_bytes=48 * 1024 * 1024),
    )


def body(residual, focus_bins, layer_class):
    depth, rows, x_cells = residual.shape
    half = x_cells // 2
    layers = layer_class.shape[0]
    hor_count = lax.axis_size("hor")
    y_cells = rows * hor_count
    chunk = half // hor_count
    plane_rows = rows * half // lanes
    dep = lax.axis_index("dep").astype(jnp.int32)
    hor = lax.axis_index("hor").astype(jnp.int32)
    dep_index = dep.reshape(1)
    spot = (hor * 2 + dep).reshape(1)

    table_high, table_low = fold_tables(x_cells)
    sine = sine_matrix(rows)
    sine_high, sine_low = split_table(np.kron(np.eye(depth), sine))
    lower_row = np.concatenate([[1.0], sine[1, 1:]])
    upper_row = np.concatenate([[0.0], sine[rows - 1, 1:]])
    edge_high, edge_low = split_table(
        np.concatenate([np.kron(np.eye(depth), row[None, :]) for row in (lower_row, upper_row)])
    )
    wave_x = np.stack(
        [symbol_of(2.0 * np.pi * (2 * np.arange(half) + parity) / x_cells) for parity in range(2)]
    )
    mode = symbol_of(np.pi * np.arange(rows) / rows)
    wave_inner = damping + smoothing * (mode[None, :, None] + wave_x[:, None, :])
    wave_inner = wave_inner.astype(np.float32)
    near = np.broadcast_to((lower_row * (np.arange(rows) > 0))[:, None], (rows, half))
    far = np.broadcast_to(upper_row[:, None], (rows, half))
    lane = np.arange(lanes)
    wave_number = (lane // chunk)[None, :] * plane_rows + np.arange(plane_rows)[:, None]
    wave_y = symbol_of(2.0 * np.pi * wave_number / y_cells).astype(np.float32)
    spots = np.arange(hor_count)[:, None, None] * chunk + (lane % chunk)[None, None, :]
    spots = 2 * spots + np.arange(2)[None, :, None]
    wave_spots = symbol_of(2.0 * np.pi * spots / x_cells).reshape(2 * hor_count, lanes)

    def shape(*dims):
        return jax.ShapeDtypeStruct(dims, f32)

    slab = (depth, rows, half)
    field = (layers, rows, half)
    packed = (hor_count, layers, lanes)
    steps = 2
    piece = depth // steps
    cut = pl.BlockSpec((piece, rows, x_cells), lambda i, *_: (i, 0, 0))
    cut_half = pl.BlockSpec((piece, rows, half), lambda i, *_: (i, 0, 0))
    own, send = call(
        fold_kernel, 1, [cut, cut], [cut_half, cut_half], [shape(*slab)] * 2, grid=(steps,)
    )(dep_index, residual, focus_bins)
    pairs = [(0, 1), (1, 0)]
    recv = lax.ppermute(send, "dep", pairs)

    table_spec = pl.BlockSpec((1, half, half), lambda i, dep_ref, *_: (dep_ref[0], 0, 0))
    sine_spec = whole(sine_high.shape)
    edge_spec = whole(edge_high.shape)
    wave_spec = pl.BlockSpec((1, rows, half), lambda i, dep_ref, *_: (dep_ref[0], 0, 0))
    outgoing, source, inverse = call(
        interior_kernel,
        2,
        [whole(slab)] * 2
        + [table_spec] * 2
        + [sine_spec] * 2
        + [edge_spec] * 2
        + [wave_spec],
        [whole(packed), whole(field), whole(field)],
        [shape(*packed), shape(*field), shape(*field)],
        [pltpu.VMEM(field, f32)] * 2,
    )(
        dep_index,
        layer_class,
        own,
        recv,
        jnp.asarray(table_high),
        jnp.asarray(table_low),
        jnp.asarray(sine_high),
        jnp.asarray(sine_low),
        jnp.asarray(edge_high),
        jnp.asarray(edge_low),
        jnp.asarray(wave_inner),
    )
    incoming = lax.all_to_all(outgoing, "hor", split_axis=0, concat_axis=0, tiled=True)
    plane = (layers, plane_rows, lanes)
    answered = call(
        functools.partial(interface_kernel, chunk=chunk),
        2,
        [whole(packed), whole(wave_y.shape), whole(wave_spots.shape)],
        whole(packed),
        shape(*packed),
        [pltpu.VMEM(packed, f32)] * 3 + [pltpu.VMEM(plane, f32)] * 2,
    )(
        spot,
        layer_class,
        incoming,
        jnp.asarray(wave_y),
        jnp.asarray(wave_spots.astype(np.float32)),
    )
    edges = lax.all_to_all(answered, "hor", split_axis=0, concat_axis=0, tiled=True)
    own, send = call(
        finish_kernel,
        2,
        [whole(packed), whole(field), whole(field)]
        + [table_spec] * 2
        + [sine_spec] * 2
        + [whole((rows, half))] * 2,
        [whole(slab)] * 2,
        [shape(*slab)] * 2,
        [pltpu.VMEM((layers, half), f32)] * 2 + [pltpu.VMEM(field, f32)] * 2,
    )(
        dep_index,
        layer_class,
        edges,
        source,
        inverse,
        jnp.asarray(table_high),
        jnp.asarray(table_low),
        jnp.asarray(sine_high),
        jnp.asarray(sine_low),
        jnp.asarray(near.astype(np.float32)),
        jnp.asarray(far.astype(np.float32)),
    )
    recv = lax.ppermute(send, "dep", pairs)
    return call(
        functools.partial(unfold_kernel, scale=1.0 / x_cells),
        1,
        [cut_half, cut_half, cut],
        cut,
        shape(depth, rows, x_cells),
        grid=(steps,),
    )(dep_index, own, recv, focus_bins)


def solution(mesh):
    return jax.shard_map(
        body,
        mesh=mesh,
        in_specs=(P(("grp", "dep"), "hor", None), P(("grp", "dep"), "hor", None), P("grp")),
        out_specs=P(("grp", "dep"), "hor", None),
        check_vma=False,
    )
```

```python
import functools
import math

import jax
import jax.numpy as jnp
import ml_dtypes
import numpy as np
from jax import lax
from jax.experimental import pallas as pl
from jax.experimental.pallas import tpu as pltpu
from jax.sharding import PartitionSpec as P

damping = 0.01
smoothing = 1.0
coupling_scale = 1.0
weight_base = 0.5
weight_step = 0.2
focus_base = 0.5
focus_step = 0.09242
lanes = 128
f32 = jnp.float32
bf16 = jnp.bfloat16


def cas(angle):
    return np.cos(angle) + np.sin(angle)


def split_table(table):
    table = table.astype(np.float32)
    high = table.astype(ml_dtypes.bfloat16)
    low = (table - high.astype(np.float32)).astype(ml_dtypes.bfloat16)
    return high, low


def fold_tables(length):
    half = length // 2
    cell = np.arange(half)[:, None]
    tables = []
    for parity in range(2):
        wave = 2 * np.arange(half)[None, :] + parity
        tables.append(cas(2.0 * np.pi * (cell * wave % length) / length))
    return split_table(np.stack(tables))


def sine_matrix(rows):
    index = np.arange(1, rows)
    matrix = np.zeros((rows, rows))
    matrix[0, 0] = 1.0
    matrix[1:, 1:] = np.sqrt(2.0 / rows) * np.sin(np.pi * np.outer(index, index) / rows)
    return matrix


def symbol_of(angle):
    return 2.0 - 2.0 * np.cos(angle)


def split(values):
    high = values.astype(bf16)
    low = (values - high.astype(f32)).astype(bf16)
    return high, low


def dot3(left, right, dims=(((1,), (0,)), ((), ()))):
    dot = functools.partial(lax.dot_general, dimension_numbers=dims, preferred_element_type=f32)
    left_high, left_low = left
    right_high, right_low = right
    return dot(left_high, right_high) + (dot(left_low, right_high) + dot(left_high, right_low))


def focusing(focus_bins):
    return focus_base * jnp.exp(focus_step * focus_bins.astype(f32))


def layer_weights(class_ref, weight_ref):
    for layer in range(weight_ref.shape[0]):
        level = jnp.full(weight_ref.shape[1:], class_ref[layer], jnp.int32).astype(f32)
        weight_ref[layer] = weight_base * jnp.exp(weight_step * level)


def layer_terms(weight_ref, plane_tiles, axis):
    layers = weight_ref.shape[0]
    weights = [weight_ref[layer] for layer in range(layers)]
    couple = [coupling_scale * weights[k] * weights[k + 1] for k in range(layers - 1)]

    def spread(values):
        return [jnp.concatenate([value] * plane_tiles, axis=axis) for value in values]

    return spread(weights), spread(couple)


def row_values(values, shape):
    row = lax.broadcasted_iota(jnp.int32, shape, 0)
    total = jnp.full(shape, float(values[0]), f32)
    for index in range(1, len(values)):
        total = jnp.where(row == index, float(values[index]), total)
    return total


def diagonal(layer, weights, couple, wave):
    total = weights[layer] * wave
    if layer > 0:
        total = total + couple[layer - 1]
    if layer < len(couple):
        total = total + couple[layer]
    return total


def factor(weights, couple, wave, inverse_ref):
    layers = len(weights)
    half = layers // 2
    top = 1.0 / diagonal(0, weights, couple, wave)
    bottom = 1.0 / diagonal(layers - 1, weights, couple, wave)
    inverse_ref[0] = top
    inverse_ref[layers - 1] = bottom
    for step in range(1, half):
        low = step
        link = couple[low - 1]
        top = 1.0 / (diagonal(low, weights, couple, wave) - link * link * top)
        inverse_ref[low] = top
        high = layers - 1 - step
        link = couple[high]
        pivot = diagonal(high, weights, couple, wave) - link * link * bottom
        if step == half - 1:
            link = couple[half - 1]
            pivot = pivot - link * link * top
        bottom = 1.0 / pivot
        inverse_ref[high] = bottom


def substitute(couple, inverse_ref, partial_ref, source, emit):
    layers = len(couple) + 1
    half = layers // 2
    top = source(0)
    bottom = source(layers - 1)
    partial_ref[0] = top
    partial_ref[layers - 1] = bottom
    for step in range(1, half):
        low = step
        top = source(low) + couple[low - 1] * inverse_ref[low - 1] * top
        partial_ref[low] = top
        high = layers - 1 - step
        bottom = source(high) + couple[high] * inverse_ref[high + 1] * bottom
        partial_ref[high] = bottom
    link = couple[half - 1]
    bottom = (bottom + link * inverse_ref[half - 1] * top) * inverse_ref[half]
    top = (top + link * bottom) * inverse_ref[half - 1]
    emit(half, bottom)
    emit(half - 1, top)
    for step in range(1, half):
        low = half - 1 - step
        top = (partial_ref[low] + couple[low] * top) * inverse_ref[low]
        emit(low, top)
        high = half + step
        bottom = (partial_ref[high] + couple[high - 1] * bottom) * inverse_ref[high]
        emit(high, bottom)


def turn(values, shift):
    shift = shift % lanes
    return values if shift == 0 else pltpu.roll(values, shift, values.ndim - 1)


def fold_kernel(
    dep_ref,
    residual_hbm,
    bins_hbm,
    class_hbm,
    own_ref,
    send_ref,
    weight_ref,
    residual_ref,
    bins_ref,
    class_ref,
    sems,
    class_sem,
    *,
    cuts,
):
    depth, _, half = own_ref.shape
    size = depth // cuts
    class_copy = pltpu.make_async_copy(class_hbm, class_ref, class_sem)
    class_copy.start()
    copies = []
    for cut in range(cuts):
        part = pl.ds(cut * size, size)
        first = pltpu.make_async_copy(bins_hbm.at[part], bins_ref.at[part], sems.at[0, cut])
        second = pltpu.make_async_copy(
            residual_hbm.at[part], residual_ref.at[part], sems.at[1, cut]
        )
        first.start()
        second.start()
        copies.append((first, second))
    sign = jnp.where(dep_ref[0] == 0, 1.0, -1.0).astype(f32)
    class_copy.wait()
    layer_weights(class_ref, weight_ref)
    for cut in range(cuts):
        part = pl.ds(cut * size, size)
        copies[cut][0].wait()
        focus_map = focusing(bins_ref[part])
        copies[cut][1].wait()
        scaled = focus_map * residual_ref[part]
        left = scaled[..., :half]
        right = sign * scaled[..., half:]
        own_ref[part] = left + right
        send_ref[part] = left - right


def to_modes(cells, table, sine):
    depth, rows, half = cells.shape
    waves = dot3(split(cells.reshape(depth * rows, half)), table)
    return dot3(sine, split(waves)).reshape(depth, rows, half)


def from_modes(modes, sine):
    depth, rows, half = modes.shape
    return dot3(sine, split(modes.reshape(depth * rows, half)))


def parts_of(small_ref, block, depth):
    cuts = np.cumsum([0, block, block, 2 * depth, 2 * depth])
    pieces = [small_ref[low:high] for low, high in zip(cuts[:-1], cuts[1:])]
    return (pieces[0], pieces[1]), (pieces[2], pieces[3])


def prepare_kernel(
    dep_ref,
    spot_ref,
    own_ref,
    weight_ref,
    table_hbm,
    small_hbm,
    inner_hbm,
    outer_hbm,
    modes_ref,
    table_ref,
    small_ref,
    inverse_ref,
    inverse_outer_ref,
    inner_ref,
    outer_ref,
    sems,
):
    depth, rows, half = own_ref.shape
    plane_rows = inverse_outer_ref.shape[1]
    dep = dep_ref[0]
    copies = [
        pltpu.make_async_copy(inner_hbm.at[dep], inner_ref, sems.at[0]),
        pltpu.make_async_copy(outer_hbm, outer_ref, sems.at[1]),
        pltpu.make_async_copy(small_hbm, small_ref, sems.at[2]),
        pltpu.make_async_copy(table_hbm.at[dep, 0], table_ref.at[0], sems.at[3]),
        pltpu.make_async_copy(table_hbm.at[dep, 1], table_ref.at[1], sems.at[4]),
    ]
    for copy in copies:
        copy.start()
    copies[0].wait()
    copies[1].wait()
    weights, couple = layer_terms(weight_ref, half // lanes, 1)
    factor(weights, couple, inner_ref[...], inverse_ref)
    weights, couple = layer_terms(weight_ref, plane_rows // 8, 0)
    wave = outer_ref[:plane_rows] + outer_ref[pl.ds(plane_rows + spot_ref[0], 1), :]
    factor(weights, couple, damping + smoothing * wave, inverse_outer_ref)
    for copy in copies[2:]:
        copy.wait()
    sine, _ = parts_of(small_ref, depth * rows, depth)
    modes_ref[...] = to_modes(own_ref[...], (table_ref[0], table_ref[1]), sine)


def interior_kernel(
    dep_ref,
    modes_ref,
    recv_ref,
    table_ref,
    small_ref,
    weight_ref,
    inverse_ref,
    packed_ref,
    source_ref,
    stage_ref,
    partial_ref,
):
    depth, rows, half = recv_ref.shape
    layers = 2 * depth
    block = depth * rows
    hor_count = packed_ref.shape[0]
    chunk = half // hor_count
    place = dep_ref[0] * depth
    sine, edge = parts_of(small_ref, block, depth)
    source_ref[pl.ds(place, depth)] = modes_ref[...]
    source_ref[pl.ds(depth - place, depth)] = to_modes(
        recv_ref[...], (table_ref[0], table_ref[1]), sine
    )
    weights, couple = layer_terms(weight_ref, half // lanes, 1)
    edge_row = lax.broadcasted_iota(jnp.int32, (rows, half), 0) == 0

    def emit(layer, values):
        stage_ref[layer] = jnp.where(edge_row, source_ref[layer], weights[layer] * values)

    substitute(couple, inverse_ref, partial_ref, lambda layer: source_ref[layer], emit)
    lower = []
    upper = []
    for part in range(2):
        both = from_modes(stage_ref[part * depth : (part + 1) * depth], edge)
        lower.append(both[:depth])
        upper.append(both[depth:])
    lower = jnp.concatenate(lower, axis=0)
    upper = jnp.concatenate(upper, axis=0)
    lane = lax.broadcasted_iota(jnp.int32, (layers, lanes), 1)
    for index in range(hor_count):
        tile = index * chunk // lanes * lanes
        offset = index * chunk % lanes
        packed_ref[index] = jnp.where(
            lane < chunk,
            turn(lower[:, tile : tile + lanes], -offset),
            turn(upper[:, tile : tile + lanes], chunk - offset),
        )


def small_hartley(count, read, write, shape):
    if count <= 8:
        table = cas(2.0 * np.pi * (np.outer(np.arange(count), np.arange(count)) % count) / count)
        parts = [read(index) for index in range(count)]
        for wave in range(count):
            total = None
            for index in range(count):
                value = float(table[wave, index])
                if abs(value) < 1e-12:
                    continue
                if abs(value - 1.0) < 1e-12:
                    term = parts[index]
                elif abs(value + 1.0) < 1e-12:
                    term = -parts[index]
                else:
                    term = parts[index] * value
                total = term if total is None else total + term
            write(wave, total)
        return

    def outer(wave, carry):
        def inner(index, total):
            angle = jnp.full(shape, wave * index % count, jnp.int32).astype(f32)
            angle = angle * (2.0 * math.pi / count)
            return total + read(index) * (jnp.cos(angle) + jnp.sin(angle))

        write(wave, lax.fori_loop(0, count, inner, jnp.zeros(shape, f32)))
        return carry

    lax.fori_loop(0, count, outer, 0)


def interface_kernel(
    packed_ref,
    weight_ref,
    inverse_ref,
    back_ref,
    sum_ref,
    wave_ref,
    answer_ref,
    partial_ref,
    *,
    chunk,
):
    hor_count, layers, _ = packed_ref.shape
    rows = inverse_ref.shape[1]
    subsets = lanes // chunk
    classes = max(1, hor_count // rows)
    repeats = max(1, rows // hor_count)
    lane = lax.broadcasted_iota(jnp.int32, (layers, lanes), 1)
    first = lane % (2 * chunk) < chunk

    def halves(index):
        values = packed_ref[index]
        width = 2 * chunk
        while width < lanes:
            values = jnp.where(lane < width, values, turn(values, width))
            width = width * 2
        return values

    def joined(index):
        here = halves(index)
        before = halves((index + hor_count - 1) % hor_count)
        return jnp.where(first, here, turn(here, chunk)) + jnp.where(
            first, turn(before, -chunk), before
        )

    def put_sum(index, values):
        sum_ref[index] = values

    if hor_count <= 8:
        small_hartley(hor_count, joined, lambda k, v: wave_ref.__setitem__(k, v), (layers, lanes))
    else:
        lax.fori_loop(0, hor_count, lambda k, c: (put_sum(k, joined(k)), c)[1], 0)
        small_hartley(
            hor_count,
            lambda k: sum_ref[k],
            lambda k, v: wave_ref.__setitem__(k, v),
            (layers, lanes),
        )
    weights, couple = layer_terms(weight_ref, rows // 8, 0)
    plane_lane = lax.broadcasted_iota(jnp.int32, (rows, lanes), 1)
    group = plane_lane // chunk % classes

    def source(layer):
        if classes == 1:
            return jnp.concatenate([wave_ref[:, layer, :]] * repeats, axis=0)
        total = wave_ref[0:rows, layer, :]
        for part in range(1, classes):
            piece = wave_ref[part * rows : (part + 1) * rows, layer, :]
            total = jnp.where(group == part, piece, total)
        return total

    def emit(layer, values):
        if classes == 1:
            total = values[0:hor_count]
            for part in range(1, repeats):
                total = total + values[part * hor_count : (part + 1) * hor_count]
            answer_ref[:, layer, :] = total
            return
        for part in range(classes):
            answer_ref[part * rows : (part + 1) * rows, layer, :] = jnp.where(
                group == part, values, 0.0
            )

    substitute(couple, inverse_ref, partial_ref, source, emit)

    def gathered(index):
        values = answer_ref[index]
        shift = chunk
        while shift < lanes:
            values = values + turn(values, shift)
            shift = shift * 2
        return values

    scale = 1.0 / (rows * subsets)

    def put_scaled(index, values):
        sum_ref[index] = values * scale

    if hor_count <= 8:
        small_hartley(hor_count, gathered, put_scaled, (layers, lanes))
    else:
        lax.fori_loop(
            0, hor_count, lambda k, c: (wave_ref.__setitem__(k, gathered(k)), c)[1], 0
        )
        small_hartley(hor_count, lambda k: wave_ref[k], put_scaled, (layers, lanes))
    for index in range(hor_count):
        back_ref[index] = jnp.where(first, sum_ref[index], sum_ref[(index + 1) % hor_count])


def finish_kernel(
    dep_ref,
    back_ref,
    source_ref,
    table_ref,
    small_ref,
    weight_ref,
    inverse_ref,
    send_ref,
    waves_ref,
    left_ref,
    right_ref,
    stage_ref,
    partial_ref,
    *,
    near_values,
    far_values,
):
    layers, rows, half = source_ref.shape
    depth = layers // 2
    hor_count = back_ref.shape[0]
    chunk = half // hor_count
    lane = lax.broadcasted_iota(jnp.int32, (layers, lanes), 1)
    for tile in range(half // lanes):
        left = None
        right = None
        for index in range(tile * lanes // chunk, (tile + 1) * lanes // chunk):
            offset = index * chunk % lanes
            values = back_ref[index]
            left_part = turn(values, offset)
            right_part = turn(values, offset - chunk)
            inside = lane >= offset
            left = left_part if left is None else jnp.where(inside, left_part, left)
            right = right_part if right is None else jnp.where(inside, right_part, right)
        left_ref[:, tile * lanes : (tile + 1) * lanes] = left
        right_ref[:, tile * lanes : (tile + 1) * lanes] = right
    weights, couple = layer_terms(weight_ref, half // lanes, 1)
    near = row_values(near_values, (rows, half))
    far = row_values(far_values, (rows, half))
    edge_row = lax.broadcasted_iota(jnp.int32, (rows, half), 0) == 0

    def row_of(ref, layer):
        return jnp.broadcast_to(ref[pl.ds(layer, 1), :], (rows, half))

    def source(layer):
        pull = near * row_of(left_ref, layer) + far * row_of(right_ref, layer)
        return source_ref[layer] + weights[layer] * pull

    def emit(layer, values):
        stage_ref[layer] = jnp.where(edge_row, row_of(left_ref, layer), values)

    substitute(couple, inverse_ref, partial_ref, source, emit)
    place = dep_ref[0] * depth
    sine, _ = parts_of(small_ref, depth * rows, depth)
    waves = from_modes(stage_ref[pl.ds(depth - place, depth)], sine)
    cells = dot3(split(waves), (table_ref[0], table_ref[1]), (((1,), (1,)), ((), ())))
    send_ref[...] = cells.reshape(depth, rows, half)
    waves_ref[...] = stage_ref[pl.ds(place, depth)]


def restore_kernel(waves_ref, bins_ref, table_ref, small_ref, own_ref, focus_ref):
    depth, rows, half = own_ref.shape
    focus_ref[...] = focusing(bins_ref[...])
    sine, _ = parts_of(small_ref, depth * rows, depth)
    waves = from_modes(waves_ref[...], sine)
    cells = dot3(split(waves), (table_ref[0], table_ref[1]), (((1,), (1,)), ((), ())))
    own_ref[...] = cells.reshape(depth, rows, half)


def unfold_kernel(dep_ref, own_ref, recv_ref, focus_ref, out_hbm, out_ref, sems, *, scale, cuts):
    depth, _, half = own_ref.shape
    size = depth // cuts
    sign = jnp.where(dep_ref[0] == 0, scale, -scale).astype(f32)
    copies = []
    for cut in range(cuts):
        part = pl.ds(cut * size, size)
        own = own_ref[part]
        recv = recv_ref[part]
        focus_map = focus_ref[part]
        out_ref[part, :, :half] = focus_map[..., :half] * ((own + recv) * scale)
        out_ref[part, :, half:] = focus_map[..., half:] * ((own - recv) * sign)
        copy = pltpu.make_async_copy(out_ref.at[part], out_hbm.at[part], sems.at[cut])
        copy.start()
        copies.append(copy)
    for copy in copies:
        copy.wait()


def call(kernel, operands, out_shape, scratch=(), outside=False):
    specs = []
    values = []
    for space, value in operands:
        specs.append(pl.BlockSpec(memory_space=space))
        if space is pltpu.HBM:
            value = pltpu.with_memory_space_constraint(value, pltpu.HBM)
        values.append(value)
    out_space = pltpu.HBM if outside else pltpu.VMEM
    single = not isinstance(out_shape, list)
    out_specs = pl.BlockSpec(memory_space=out_space)
    return pl.pallas_call(
        kernel,
        in_specs=specs,
        out_specs=out_specs if single else [out_specs] * len(out_shape),
        out_shape=out_shape,
        scratch_shapes=list(scratch),
        compiler_params=pltpu.CompilerParams(vmem_limit_bytes=48 * 1024 * 1024),
    )(*values)


def body(residual, focus_bins, layer_class):
    depth, rows, x_cells = residual.shape
    half = x_cells // 2
    layers = layer_class.shape[0]
    hor_count = lax.axis_size("hor")
    y_cells = rows * hor_count
    chunk = half // hor_count
    plane_rows = rows * half // lanes
    dep = lax.axis_index("dep").astype(jnp.int32)
    hor = lax.axis_index("hor").astype(jnp.int32)
    dep_index = dep.reshape(1)
    spot = (hor * 2 + dep).reshape(1)

    table = np.stack(fold_tables(x_cells), axis=1)
    sine = sine_matrix(rows)
    near = np.concatenate([[0.0], sine[1, 1:]])
    far = np.concatenate([[0.0], sine[rows - 1, 1:]])
    lower_row = np.concatenate([[1.0], sine[1, 1:]])
    edge = np.concatenate([np.kron(np.eye(depth), row[None, :]) for row in (lower_row, far)])
    small = np.concatenate(split_table(np.kron(np.eye(depth), sine)) + split_table(edge))
    wave_x = np.stack(
        [symbol_of(2.0 * np.pi * (2 * np.arange(half) + parity) / x_cells) for parity in range(2)]
    )
    mode = symbol_of(np.pi * np.arange(rows) / rows)
    inner = damping + smoothing * (mode[None, :, None] + wave_x[:, None, :])
    lane = np.arange(lanes)
    wave_number = (lane // chunk)[None, :] * plane_rows + np.arange(plane_rows)[:, None]
    wave_y = symbol_of(2.0 * np.pi * wave_number / y_cells)
    spots = np.arange(hor_count)[:, None, None] * chunk + (lane % chunk)[None, None, :]
    spots = 2 * spots + np.arange(2)[None, :, None]
    wave_spots = symbol_of(2.0 * np.pi * spots / x_cells).reshape(2 * hor_count, lanes)
    outer = np.concatenate([wave_y, wave_spots]).astype(np.float32)

    def shape(*dims):
        return jax.ShapeDtypeStruct(dims, f32)

    def constant(value):
        return (pltpu.HBM, jnp.asarray(value))

    def scalar(value):
        return (pltpu.SMEM, value)

    def near_by(value):
        return (pltpu.VMEM, value)

    slab = (depth, rows, half)
    full = (depth, rows, x_cells)
    field = (layers, rows, half)
    packed = (hor_count, layers, lanes)
    plane = (layers, plane_rows, lanes)
    cuts = 4
    own, send, weight = call(
        functools.partial(fold_kernel, cuts=cuts),
        [scalar(dep_index)]
        + [(pltpu.HBM, value) for value in (residual, focus_bins, layer_class)],
        [shape(*slab), shape(*slab), shape(layers, 8, lanes)],
        [
            pltpu.VMEM(full, f32),
            pltpu.VMEM(full, jnp.int32),
            pltpu.SMEM((layers,), jnp.int32),
            pltpu.SemaphoreType.DMA((2, cuts)),
            pltpu.SemaphoreType.DMA,
        ],
    )
    pairs = [(0, 1), (1, 0)]
    recv = lax.ppermute(send, "dep", pairs)
    modes, table_here, small_here, inverse, inverse_outer = call(
        prepare_kernel,
        [scalar(dep_index), scalar(spot), near_by(own), near_by(weight)]
        + [constant(value) for value in (table, small, inner.astype(np.float32), outer)],
        [
            shape(*slab),
            jax.ShapeDtypeStruct((2, half, half), bf16),
            jax.ShapeDtypeStruct(small.shape, bf16),
            shape(*field),
            shape(*plane),
        ],
        [
            pltpu.VMEM((rows, half), f32),
            pltpu.VMEM(outer.shape, f32),
            pltpu.SemaphoreType.DMA((5,)),
        ],
    )
    shared = [near_by(value) for value in (table_here, small_here, weight, inverse)]
    outgoing, source = call(
        interior_kernel,
        [scalar(dep_index), near_by(modes), near_by(recv)] + shared,
        [shape(*packed), shape(*field)],
        [pltpu.VMEM(field, f32)] * 2,
    )
    incoming = lax.all_to_all(outgoing, "hor", split_axis=0, concat_axis=0, tiled=True)
    answered = call(
        functools.partial(interface_kernel, chunk=chunk),
        [near_by(incoming), near_by(weight), near_by(inverse_outer)],
        shape(*packed),
        [pltpu.VMEM(packed, f32)] * 3 + [pltpu.VMEM(plane, f32)],
    )
    edges = lax.all_to_all(answered, "hor", split_axis=0, concat_axis=0, tiled=True)
    send, waves = call(
        functools.partial(finish_kernel, near_values=near, far_values=far),
        [scalar(dep_index), near_by(edges), near_by(source)] + shared,
        [shape(*slab)] * 2,
        [pltpu.VMEM((layers, half), f32)] * 2 + [pltpu.VMEM(field, f32)] * 2,
    )
    recv = lax.ppermute(send, "dep", pairs)
    own, focus_map = call(
        restore_kernel,
        [near_by(value) for value in (waves, focus_bins, table_here, small_here)],
        [shape(*slab), shape(*full)],
    )
    return call(
        functools.partial(unfold_kernel, scale=1.0 / x_cells, cuts=cuts),
        [scalar(dep_index)] + [near_by(value) for value in (own, recv, focus_map)],
        shape(*full),
        [pltpu.VMEM(full, f32), pltpu.SemaphoreType.DMA((cuts,))],
        outside=True,
    )


def solution(mesh):
    return jax.shard_map(
        body,
        mesh=mesh,
        in_specs=(P(("grp", "dep"), "hor", None), P(("grp", "dep"), "hor", None), P("grp")),
        out_specs=P(("grp", "dep"), "hor", None),
        check_vma=False,
    )
```

```python
import functools
import math

import jax
import jax.numpy as jnp
import ml_dtypes
import numpy as np
from jax import lax
from jax.experimental import pallas as pl
from jax.experimental.pallas import tpu as pltpu
from jax.sharding import PartitionSpec as P

damping = 0.01
smoothing = 1.0
coupling_scale = 1.0
weight_base = 0.5
weight_step = 0.2
focus_base = 0.5
focus_step = 0.09242
lanes = 128
f32 = jnp.float32
bf16 = jnp.bfloat16


def cas(angle):
    return np.cos(angle) + np.sin(angle)


def split_table(table):
    table = table.astype(np.float32)
    high = table.astype(ml_dtypes.bfloat16)
    low = (table - high.astype(np.float32)).astype(ml_dtypes.bfloat16)
    return high, low


def fold_tables(length):
    half = length // 2
    cell = np.arange(half)[:, None]
    tables = []
    for parity in range(2):
        wave = 2 * np.arange(half)[None, :] + parity
        tables.append(cas(2.0 * np.pi * (cell * wave % length) / length))
    return split_table(np.stack(tables))


def sine_matrix(rows):
    index = np.arange(1, rows)
    matrix = np.zeros((rows, rows))
    matrix[0, 0] = 1.0
    matrix[1:, 1:] = np.sqrt(2.0 / rows) * np.sin(np.pi * np.outer(index, index) / rows)
    return matrix


def symbol_of(angle):
    return 2.0 - 2.0 * np.cos(angle)


def split(values):
    high = values.astype(bf16)
    low = (values - high.astype(f32)).astype(bf16)
    return high, low


def dot3(left, right, dims=(((1,), (0,)), ((), ()))):
    dot = functools.partial(lax.dot_general, dimension_numbers=dims, preferred_element_type=f32)
    left_high, left_low = left
    right_high, right_low = right
    rows = left_high.shape[0]
    both = dot(jnp.concatenate([left_high, left_low], axis=0), right_high)
    return both[:rows] + (both[rows:] + dot(left_high, right_low))


def focusing(focus_bins):
    return focus_base * jnp.exp(focus_step * focus_bins.astype(f32))


def layer_weights(class_ref, weight_ref):
    for layer in range(weight_ref.shape[0]):
        level = jnp.full(weight_ref.shape[1:], class_ref[layer], jnp.int32).astype(f32)
        weight_ref[layer] = weight_base * jnp.exp(weight_step * level)


def layer_terms(weight_ref, plane_tiles, axis):
    layers = weight_ref.shape[0]
    weights = [weight_ref[layer] for layer in range(layers)]
    couple = [coupling_scale * weights[k] * weights[k + 1] for k in range(layers - 1)]

    def spread(values):
        return [jnp.concatenate([value] * plane_tiles, axis=axis) for value in values]

    return spread(weights), spread(couple)


def row_values(values, shape):
    row = lax.broadcasted_iota(jnp.int32, shape, 0)
    total = jnp.full(shape, float(values[0]), f32)
    for index in range(1, len(values)):
        total = jnp.where(row == index, float(values[index]), total)
    return total


def diagonal(layer, weights, couple, wave):
    total = weights[layer] * wave
    if layer > 0:
        total = total + couple[layer - 1]
    if layer < len(couple):
        total = total + couple[layer]
    return total


def factor(weights, couple, wave, inverse_ref):
    layers = len(weights)
    half = layers // 2
    top = 1.0 / diagonal(0, weights, couple, wave)
    bottom = 1.0 / diagonal(layers - 1, weights, couple, wave)
    inverse_ref[0] = top
    inverse_ref[layers - 1] = bottom
    for step in range(1, half):
        low = step
        link = couple[low - 1]
        top = 1.0 / (diagonal(low, weights, couple, wave) - link * link * top)
        inverse_ref[low] = top
        high = layers - 1 - step
        link = couple[high]
        pivot = diagonal(high, weights, couple, wave) - link * link * bottom
        if step == half - 1:
            link = couple[half - 1]
            pivot = pivot - link * link * top
        bottom = 1.0 / pivot
        inverse_ref[high] = bottom


def substitute(couple, inverse_ref, partial_ref, source, emit):
    layers = len(couple) + 1
    half = layers // 2
    top = source(0)
    bottom = source(layers - 1)
    partial_ref[0] = top
    partial_ref[layers - 1] = bottom
    for step in range(1, half):
        low = step
        top = source(low) + couple[low - 1] * inverse_ref[low - 1] * top
        partial_ref[low] = top
        high = layers - 1 - step
        bottom = source(high) + couple[high] * inverse_ref[high + 1] * bottom
        partial_ref[high] = bottom
    link = couple[half - 1]
    bottom = (bottom + link * inverse_ref[half - 1] * top) * inverse_ref[half]
    top = (top + link * bottom) * inverse_ref[half - 1]
    emit(half, bottom)
    emit(half - 1, top)
    for step in range(1, half):
        low = half - 1 - step
        top = (partial_ref[low] + couple[low] * top) * inverse_ref[low]
        emit(low, top)
        high = half + step
        bottom = (partial_ref[high] + couple[high - 1] * bottom) * inverse_ref[high]
        emit(high, bottom)


def turn(values, shift):
    shift = shift % lanes
    return values if shift == 0 else pltpu.roll(values, shift, values.ndim - 1)


def fold_kernel(
    dep_ref,
    residual_hbm,
    bins_hbm,
    class_hbm,
    small_hbm,
    inner_hbm,
    outer_hbm,
    own_ref,
    send_ref,
    weight_ref,
    small_ref,
    inner_ref,
    outer_ref,
    residual_ref,
    bins_ref,
    class_ref,
    sems,
    class_sem,
    table_sems,
    *,
    cuts,
):
    depth, _, half = own_ref.shape
    size = depth // cuts
    class_copy = pltpu.make_async_copy(class_hbm, class_ref, class_sem)
    class_copy.start()
    copies = []
    for cut in range(cuts):
        part = pl.ds(cut * size, size)
        first = pltpu.make_async_copy(bins_hbm.at[part], bins_ref.at[part], sems.at[0, cut])
        second = pltpu.make_async_copy(
            residual_hbm.at[part], residual_ref.at[part], sems.at[1, cut]
        )
        first.start()
        second.start()
        copies.append((first, second))
    dep = dep_ref[0]
    tables = [
        pltpu.make_async_copy(inner_hbm.at[dep], inner_ref, table_sems.at[0]),
        pltpu.make_async_copy(outer_hbm, outer_ref, table_sems.at[1]),
        pltpu.make_async_copy(small_hbm, small_ref, table_sems.at[2]),
    ]
    for copy in tables:
        copy.start()
    sign = jnp.where(dep_ref[0] == 0, 1.0, -1.0).astype(f32)
    class_copy.wait()
    layer_weights(class_ref, weight_ref)
    for cut in range(cuts):
        part = pl.ds(cut * size, size)
        copies[cut][0].wait()
        focus_map = focusing(bins_ref[part])
        copies[cut][1].wait()
        scaled = focus_map * residual_ref[part]
        left = scaled[..., :half]
        right = sign * scaled[..., half:]
        own_ref[part] = left + right
        send_ref[part] = left - right
    for copy in tables:
        copy.wait()


def dot2(left, right):
    return jnp.dot(left, right, preferred_element_type=f32)


def to_modes(cells, table, sine):
    return dot3(split(from_modes(cells, sine)), table).reshape(cells.shape)


def from_modes(modes, sine):
    depth, rows, half = modes.shape
    return dot3(sine, split(modes.reshape(depth * rows, half)))


def parts_of(small_ref, block, depth):
    cuts = np.cumsum([0, block, block, 2 * depth, 2 * depth])
    pieces = [small_ref[low:high] for low, high in zip(cuts[:-1], cuts[1:])]
    return (pieces[0], pieces[1]), (pieces[2], pieces[3])


def prepare_kernel(
    dep_ref,
    spot_ref,
    own_ref,
    weight_ref,
    table_hbm,
    small_ref,
    inner_ref,
    outer_ref,
    modes_ref,
    table_ref,
    inverse_ref,
    inverse_outer_ref,
    sems,
):
    copies = [
        pltpu.make_async_copy(table_hbm.at[dep_ref[0], part], table_ref.at[part], sems.at[part])
        for part in range(2)
    ]
    for copy in copies:
        copy.start()
    depth, rows, half = own_ref.shape
    plane_rows = inverse_outer_ref.shape[1]
    weights, couple = layer_terms(weight_ref, half // lanes, 1)
    factor(weights, couple, inner_ref[...], inverse_ref)
    weights, couple = layer_terms(weight_ref, plane_rows // 8, 0)
    wave = outer_ref[:plane_rows] + outer_ref[pl.ds(plane_rows + spot_ref[0], 1), :]
    factor(weights, couple, damping + smoothing * wave, inverse_outer_ref)
    sine, _ = parts_of(small_ref, depth * rows, depth)
    high, low = split(from_modes(own_ref[...], sine))
    block = depth * rows
    copies[0].wait()
    both = dot2(jnp.concatenate([high, low], axis=0), table_ref[0])
    copies[1].wait()
    total = both[:block] + (both[block:] + dot2(high, table_ref[1]))
    modes_ref[...] = total.reshape(depth, rows, half)


def interior_kernel(
    dep_ref,
    modes_ref,
    recv_ref,
    table_ref,
    small_ref,
    weight_ref,
    inverse_ref,
    packed_ref,
    source_ref,
    stage_ref,
    partial_ref,
):
    depth, rows, half = recv_ref.shape
    layers = 2 * depth
    block = depth * rows
    hor_count = packed_ref.shape[0]
    chunk = half // hor_count
    place = dep_ref[0] * depth
    sine, edge = parts_of(small_ref, block, depth)
    source_ref[pl.ds(place, depth)] = modes_ref[...]
    source_ref[pl.ds(depth - place, depth)] = to_modes(
        recv_ref[...], (table_ref[0], table_ref[1]), sine
    )
    weights, couple = layer_terms(weight_ref, half // lanes, 1)
    edge_row = lax.broadcasted_iota(jnp.int32, (rows, half), 0) == 0

    def emit(layer, values):
        stage_ref[layer] = jnp.where(edge_row, source_ref[layer], weights[layer] * values)

    substitute(couple, inverse_ref, partial_ref, lambda layer: source_ref[layer], emit)
    lower = []
    upper = []
    for part in range(2):
        both = from_modes(stage_ref[part * depth : (part + 1) * depth], edge)
        lower.append(both[:depth])
        upper.append(both[depth:])
    lower = jnp.concatenate(lower, axis=0)
    upper = jnp.concatenate(upper, axis=0)
    lane = lax.broadcasted_iota(jnp.int32, (layers, lanes), 1)
    for index in range(hor_count):
        tile = index * chunk // lanes * lanes
        offset = index * chunk % lanes
        packed_ref[index] = jnp.where(
            lane < chunk,
            turn(lower[:, tile : tile + lanes], -offset),
            turn(upper[:, tile : tile + lanes], chunk - offset),
        )


def small_hartley(count, read, write, shape):
    if count <= 8:
        table = cas(2.0 * np.pi * (np.outer(np.arange(count), np.arange(count)) % count) / count)
        parts = [read(index) for index in range(count)]
        for wave in range(count):
            total = None
            for index in range(count):
                value = float(table[wave, index])
                if abs(value) < 1e-12:
                    continue
                if abs(value - 1.0) < 1e-12:
                    term = parts[index]
                elif abs(value + 1.0) < 1e-12:
                    term = -parts[index]
                else:
                    term = parts[index] * value
                total = term if total is None else total + term
            write(wave, total)
        return

    def outer(wave, carry):
        def inner(index, total):
            angle = jnp.full(shape, wave * index % count, jnp.int32).astype(f32)
            angle = angle * (2.0 * math.pi / count)
            return total + read(index) * (jnp.cos(angle) + jnp.sin(angle))

        write(wave, lax.fori_loop(0, count, inner, jnp.zeros(shape, f32)))
        return carry

    lax.fori_loop(0, count, outer, 0)


def interface_kernel(
    packed_ref,
    weight_ref,
    inverse_ref,
    back_ref,
    sum_ref,
    wave_ref,
    answer_ref,
    partial_ref,
    *,
    chunk,
):
    hor_count, layers, _ = packed_ref.shape
    rows = inverse_ref.shape[1]
    subsets = lanes // chunk
    classes = max(1, hor_count // rows)
    repeats = max(1, rows // hor_count)
    lane = lax.broadcasted_iota(jnp.int32, (layers, lanes), 1)
    first = lane % (2 * chunk) < chunk

    def halves(index):
        values = packed_ref[index]
        width = 2 * chunk
        while width < lanes:
            values = jnp.where(lane < width, values, turn(values, width))
            width = width * 2
        return values

    def joined(index):
        here = halves(index)
        before = halves((index + hor_count - 1) % hor_count)
        return jnp.where(first, here, turn(here, chunk)) + jnp.where(
            first, turn(before, -chunk), before
        )

    def put_sum(index, values):
        sum_ref[index] = values

    if hor_count <= 8:
        small_hartley(hor_count, joined, lambda k, v: wave_ref.__setitem__(k, v), (layers, lanes))
    else:
        lax.fori_loop(0, hor_count, lambda k, c: (put_sum(k, joined(k)), c)[1], 0)
        small_hartley(
            hor_count,
            lambda k: sum_ref[k],
            lambda k, v: wave_ref.__setitem__(k, v),
            (layers, lanes),
        )
    weights, couple = layer_terms(weight_ref, rows // 8, 0)
    plane_lane = lax.broadcasted_iota(jnp.int32, (rows, lanes), 1)
    group = plane_lane // chunk % classes

    def source(layer):
        if classes == 1:
            return jnp.concatenate([wave_ref[:, layer, :]] * repeats, axis=0)
        total = wave_ref[0:rows, layer, :]
        for part in range(1, classes):
            piece = wave_ref[part * rows : (part + 1) * rows, layer, :]
            total = jnp.where(group == part, piece, total)
        return total

    def emit(layer, values):
        if classes == 1:
            total = values[0:hor_count]
            for part in range(1, repeats):
                total = total + values[part * hor_count : (part + 1) * hor_count]
            answer_ref[:, layer, :] = total
            return
        for part in range(classes):
            answer_ref[part * rows : (part + 1) * rows, layer, :] = jnp.where(
                group == part, values, 0.0
            )

    substitute(couple, inverse_ref, partial_ref, source, emit)

    def gathered(index):
        values = answer_ref[index]
        shift = chunk
        while shift < lanes:
            values = values + turn(values, shift)
            shift = shift * 2
        return values

    scale = 1.0 / (rows * subsets)

    def put_scaled(index, values):
        sum_ref[index] = values * scale

    if hor_count <= 8:
        small_hartley(hor_count, gathered, put_scaled, (layers, lanes))
    else:
        lax.fori_loop(
            0, hor_count, lambda k, c: (wave_ref.__setitem__(k, gathered(k)), c)[1], 0
        )
        small_hartley(hor_count, lambda k: wave_ref[k], put_scaled, (layers, lanes))
    for index in range(hor_count):
        back_ref[index] = jnp.where(first, sum_ref[index], sum_ref[(index + 1) % hor_count])


def finish_kernel(
    dep_ref,
    back_ref,
    source_ref,
    table_ref,
    small_ref,
    weight_ref,
    inverse_ref,
    send_ref,
    waves_ref,
    left_ref,
    right_ref,
    stage_ref,
    partial_ref,
    *,
    near_values,
    far_values,
):
    layers, rows, half = source_ref.shape
    depth = layers // 2
    hor_count = back_ref.shape[0]
    chunk = half // hor_count
    lane = lax.broadcasted_iota(jnp.int32, (layers, lanes), 1)
    for tile in range(half // lanes):
        left = None
        right = None
        for index in range(tile * lanes // chunk, (tile + 1) * lanes // chunk):
            offset = index * chunk % lanes
            values = back_ref[index]
            left_part = turn(values, offset)
            right_part = turn(values, offset - chunk)
            inside = lane >= offset
            left = left_part if left is None else jnp.where(inside, left_part, left)
            right = right_part if right is None else jnp.where(inside, right_part, right)
        left_ref[:, tile * lanes : (tile + 1) * lanes] = left
        right_ref[:, tile * lanes : (tile + 1) * lanes] = right
    weights, couple = layer_terms(weight_ref, half // lanes, 1)
    near = row_values(near_values, (rows, half))
    far = row_values(far_values, (rows, half))
    edge_row = lax.broadcasted_iota(jnp.int32, (rows, half), 0) == 0

    def row_of(ref, layer):
        return jnp.broadcast_to(ref[pl.ds(layer, 1), :], (rows, half))

    def source(layer):
        pull = near * row_of(left_ref, layer) + far * row_of(right_ref, layer)
        return source_ref[layer] + weights[layer] * pull

    def emit(layer, values):
        stage_ref[layer] = jnp.where(edge_row, row_of(left_ref, layer), values)

    substitute(couple, inverse_ref, partial_ref, source, emit)
    place = dep_ref[0] * depth
    sine, _ = parts_of(small_ref, depth * rows, depth)
    waves = from_modes(stage_ref[pl.ds(depth - place, depth)], sine)
    cells = dot3(split(waves), (table_ref[0], table_ref[1]), (((1,), (1,)), ((), ())))
    send_ref[...] = cells.reshape(depth, rows, half)
    waves_ref[...] = stage_ref[pl.ds(place, depth)]


def restore_kernel(waves_ref, bins_ref, table_ref, small_ref, own_ref, focus_ref):
    depth, rows, half = own_ref.shape
    focus_ref[...] = focusing(bins_ref[...])
    sine, _ = parts_of(small_ref, depth * rows, depth)
    waves = from_modes(waves_ref[...], sine)
    cells = dot3(split(waves), (table_ref[0], table_ref[1]), (((1,), (1,)), ((), ())))
    own_ref[...] = cells.reshape(depth, rows, half)


def unfold_kernel(dep_ref, own_ref, recv_ref, focus_ref, out_hbm, out_ref, sems, *, scale, cuts):
    depth, _, half = own_ref.shape
    size = depth // cuts
    sign = jnp.where(dep_ref[0] == 0, scale, -scale).astype(f32)
    copies = []
    for cut in range(cuts):
        part = pl.ds(cut * size, size)
        own = own_ref[part]
        recv = recv_ref[part]
        focus_map = focus_ref[part]
        out_ref[part, :, :half] = focus_map[..., :half] * ((own + recv) * scale)
        out_ref[part, :, half:] = focus_map[..., half:] * ((own - recv) * sign)
        copy = pltpu.make_async_copy(out_ref.at[part], out_hbm.at[part], sems.at[cut])
        copy.start()
        copies.append(copy)
    for copy in copies:
        copy.wait()


def call(kernel, operands, out_shape, scratch=(), outside=False):
    specs = []
    values = []
    for space, value in operands:
        specs.append(pl.BlockSpec(memory_space=space))
        if space is pltpu.HBM:
            value = pltpu.with_memory_space_constraint(value, pltpu.HBM)
        values.append(value)
    out_space = pltpu.HBM if outside else pltpu.VMEM
    single = not isinstance(out_shape, list)
    out_specs = pl.BlockSpec(memory_space=out_space)
    return pl.pallas_call(
        kernel,
        in_specs=specs,
        out_specs=out_specs if single else [out_specs] * len(out_shape),
        out_shape=out_shape,
        scratch_shapes=list(scratch),
        compiler_params=pltpu.CompilerParams(vmem_limit_bytes=48 * 1024 * 1024),
    )(*values)


def body(residual, focus_bins, layer_class):
    depth, rows, x_cells = residual.shape
    half = x_cells // 2
    layers = layer_class.shape[0]
    hor_count = lax.axis_size("hor")
    y_cells = rows * hor_count
    chunk = half // hor_count
    plane_rows = rows * half // lanes
    dep = lax.axis_index("dep").astype(jnp.int32)
    hor = lax.axis_index("hor").astype(jnp.int32)
    dep_index = dep.reshape(1)
    spot = (hor * 2 + dep).reshape(1)

    table = np.stack(fold_tables(x_cells), axis=1)
    sine = sine_matrix(rows)
    near = np.concatenate([[0.0], sine[1, 1:]])
    far = np.concatenate([[0.0], sine[rows - 1, 1:]])
    lower_row = np.concatenate([[1.0], sine[1, 1:]])
    edge = np.concatenate([np.kron(np.eye(depth), row[None, :]) for row in (lower_row, far)])
    small = np.concatenate(split_table(np.kron(np.eye(depth), sine)) + split_table(edge))
    wave_x = np.stack(
        [symbol_of(2.0 * np.pi * (2 * np.arange(half) + parity) / x_cells) for parity in range(2)]
    )
    mode = symbol_of(np.pi * np.arange(rows) / rows)
    inner = damping + smoothing * (mode[None, :, None] + wave_x[:, None, :])
    lane = np.arange(lanes)
    wave_number = (lane // chunk)[None, :] * plane_rows + np.arange(plane_rows)[:, None]
    wave_y = symbol_of(2.0 * np.pi * wave_number / y_cells)
    spots = np.arange(hor_count)[:, None, None] * chunk + (lane % chunk)[None, None, :]
    spots = 2 * spots + np.arange(2)[None, :, None]
    wave_spots = symbol_of(2.0 * np.pi * spots / x_cells).reshape(2 * hor_count, lanes)
    outer = np.concatenate([wave_y, wave_spots]).astype(np.float32)

    def shape(*dims):
        return jax.ShapeDtypeStruct(dims, f32)

    def constant(value):
        return (pltpu.HBM, jnp.asarray(value))

    def scalar(value):
        return (pltpu.SMEM, value)

    def near_by(value):
        return (pltpu.VMEM, value)

    slab = (depth, rows, half)
    full = (depth, rows, x_cells)
    field = (layers, rows, half)
    packed = (hor_count, layers, lanes)
    plane = (layers, plane_rows, lanes)
    cuts = 4
    own, send, weight, small_here, inner_here, outer_here = call(
        functools.partial(fold_kernel, cuts=cuts),
        [scalar(dep_index)]
        + [(pltpu.HBM, value) for value in (residual, focus_bins, layer_class)]
        + [constant(value) for value in (small, inner.astype(np.float32), outer)],
        [
            shape(*slab),
            shape(*slab),
            shape(layers, 8, lanes),
            jax.ShapeDtypeStruct(small.shape, bf16),
            shape(rows, half),
            shape(*outer.shape),
        ],
        [
            pltpu.VMEM(full, f32),
            pltpu.VMEM(full, jnp.int32),
            pltpu.SMEM((layers,), jnp.int32),
            pltpu.SemaphoreType.DMA((2, cuts)),
            pltpu.SemaphoreType.DMA,
            pltpu.SemaphoreType.DMA((3,)),
        ],
    )
    pairs = [(0, 1), (1, 0)]
    recv = lax.ppermute(send, "dep", pairs)
    modes, table_here, inverse, inverse_outer = call(
        prepare_kernel,
        [scalar(dep_index), scalar(spot), near_by(own), near_by(weight), constant(table)]
        + [near_by(value) for value in (small_here, inner_here, outer_here)],
        [
            shape(*slab),
            jax.ShapeDtypeStruct((2, half, half), bf16),
            shape(*field),
            shape(*plane),
        ],
        [pltpu.SemaphoreType.DMA((2,))],
    )
    shared = [near_by(value) for value in (table_here, small_here, weight, inverse)]
    outgoing, source = call(
        interior_kernel,
        [scalar(dep_index), near_by(modes), near_by(recv)] + shared,
        [shape(*packed), shape(*field)],
        [pltpu.VMEM(field, f32)] * 2,
    )
    incoming = lax.all_to_all(outgoing, "hor", split_axis=0, concat_axis=0, tiled=True)
    answered = call(
        functools.partial(interface_kernel, chunk=chunk),
        [near_by(incoming), near_by(weight), near_by(inverse_outer)],
        shape(*packed),
        [pltpu.VMEM(packed, f32)] * 3 + [pltpu.VMEM(plane, f32)],
    )
    edges = lax.all_to_all(answered, "hor", split_axis=0, concat_axis=0, tiled=True)
    send, waves = call(
        functools.partial(finish_kernel, near_values=near, far_values=far),
        [scalar(dep_index), near_by(edges), near_by(source)] + shared,
        [shape(*slab)] * 2,
        [pltpu.VMEM((layers, half), f32)] * 2 + [pltpu.VMEM(field, f32)] * 2,
    )
    recv = lax.ppermute(send, "dep", pairs)
    own, focus_map = call(
        restore_kernel,
        [near_by(value) for value in (waves, focus_bins, table_here, small_here)],
        [shape(*slab), shape(*full)],
    )
    return call(
        functools.partial(unfold_kernel, scale=1.0 / x_cells, cuts=cuts),
        [scalar(dep_index)] + [near_by(value) for value in (own, recv, focus_map)],
        shape(*full),
        [pltpu.VMEM(full, f32), pltpu.SemaphoreType.DMA((cuts,))],
        outside=True,
    )


def solution(mesh):
    return jax.shard_map(
        body,
        mesh=mesh,
        in_specs=(P(("grp", "dep"), "hor", None), P(("grp", "dep"), "hor", None), P("grp")),
        out_specs=P(("grp", "dep"), "hor", None),
        check_vma=False,
    )
```

```python
import functools
import math

import jax
import jax.numpy as jnp
import ml_dtypes
import numpy as np
from jax import lax
from jax.experimental import pallas as pl
from jax.experimental.pallas import tpu as pltpu
from jax.sharding import PartitionSpec as P

damping = 0.01
smoothing = 1.0
coupling_scale = 1.0
weight_base = 0.5
weight_step = 0.2
focus_base = 0.5
focus_step = 0.09242
lanes = 128
f32 = jnp.float32
bf16 = jnp.bfloat16


def cas(angle):
    return np.cos(angle) + np.sin(angle)


def split_table(table):
    table = table.astype(np.float32)
    high = table.astype(ml_dtypes.bfloat16)
    low = (table - high.astype(np.float32)).astype(ml_dtypes.bfloat16)
    return high, low


def fold_tables(length):
    half = length // 2
    cell = np.arange(half)[:, None]
    tables = []
    for parity in range(2):
        wave = 2 * np.arange(half)[None, :] + parity
        tables.append(cas(2.0 * np.pi * (cell * wave % length) / length))
    return split_table(np.stack(tables))


def sine_matrix(rows):
    index = np.arange(1, rows)
    matrix = np.zeros((rows, rows))
    matrix[0, 0] = 1.0
    matrix[1:, 1:] = np.sqrt(2.0 / rows) * np.sin(np.pi * np.outer(index, index) / rows)
    return matrix


def symbol_of(angle):
    return 2.0 - 2.0 * np.cos(angle)


def split(values):
    high = values.astype(bf16)
    low = (values - high.astype(f32)).astype(bf16)
    return high, low


def dot3(left, right, dims=(((1,), (0,)), ((), ()))):
    dot = functools.partial(lax.dot_general, dimension_numbers=dims, preferred_element_type=f32)
    left_high, left_low = left
    right_high, right_low = right
    rows = left_high.shape[0]
    both = dot(jnp.concatenate([left_high, left_low], axis=0), right_high)
    return both[:rows] + (both[rows:] + dot(left_high, right_low))


def focusing(focus_bins):
    return focus_base * jnp.exp(focus_step * focus_bins.astype(f32))


def layer_weights(class_ref, weight_ref):
    for layer in range(weight_ref.shape[0]):
        level = jnp.full(weight_ref.shape[1:], class_ref[layer], jnp.int32).astype(f32)
        weight_ref[layer] = weight_base * jnp.exp(weight_step * level)


def layer_terms(weight_ref, plane_tiles, axis):
    layers = weight_ref.shape[0]
    weights = [weight_ref[layer] for layer in range(layers)]
    couple = [coupling_scale * weights[k] * weights[k + 1] for k in range(layers - 1)]

    def spread(values):
        return [jnp.concatenate([value] * plane_tiles, axis=axis) for value in values]

    return spread(weights), spread(couple)


def row_values(values, shape):
    row = lax.broadcasted_iota(jnp.int32, shape, 0)
    total = jnp.full(shape, float(values[0]), f32)
    for index in range(1, len(values)):
        total = jnp.where(row == index, float(values[index]), total)
    return total


def diagonal(layer, weights, couple, wave):
    total = weights[layer] * wave
    if layer > 0:
        total = total + couple[layer - 1]
    if layer < len(couple):
        total = total + couple[layer]
    return total


def factor(weights, couple, wave, inverse_ref):
    layers = len(weights)
    half = layers // 2
    top = 1.0 / diagonal(0, weights, couple, wave)
    bottom = 1.0 / diagonal(layers - 1, weights, couple, wave)
    inverse_ref[0] = top
    inverse_ref[layers - 1] = bottom
    for step in range(1, half):
        low = step
        link = couple[low - 1]
        top = 1.0 / (diagonal(low, weights, couple, wave) - link * link * top)
        inverse_ref[low] = top
        high = layers - 1 - step
        link = couple[high]
        pivot = diagonal(high, weights, couple, wave) - link * link * bottom
        if step == half - 1:
            link = couple[half - 1]
            pivot = pivot - link * link * top
        bottom = 1.0 / pivot
        inverse_ref[high] = bottom


def substitute(couple, inverse_ref, partial_ref, source, emit):
    layers = len(couple) + 1
    half = layers // 2
    top = source(0)
    bottom = source(layers - 1)
    partial_ref[0] = top
    partial_ref[layers - 1] = bottom
    for step in range(1, half):
        low = step
        top = source(low) + couple[low - 1] * inverse_ref[low - 1] * top
        partial_ref[low] = top
        high = layers - 1 - step
        bottom = source(high) + couple[high] * inverse_ref[high + 1] * bottom
        partial_ref[high] = bottom
    link = couple[half - 1]
    bottom = (bottom + link * inverse_ref[half - 1] * top) * inverse_ref[half]
    top = (top + link * bottom) * inverse_ref[half - 1]
    emit(half, bottom)
    emit(half - 1, top)
    for step in range(1, half):
        low = half - 1 - step
        top = (partial_ref[low] + couple[low] * top) * inverse_ref[low]
        emit(low, top)
        high = half + step
        bottom = (partial_ref[high] + couple[high - 1] * bottom) * inverse_ref[high]
        emit(high, bottom)


def turn(values, shift):
    shift = shift % lanes
    return values if shift == 0 else pltpu.roll(values, shift, values.ndim - 1)


def fold_kernel(
    dep_ref,
    residual_hbm,
    bins_hbm,
    class_hbm,
    small_hbm,
    inner_hbm,
    outer_hbm,
    own_ref,
    send_ref,
    weight_ref,
    small_ref,
    inner_ref,
    outer_ref,
    residual_ref,
    bins_ref,
    class_ref,
    sems,
    class_sem,
    table_sems,
    *,
    cuts,
):
    depth, _, half = own_ref.shape
    size = depth // cuts
    class_copy = pltpu.make_async_copy(class_hbm, class_ref, class_sem)
    class_copy.start()
    copies = []
    for cut in range(cuts):
        part = pl.ds(cut * size, size)
        first = pltpu.make_async_copy(bins_hbm.at[part], bins_ref.at[part], sems.at[0, cut])
        second = pltpu.make_async_copy(
            residual_hbm.at[part], residual_ref.at[part], sems.at[1, cut]
        )
        first.start()
        second.start()
        copies.append((first, second))
    tables = [
        pltpu.make_async_copy(inner_hbm, inner_ref, table_sems.at[0]),
        pltpu.make_async_copy(outer_hbm, outer_ref, table_sems.at[1]),
        pltpu.make_async_copy(small_hbm, small_ref, table_sems.at[2]),
    ]
    for copy in tables:
        copy.start()
    sign = jnp.where(dep_ref[0] == 0, 1.0, -1.0).astype(f32)
    class_copy.wait()
    layer_weights(class_ref, weight_ref)
    for cut in range(cuts):
        part = pl.ds(cut * size, size)
        copies[cut][0].wait()
        focus_map = focusing(bins_ref[part])
        copies[cut][1].wait()
        scaled = focus_map * residual_ref[part]
        left = scaled[..., :half]
        right = sign * scaled[..., half:]
        own_ref[part] = left + right
        send_ref[part] = left - right
    for copy in tables:
        copy.wait()


def dot2(left, right):
    return jnp.dot(left, right, preferred_element_type=f32)


def to_modes(cells, table, sine):
    return dot3(split(from_modes(cells, sine)), table).reshape(cells.shape)


def from_modes(modes, sine):
    depth, rows, half = modes.shape
    return dot3(sine, split(modes.reshape(depth * rows, half)))


def parts_of(small_ref, block, depth):
    cuts = np.cumsum([0, block, block, 2 * depth, 2 * depth])
    pieces = [small_ref[low:high] for low, high in zip(cuts[:-1], cuts[1:])]
    return (pieces[0], pieces[1]), (pieces[2], pieces[3])


def prepare_kernel(
    dep_ref,
    spot_ref,
    own_ref,
    weight_ref,
    table_hbm,
    small_ref,
    inner_ref,
    outer_ref,
    modes_ref,
    table_ref,
    inverse_ref,
    inverse_other_ref,
    inverse_outer_ref,
    sems,
):
    copies = [
        pltpu.make_async_copy(table_hbm.at[dep_ref[0], part], table_ref.at[part], sems.at[part])
        for part in range(2)
    ]
    for copy in copies:
        copy.start()
    depth, rows, half = own_ref.shape
    plane_rows = inverse_outer_ref.shape[1]
    weights, couple = layer_terms(weight_ref, half // lanes, 1)
    factor(weights, couple, inner_ref[dep_ref[0]], inverse_ref)
    factor(weights, couple, inner_ref[1 - dep_ref[0]], inverse_other_ref)
    weights, couple = layer_terms(weight_ref, plane_rows // 8, 0)
    wave = outer_ref[:plane_rows] + outer_ref[pl.ds(plane_rows + spot_ref[0], 1), :]
    factor(weights, couple, damping + smoothing * wave, inverse_outer_ref)
    sine, _ = parts_of(small_ref, depth * rows, depth)
    high, low = split(from_modes(own_ref[...], sine))
    block = depth * rows
    copies[0].wait()
    both = dot2(jnp.concatenate([high, low], axis=0), table_ref[0])
    copies[1].wait()
    total = both[:block] + (both[block:] + dot2(high, table_ref[1]))
    modes_ref[...] = total.reshape(depth, rows, half)


def interior_kernel(
    dep_ref,
    modes_ref,
    recv_ref,
    table_ref,
    small_ref,
    weight_ref,
    inverse_ref,
    packed_ref,
    keep_ref,
    give_ref,
    source_ref,
    solved_ref,
    stage_ref,
    partial_ref,
):
    depth, rows, half = recv_ref.shape
    layers = 2 * depth
    block = depth * rows
    hor_count = packed_ref.shape[0]
    chunk = half // hor_count
    place = dep_ref[0] * depth
    sine, edge = parts_of(small_ref, block, depth)
    source_ref[pl.ds(place, depth)] = modes_ref[...]
    source_ref[pl.ds(depth - place, depth)] = to_modes(
        recv_ref[...], (table_ref[0], table_ref[1]), sine
    )
    weights, couple = layer_terms(weight_ref, half // lanes, 1)
    edge_row = lax.broadcasted_iota(jnp.int32, (rows, half), 0) == 0

    def emit(layer, values):
        solved_ref[layer] = values
        stage_ref[layer] = jnp.where(edge_row, source_ref[layer], weights[layer] * values)

    substitute(couple, inverse_ref, partial_ref, lambda layer: source_ref[layer], emit)
    keep_ref[...] = solved_ref[pl.ds(place, depth)]
    give_ref[...] = solved_ref[pl.ds(depth - place, depth)]
    lower = []
    upper = []
    for part in range(2):
        both = from_modes(stage_ref[part * depth : (part + 1) * depth], edge)
        lower.append(both[:depth])
        upper.append(both[depth:])
    lower = jnp.concatenate(lower, axis=0)
    upper = jnp.concatenate(upper, axis=0)
    lane = lax.broadcasted_iota(jnp.int32, (layers, lanes), 1)
    for index in range(hor_count):
        tile = index * chunk // lanes * lanes
        offset = index * chunk % lanes
        packed_ref[index] = jnp.where(
            lane < chunk,
            turn(lower[:, tile : tile + lanes], -offset),
            turn(upper[:, tile : tile + lanes], chunk - offset),
        )


def small_hartley(count, read, write, shape):
    if count <= 8:
        table = cas(2.0 * np.pi * (np.outer(np.arange(count), np.arange(count)) % count) / count)
        parts = [read(index) for index in range(count)]
        for wave in range(count):
            total = None
            for index in range(count):
                value = float(table[wave, index])
                if abs(value) < 1e-12:
                    continue
                if abs(value - 1.0) < 1e-12:
                    term = parts[index]
                elif abs(value + 1.0) < 1e-12:
                    term = -parts[index]
                else:
                    term = parts[index] * value
                total = term if total is None else total + term
            write(wave, total)
        return

    def outer(wave, carry):
        def inner(index, total):
            angle = jnp.full(shape, wave * index % count, jnp.int32).astype(f32)
            angle = angle * (2.0 * math.pi / count)
            return total + read(index) * (jnp.cos(angle) + jnp.sin(angle))

        write(wave, lax.fori_loop(0, count, inner, jnp.zeros(shape, f32)))
        return carry

    lax.fori_loop(0, count, outer, 0)


def interface_kernel(
    packed_ref,
    weight_ref,
    inverse_ref,
    back_ref,
    sum_ref,
    wave_ref,
    answer_ref,
    partial_ref,
    *,
    chunk,
):
    hor_count, layers, _ = packed_ref.shape
    rows = inverse_ref.shape[1]
    subsets = lanes // chunk
    classes = max(1, hor_count // rows)
    repeats = max(1, rows // hor_count)
    lane = lax.broadcasted_iota(jnp.int32, (layers, lanes), 1)
    first = lane % (2 * chunk) < chunk

    def halves(index):
        values = packed_ref[index]
        width = 2 * chunk
        while width < lanes:
            values = jnp.where(lane < width, values, turn(values, width))
            width = width * 2
        return values

    def joined(index):
        here = halves(index)
        before = halves((index + hor_count - 1) % hor_count)
        return jnp.where(first, here, turn(here, chunk)) + jnp.where(
            first, turn(before, -chunk), before
        )

    def put_sum(index, values):
        sum_ref[index] = values

    if hor_count <= 8:
        small_hartley(hor_count, joined, lambda k, v: wave_ref.__setitem__(k, v), (layers, lanes))
    else:
        lax.fori_loop(0, hor_count, lambda k, c: (put_sum(k, joined(k)), c)[1], 0)
        small_hartley(
            hor_count,
            lambda k: sum_ref[k],
            lambda k, v: wave_ref.__setitem__(k, v),
            (layers, lanes),
        )
    weights, couple = layer_terms(weight_ref, rows // 8, 0)
    plane_lane = lax.broadcasted_iota(jnp.int32, (rows, lanes), 1)
    group = plane_lane // chunk % classes

    def source(layer):
        if classes == 1:
            return jnp.concatenate([wave_ref[:, layer, :]] * repeats, axis=0)
        total = wave_ref[0:rows, layer, :]
        for part in range(1, classes):
            piece = wave_ref[part * rows : (part + 1) * rows, layer, :]
            total = jnp.where(group == part, piece, total)
        return total

    def emit(layer, values):
        if classes == 1:
            total = values[0:hor_count]
            for part in range(1, repeats):
                total = total + values[part * hor_count : (part + 1) * hor_count]
            answer_ref[:, layer, :] = total
            return
        for part in range(classes):
            answer_ref[part * rows : (part + 1) * rows, layer, :] = jnp.where(
                group == part, values, 0.0
            )

    substitute(couple, inverse_ref, partial_ref, source, emit)

    def gathered(index):
        values = answer_ref[index]
        shift = chunk
        while shift < lanes:
            values = values + turn(values, shift)
            shift = shift * 2
        return values

    scale = 1.0 / (rows * subsets)

    def put_scaled(index, values):
        sum_ref[index] = values * scale

    if hor_count <= 8:
        small_hartley(hor_count, gathered, put_scaled, (layers, lanes))
    else:
        lax.fori_loop(
            0, hor_count, lambda k, c: (wave_ref.__setitem__(k, gathered(k)), c)[1], 0
        )
        small_hartley(hor_count, lambda k: wave_ref[k], put_scaled, (layers, lanes))
    for index in range(hor_count):
        back_ref[index] = jnp.where(first, sum_ref[index], sum_ref[(index + 1) % hor_count])


def extend(
    dep_ref,
    back_ref,
    solved_ref,
    table,
    small_ref,
    weight_ref,
    inverse_ref,
    left_ref,
    right_ref,
    stage_ref,
    partial_ref,
    ends,
):
    depth, rows, half = solved_ref.shape
    layers = 2 * depth
    hor_count = back_ref.shape[0]
    chunk = half // hor_count
    lane = lax.broadcasted_iota(jnp.int32, (layers, lanes), 1)
    for tile in range(half // lanes):
        left = None
        right = None
        for index in range(tile * lanes // chunk, (tile + 1) * lanes // chunk):
            offset = index * chunk % lanes
            values = back_ref[index]
            left_part = turn(values, offset)
            right_part = turn(values, offset - chunk)
            inside = lane >= offset
            left = left_part if left is None else jnp.where(inside, left_part, left)
            right = right_part if right is None else jnp.where(inside, right_part, right)
        left_ref[:, tile * lanes : (tile + 1) * lanes] = left
        right_ref[:, tile * lanes : (tile + 1) * lanes] = right
    weights, couple = layer_terms(weight_ref, half // lanes, 1)
    near = row_values(ends[0], (rows, half))
    far = row_values(ends[1], (rows, half))

    def row_of(ref, layer):
        return jnp.broadcast_to(ref[pl.ds(layer, 1), :], (rows, half))

    def source(layer):
        pull = near * row_of(left_ref, layer) + far * row_of(right_ref, layer)
        return weights[layer] * pull

    def emit(layer, values):
        stage_ref[layer] = values

    substitute(couple, inverse_ref, partial_ref, source, emit)
    place = pl.multiple_of(dep_ref[0] * depth, depth)
    edge_row = lax.broadcasted_iota(jnp.int32, (depth, rows, half), 1) == 0
    edge = left_ref[pl.ds(place, depth), :]
    modes = jnp.where(edge_row, edge[:, None, :], solved_ref[...] + stage_ref[pl.ds(place, depth)])
    sine, _ = parts_of(small_ref, depth * rows, depth)
    waves = from_modes(modes, sine)
    cells = dot3(split(waves), table, (((1,), (1,)), ((), ())))
    return cells.reshape(depth, rows, half)


def restore_kernel(
    dep_ref,
    back_ref,
    solved_ref,
    table_ref,
    small_ref,
    weight_ref,
    inverse_ref,
    bins_ref,
    own_ref,
    focus_ref,
    *scratch,
    ends,
):
    own_ref[...] = extend(
        dep_ref,
        back_ref,
        solved_ref,
        (table_ref[0], table_ref[1]),
        small_ref,
        weight_ref,
        inverse_ref,
        *scratch,
        ends,
    )
    focus_ref[...] = focusing(bins_ref[...])


def unfold_kernel(
    dep_ref,
    back_ref,
    solved_ref,
    table_ref,
    small_ref,
    weight_ref,
    inverse_ref,
    own_ref,
    focus_ref,
    out_hbm,
    out_ref,
    sems,
    *scratch,
    ends,
    scale,
    cuts,
):
    depth, _, half = own_ref.shape
    size = depth // cuts
    other = 1 - dep_ref[0]
    cells = extend(
        dep_ref,
        back_ref,
        solved_ref,
        (table_ref[other, 0], table_ref[other, 1]),
        small_ref,
        weight_ref,
        inverse_ref,
        *scratch,
        ends,
    )
    sign = jnp.where(dep_ref[0] == 0, scale, -scale).astype(f32)
    copies = []
    for cut in range(cuts):
        part = pl.ds(cut * size, size)
        own = own_ref[part]
        recv = cells[cut * size : (cut + 1) * size]
        focus_map = focus_ref[part]
        out_ref[part, :, :half] = focus_map[..., :half] * ((own + recv) * scale)
        out_ref[part, :, half:] = focus_map[..., half:] * ((own - recv) * sign)
        copy = pltpu.make_async_copy(out_ref.at[part], out_hbm.at[part], sems.at[cut])
        copy.start()
        copies.append(copy)
    for copy in copies:
        copy.wait()


def call(kernel, operands, out_shape, scratch=(), outside=False):
    specs = []
    values = []
    for space, value in operands:
        specs.append(pl.BlockSpec(memory_space=space))
        if space is pltpu.HBM:
            value = pltpu.with_memory_space_constraint(value, pltpu.HBM)
        values.append(value)
    out_space = pltpu.HBM if outside else pltpu.VMEM
    single = not isinstance(out_shape, list)
    out_specs = pl.BlockSpec(memory_space=out_space)
    return pl.pallas_call(
        kernel,
        in_specs=specs,
        out_specs=out_specs if single else [out_specs] * len(out_shape),
        out_shape=out_shape,
        scratch_shapes=list(scratch),
        compiler_params=pltpu.CompilerParams(vmem_limit_bytes=16 * 1024 * 1024),
    )(*values)


def body(residual, focus_bins, layer_class):
    depth, rows, x_cells = residual.shape
    half = x_cells // 2
    layers = layer_class.shape[0]
    hor_count = lax.axis_size("hor")
    y_cells = rows * hor_count
    chunk = half // hor_count
    plane_rows = rows * half // lanes
    dep = lax.axis_index("dep").astype(jnp.int32)
    hor = lax.axis_index("hor").astype(jnp.int32)
    dep_index = dep.reshape(1)
    spot = (hor * 2 + dep).reshape(1)

    table = np.stack(fold_tables(x_cells), axis=1)
    sine = sine_matrix(rows)
    near = np.concatenate([[0.0], sine[1, 1:]])
    far = np.concatenate([[0.0], sine[rows - 1, 1:]])
    lower_row = np.concatenate([[1.0], sine[1, 1:]])
    edge = np.concatenate([np.kron(np.eye(depth), row[None, :]) for row in (lower_row, far)])
    small = np.concatenate(split_table(np.kron(np.eye(depth), sine)) + split_table(edge))
    wave_x = np.stack(
        [symbol_of(2.0 * np.pi * (2 * np.arange(half) + parity) / x_cells) for parity in range(2)]
    )
    mode = symbol_of(np.pi * np.arange(rows) / rows)
    inner = damping + smoothing * (mode[None, :, None] + wave_x[:, None, :])
    lane = np.arange(lanes)
    wave_number = (lane // chunk)[None, :] * plane_rows + np.arange(plane_rows)[:, None]
    wave_y = symbol_of(2.0 * np.pi * wave_number / y_cells)
    spots = np.arange(hor_count)[:, None, None] * chunk + (lane % chunk)[None, None, :]
    spots = 2 * spots + np.arange(2)[None, :, None]
    wave_spots = symbol_of(2.0 * np.pi * spots / x_cells).reshape(2 * hor_count, lanes)
    outer = np.concatenate([wave_y, wave_spots]).astype(np.float32)

    def shape(*dims):
        return jax.ShapeDtypeStruct(dims, f32)

    def constant(value):
        return (pltpu.HBM, jnp.asarray(value))

    def scalar(value):
        return (pltpu.SMEM, value)

    def near_by(value):
        return (pltpu.VMEM, value)

    slab = (depth, rows, half)
    full = (depth, rows, x_cells)
    field = (layers, rows, half)
    packed = (hor_count, layers, lanes)
    plane = (layers, plane_rows, lanes)
    cuts = 4
    own, send, weight, small_here, inner_here, outer_here = call(
        functools.partial(fold_kernel, cuts=cuts // 2),
        [scalar(dep_index)]
        + [(pltpu.HBM, value) for value in (residual, focus_bins, layer_class)]
        + [constant(value) for value in (small, inner.astype(np.float32), outer)],
        [
            shape(*slab),
            shape(*slab),
            shape(layers, 8, lanes),
            jax.ShapeDtypeStruct(small.shape, bf16),
            shape(2, rows, half),
            shape(*outer.shape),
        ],
        [
            pltpu.VMEM(full, f32),
            pltpu.VMEM(full, jnp.int32),
            pltpu.SMEM((layers,), jnp.int32),
            pltpu.SemaphoreType.DMA((2, cuts // 2)),
            pltpu.SemaphoreType.DMA,
            pltpu.SemaphoreType.DMA((3,)),
        ],
    )
    pairs = [(0, 1), (1, 0)]
    recv = lax.ppermute(send, "dep", pairs)
    modes, table_here, inverse, inverse_other, inverse_outer = call(
        prepare_kernel,
        [scalar(dep_index), scalar(spot), near_by(own), near_by(weight), constant(table)]
        + [near_by(value) for value in (small_here, inner_here, outer_here)],
        [
            shape(*slab),
            jax.ShapeDtypeStruct((2, half, half), bf16),
            shape(*field),
            shape(*field),
            shape(*plane),
        ],
        [pltpu.SemaphoreType.DMA((2,))],
    )
    outgoing, keep, give = call(
        interior_kernel,
        [scalar(dep_index)]
        + [near_by(v) for v in (modes, recv, table_here, small_here, weight, inverse)],
        [shape(*packed), shape(*slab), shape(*slab)],
        [pltpu.VMEM(field, f32)] * 4,
    )
    got = lax.ppermute(give, "dep", pairs)
    incoming = lax.all_to_all(outgoing, "hor", split_axis=0, concat_axis=0, tiled=True)
    incoming, got = lax.optimization_barrier((incoming, got))
    answered = call(
        functools.partial(interface_kernel, chunk=chunk),
        [near_by(incoming), near_by(weight), near_by(inverse_outer)],
        shape(*packed),
        [pltpu.VMEM(packed, f32)] * 3 + [pltpu.VMEM(plane, f32)],
    )
    edges = lax.all_to_all(answered, "hor", split_axis=0, concat_axis=0, tiled=True)
    other_edges = lax.ppermute(edges, "dep", pairs)
    scratch = [pltpu.VMEM((layers, half), f32)] * 2 + [pltpu.VMEM(field, f32)] * 2
    own, focus_map = call(
        functools.partial(restore_kernel, ends=(near, far)),
        [scalar(dep_index)]
        + [
            near_by(v)
            for v in (edges, keep, table_here, small_here, weight, inverse, focus_bins)
        ],
        [shape(*slab), shape(*full)],
        scratch,
    )
    return call(
        functools.partial(unfold_kernel, ends=(near, far), scale=1.0 / x_cells, cuts=cuts),
        [scalar(dep_index)]
        + [
            near_by(v)
            for v in (
                other_edges,
                got,
                jnp.asarray(table),
                small_here,
                weight,
                inverse_other,
                own,
                focus_map,
            )
        ],
        shape(*full),
        [pltpu.VMEM(full, f32), pltpu.SemaphoreType.DMA((cuts,))] + scratch,
        outside=True,
    )


def solution(mesh):
    return jax.shard_map(
        body,
        mesh=mesh,
        in_specs=(P(("grp", "dep"), "hor", None), P(("grp", "dep"), "hor", None), P("grp")),
        out_specs=P(("grp", "dep"), "hor", None),
        check_vma=False,
    )
```

```python
import functools
import math

import jax
import jax.numpy as jnp
import ml_dtypes
import numpy as np
from jax import lax
from jax.experimental import pallas as pl
from jax.experimental.pallas import tpu as pltpu
from jax.sharding import PartitionSpec as P

damping = 0.01
smoothing = 1.0
coupling_scale = 1.0
weight_base = 0.5
weight_step = 0.2
focus_base = 0.5
focus_step = 0.09242
lanes = 128
f32 = jnp.float32
bf16 = jnp.bfloat16


def cas(angle):
    return np.cos(angle) + np.sin(angle)


def split_table(table):
    table = table.astype(np.float32)
    high = table.astype(ml_dtypes.bfloat16)
    low = (table - high.astype(np.float32)).astype(ml_dtypes.bfloat16)
    return high, low


def fold_tables(length):
    half = length // 2
    cell = np.arange(half)[:, None]
    tables = []
    for parity in range(2):
        wave = 2 * np.arange(half)[None, :] + parity
        tables.append(cas(2.0 * np.pi * (cell * wave % length) / length))
    return split_table(np.stack(tables))


def sine_matrix(rows):
    index = np.arange(1, rows)
    matrix = np.zeros((rows, rows))
    matrix[0, 0] = 1.0
    matrix[1:, 1:] = np.sqrt(2.0 / rows) * np.sin(np.pi * np.outer(index, index) / rows)
    return matrix


def symbol_of(angle):
    return 2.0 - 2.0 * np.cos(angle)


def split(values):
    high = values.astype(bf16)
    low = (values - high.astype(f32)).astype(bf16)
    return high, low


def dot3(left, right, dims=(((1,), (0,)), ((), ()))):
    dot = functools.partial(lax.dot_general, dimension_numbers=dims, preferred_element_type=f32)
    left_high, left_low = left
    right_high, right_low = right
    rows = left_high.shape[0]
    both = dot(jnp.concatenate([left_high, left_low], axis=0), right_high)
    return both[:rows] + (both[rows:] + dot(left_high, right_low))


def focusing(focus_bins):
    return focus_base * jnp.exp(focus_step * focus_bins.astype(f32))


def layer_weights(class_ref, weight_ref):
    for layer in range(weight_ref.shape[0]):
        level = jnp.full(weight_ref.shape[1:], class_ref[layer], jnp.int32).astype(f32)
        weight_ref[layer] = weight_base * jnp.exp(weight_step * level)


def layer_terms(weight_ref, plane_tiles, axis):
    layers = weight_ref.shape[0]
    weights = [weight_ref[layer] for layer in range(layers)]
    couple = [coupling_scale * weights[k] * weights[k + 1] for k in range(layers - 1)]

    def spread(values):
        return [jnp.concatenate([value] * plane_tiles, axis=axis) for value in values]

    return spread(weights), spread(couple)


def row_values(values, shape):
    row = lax.broadcasted_iota(jnp.int32, shape, 0)
    total = jnp.full(shape, float(values[0]), f32)
    for index in range(1, len(values)):
        total = jnp.where(row == index, float(values[index]), total)
    return total


def diagonal(layer, weights, couple, wave):
    total = weights[layer] * wave
    if layer > 0:
        total = total + couple[layer - 1]
    if layer < len(couple):
        total = total + couple[layer]
    return total


def factor(weights, couple, wave, inverse_ref):
    layers = len(weights)
    half = layers // 2
    top = 1.0 / diagonal(0, weights, couple, wave)
    bottom = 1.0 / diagonal(layers - 1, weights, couple, wave)
    inverse_ref[0] = top
    inverse_ref[layers - 1] = bottom
    for step in range(1, half):
        low = step
        link = couple[low - 1]
        top = 1.0 / (diagonal(low, weights, couple, wave) - link * link * top)
        inverse_ref[low] = top
        high = layers - 1 - step
        link = couple[high]
        pivot = diagonal(high, weights, couple, wave) - link * link * bottom
        if step == half - 1:
            link = couple[half - 1]
            pivot = pivot - link * link * top
        bottom = 1.0 / pivot
        inverse_ref[high] = bottom


def substitute(couple, inverse_ref, partial_ref, source, emit):
    layers = len(couple) + 1
    half = layers // 2
    top = source(0)
    bottom = source(layers - 1)
    partial_ref[0] = top
    partial_ref[layers - 1] = bottom
    for step in range(1, half):
        low = step
        top = source(low) + couple[low - 1] * inverse_ref[low - 1] * top
        partial_ref[low] = top
        high = layers - 1 - step
        bottom = source(high) + couple[high] * inverse_ref[high + 1] * bottom
        partial_ref[high] = bottom
    link = couple[half - 1]
    bottom = (bottom + link * inverse_ref[half - 1] * top) * inverse_ref[half]
    top = (top + link * bottom) * inverse_ref[half - 1]
    emit(half, bottom)
    emit(half - 1, top)
    for step in range(1, half):
        low = half - 1 - step
        top = (partial_ref[low] + couple[low] * top) * inverse_ref[low]
        emit(low, top)
        high = half + step
        bottom = (partial_ref[high] + couple[high - 1] * bottom) * inverse_ref[high]
        emit(high, bottom)


def turn(values, shift):
    shift = shift % lanes
    return values if shift == 0 else pltpu.roll(values, shift, values.ndim - 1)


def fold_kernel(
    dep_ref,
    residual_hbm,
    bins_hbm,
    class_hbm,
    small_hbm,
    inner_hbm,
    outer_hbm,
    own_ref,
    send_ref,
    weight_ref,
    small_ref,
    inner_ref,
    outer_ref,
    residual_ref,
    bins_ref,
    class_ref,
    sems,
    class_sem,
    table_sems,
    *,
    cuts,
):
    depth, _, half = own_ref.shape
    size = depth // cuts
    class_copy = pltpu.make_async_copy(class_hbm, class_ref, class_sem)
    class_copy.start()
    copies = []
    for cut in range(cuts):
        part = pl.ds(cut * size, size)
        first = pltpu.make_async_copy(bins_hbm.at[part], bins_ref.at[part], sems.at[0, cut])
        second = pltpu.make_async_copy(
            residual_hbm.at[part], residual_ref.at[part], sems.at[1, cut]
        )
        first.start()
        second.start()
        copies.append((first, second))
    tables = [
        pltpu.make_async_copy(inner_hbm, inner_ref, table_sems.at[0]),
        pltpu.make_async_copy(outer_hbm, outer_ref, table_sems.at[1]),
        pltpu.make_async_copy(small_hbm, small_ref, table_sems.at[2]),
    ]
    for copy in tables:
        copy.start()
    sign = jnp.where(dep_ref[0] == 0, 1.0, -1.0).astype(f32)
    class_copy.wait()
    layer_weights(class_ref, weight_ref)
    for cut in range(cuts):
        part = pl.ds(cut * size, size)
        copies[cut][0].wait()
        focus_map = focusing(bins_ref[part])
        copies[cut][1].wait()
        scaled = focus_map * residual_ref[part]
        left = scaled[..., :half]
        right = sign * scaled[..., half:]
        own_ref[part] = left + right
        send_ref[part] = left - right
    for copy in tables:
        copy.wait()


def dot2(left, right):
    return jnp.dot(left, right, preferred_element_type=f32)


def to_modes(cells, table, sine):
    return dot3(split(from_modes(cells, sine)), table).reshape(cells.shape)


def from_modes(modes, sine):
    depth, rows, half = modes.shape
    return dot3(sine, split(modes.reshape(depth * rows, half)))


def parts_of(small_ref, block, depth):
    cuts = np.cumsum([0, block, block, 2 * depth, 2 * depth])
    pieces = [small_ref[low:high] for low, high in zip(cuts[:-1], cuts[1:])]
    return (pieces[0], pieces[1]), (pieces[2], pieces[3])


def prepare_kernel(
    dep_ref,
    spot_ref,
    own_ref,
    weight_ref,
    table_hbm,
    small_ref,
    inner_ref,
    outer_ref,
    modes_ref,
    table_ref,
    inverse_ref,
    inverse_other_ref,
    inverse_outer_ref,
    sems,
):
    copies = [
        pltpu.make_async_copy(table_hbm.at[dep_ref[0], part], table_ref.at[part], sems.at[part])
        for part in range(2)
    ]
    for copy in copies:
        copy.start()
    depth, rows, half = own_ref.shape
    plane_rows = inverse_outer_ref.shape[1]
    weights, couple = layer_terms(weight_ref, half // lanes, 1)
    factor(weights, couple, inner_ref[dep_ref[0]], inverse_ref)
    factor(weights, couple, inner_ref[1 - dep_ref[0]], inverse_other_ref)
    weights, couple = layer_terms(weight_ref, plane_rows // 8, 0)
    wave = outer_ref[:plane_rows] + outer_ref[pl.ds(plane_rows + spot_ref[0], 1), :]
    factor(weights, couple, damping + smoothing * wave, inverse_outer_ref)
    sine, _ = parts_of(small_ref, depth * rows, depth)
    high, low = split(from_modes(own_ref[...], sine))
    block = depth * rows
    copies[0].wait()
    both = dot2(jnp.concatenate([high, low], axis=0), table_ref[0])
    copies[1].wait()
    total = both[:block] + (both[block:] + dot2(high, table_ref[1]))
    modes_ref[...] = total.reshape(depth, rows, half)


def interior_kernel(
    dep_ref,
    modes_ref,
    recv_ref,
    table_ref,
    small_ref,
    weight_ref,
    inverse_ref,
    packed_ref,
    keep_ref,
    give_ref,
    source_ref,
    solved_ref,
    stage_ref,
    partial_ref,
):
    depth, rows, half = recv_ref.shape
    layers = 2 * depth
    block = depth * rows
    hor_count = packed_ref.shape[0]
    chunk = half // hor_count
    place = dep_ref[0] * depth
    sine, edge = parts_of(small_ref, block, depth)
    source_ref[pl.ds(place, depth)] = modes_ref[...]
    source_ref[pl.ds(depth - place, depth)] = to_modes(
        recv_ref[...], (table_ref[0], table_ref[1]), sine
    )
    weights, couple = layer_terms(weight_ref, half // lanes, 1)
    edge_row = lax.broadcasted_iota(jnp.int32, (rows, half), 0) == 0

    def emit(layer, values):
        solved_ref[layer] = values
        stage_ref[layer] = jnp.where(edge_row, source_ref[layer], weights[layer] * values)

    substitute(couple, inverse_ref, partial_ref, lambda layer: source_ref[layer], emit)
    keep_ref[...] = solved_ref[pl.ds(place, depth)]
    give_ref[...] = solved_ref[pl.ds(depth - place, depth)]
    lower = []
    upper = []
    for part in range(2):
        both = from_modes(stage_ref[part * depth : (part + 1) * depth], edge)
        lower.append(both[:depth])
        upper.append(both[depth:])
    lower = jnp.concatenate(lower, axis=0)
    upper = jnp.concatenate(upper, axis=0)
    lane = lax.broadcasted_iota(jnp.int32, (layers, lanes), 1)
    if 2 * chunk == lanes:
        for tile in range(hor_count // 2):
            here = lower[:, tile * lanes : (tile + 1) * lanes]
            there = turn(upper[:, tile * lanes : (tile + 1) * lanes], chunk)
            packed_ref[2 * tile] = jnp.where(lane < chunk, here, there)
            packed_ref[2 * tile + 1] = jnp.where(lane < chunk, there, here)
        return
    for index in range(hor_count):
        tile = index * chunk // lanes * lanes
        offset = index * chunk % lanes
        packed_ref[index] = jnp.where(
            lane < chunk,
            turn(lower[:, tile : tile + lanes], -offset),
            turn(upper[:, tile : tile + lanes], chunk - offset),
        )


def hartley_8(read, write):
    parts = [read(index) for index in range(8)]
    plus = [parts[index] + parts[index + 4] for index in range(4)]
    minus = [parts[index] - parts[index + 4] for index in range(4)]
    root = math.sqrt(2.0)
    one, three = minus[1] * root, minus[3] * root
    same, cross = plus[0] + plus[2], plus[1] + plus[3]
    write(0, same + cross)
    write(4, same - cross)
    same, cross = plus[0] - plus[2], plus[1] - plus[3]
    write(2, same + cross)
    write(6, same - cross)
    same, cross = minus[0] + minus[2], minus[0] - minus[2]
    write(1, same + one)
    write(5, same - one)
    write(3, cross + three)
    write(7, cross - three)


def small_hartley(count, read, write, shape):
    if count == 8:
        hartley_8(read, write)
        return
    if count <= 8:
        table = cas(2.0 * np.pi * (np.outer(np.arange(count), np.arange(count)) % count) / count)
        parts = [read(index) for index in range(count)]
        for wave in range(count):
            total = None
            for index in range(count):
                value = float(table[wave, index])
                if abs(value) < 1e-12:
                    continue
                if abs(value - 1.0) < 1e-12:
                    term = parts[index]
                elif abs(value + 1.0) < 1e-12:
                    term = -parts[index]
                else:
                    term = parts[index] * value
                total = term if total is None else total + term
            write(wave, total)
        return

    def outer(wave, carry):
        def inner(index, total):
            angle = jnp.full(shape, wave * index % count, jnp.int32).astype(f32)
            angle = angle * (2.0 * math.pi / count)
            return total + read(index) * (jnp.cos(angle) + jnp.sin(angle))

        write(wave, lax.fori_loop(0, count, inner, jnp.zeros(shape, f32)))
        return carry

    lax.fori_loop(0, count, outer, 0)


def interface_kernel(
    spot_ref,
    packed_ref,
    weight_ref,
    inverse_ref,
    back_ref,
    sum_ref,
    wave_ref,
    answer_ref,
    partial_ref,
    *,
    chunk,
):
    hor_count, layers, _ = packed_ref.shape
    rows = inverse_ref.shape[1]
    subsets = lanes // chunk
    classes = max(1, hor_count // rows)
    repeats = max(1, rows // hor_count)
    lane = lax.broadcasted_iota(jnp.int32, (layers, lanes), 1)
    swapped = spot_ref[0] // 2 % 2 if 2 * chunk == lanes else 0
    first = lane // chunk % 2 == swapped

    def halves(index):
        values = packed_ref[index]
        width = 2 * chunk
        while width < lanes:
            values = jnp.where(lane < width, values, turn(values, width))
            width = width * 2
        return values

    def joined(index):
        here = halves(index)
        before = halves((index + hor_count - 1) % hor_count)
        return jnp.where(first, here, turn(here, chunk)) + jnp.where(
            first, turn(before, -chunk), before
        )

    def put_sum(index, values):
        sum_ref[index] = values

    if hor_count <= 8:
        pairs = []
        for index in range(hor_count):
            here = halves(index)
            there = turn(here, chunk)
            back = there if 2 * chunk == lanes else turn(here, -chunk)
            pairs.append((jnp.where(first, here, there), jnp.where(first, back, here)))
        joint = [pairs[index][0] + pairs[index - 1][1] for index in range(hor_count)]
        small_hartley(hor_count, joint.__getitem__, lambda k, v: wave_ref.__setitem__(k, v), (layers, lanes))
    else:
        lax.fori_loop(0, hor_count, lambda k, c: (put_sum(k, joined(k)), c)[1], 0)
        small_hartley(
            hor_count,
            lambda k: sum_ref[k],
            lambda k, v: wave_ref.__setitem__(k, v),
            (layers, lanes),
        )
    weights, couple = layer_terms(weight_ref, rows // 8, 0)
    plane_lane = lax.broadcasted_iota(jnp.int32, (rows, lanes), 1)
    group = plane_lane // chunk % classes

    def source(layer):
        if classes == 1:
            return jnp.concatenate([wave_ref[:, layer, :]] * repeats, axis=0)
        total = wave_ref[0:rows, layer, :]
        for part in range(1, classes):
            piece = wave_ref[part * rows : (part + 1) * rows, layer, :]
            total = jnp.where(group == part, piece, total)
        return total

    def emit(layer, values):
        if classes == 1:
            total = values[0:hor_count]
            for part in range(1, repeats):
                total = total + values[part * hor_count : (part + 1) * hor_count]
            answer_ref[:, layer, :] = total
            return
        for part in range(classes):
            answer_ref[part * rows : (part + 1) * rows, layer, :] = jnp.where(
                group == part, values, 0.0
            )

    substitute(couple, inverse_ref, partial_ref, source, emit)

    def gathered(index):
        values = answer_ref[index]
        shift = chunk
        while shift < lanes:
            values = values + turn(values, shift)
            shift = shift * 2
        return values

    scale = 1.0 / (rows * subsets)

    def put_scaled(index, values):
        sum_ref[index] = values * scale

    if hor_count <= 8:
        small_hartley(hor_count, gathered, put_scaled, (layers, lanes))
    else:
        lax.fori_loop(
            0, hor_count, lambda k, c: (wave_ref.__setitem__(k, gathered(k)), c)[1], 0
        )
        small_hartley(hor_count, lambda k: wave_ref[k], put_scaled, (layers, lanes))
    for index in range(hor_count):
        back_ref[index] = jnp.where(first, sum_ref[index], sum_ref[(index + 1) % hor_count])


def extend(
    dep_ref,
    back_ref,
    solved_ref,
    table,
    small_ref,
    weight_ref,
    inverse_ref,
    left_ref,
    right_ref,
    stage_ref,
    partial_ref,
    ends,
):
    depth, rows, half = solved_ref.shape
    layers = 2 * depth
    hor_count = back_ref.shape[0]
    chunk = half // hor_count
    lane = lax.broadcasted_iota(jnp.int32, (layers, lanes), 1)
    for tile in range(half // lanes if 2 * chunk == lanes else 0):
        even = back_ref[2 * tile]
        odd = back_ref[2 * tile + 1]
        inside = lane < chunk
        left_ref[:, tile * lanes : (tile + 1) * lanes] = jnp.where(inside, even, odd)
        right = turn(jnp.where(inside, odd, even), chunk)
        right_ref[:, tile * lanes : (tile + 1) * lanes] = right
    for tile in range(0 if 2 * chunk == lanes else half // lanes):
        left = None
        right = None
        for index in range(tile * lanes // chunk, (tile + 1) * lanes // chunk):
            offset = index * chunk % lanes
            values = back_ref[index]
            left_part = turn(values, offset)
            right_part = turn(values, offset - chunk)
            inside = lane >= offset
            left = left_part if left is None else jnp.where(inside, left_part, left)
            right = right_part if right is None else jnp.where(inside, right_part, right)
        left_ref[:, tile * lanes : (tile + 1) * lanes] = left
        right_ref[:, tile * lanes : (tile + 1) * lanes] = right
    weights, couple = layer_terms(weight_ref, half // lanes, 1)
    near = row_values(ends[0], (rows, half))
    far = row_values(ends[1], (rows, half))

    def row_of(ref, layer):
        return jnp.broadcast_to(ref[pl.ds(layer, 1), :], (rows, half))

    def source(layer):
        pull = near * row_of(left_ref, layer) + far * row_of(right_ref, layer)
        return weights[layer] * pull

    def emit(layer, values):
        stage_ref[layer] = values

    substitute(couple, inverse_ref, partial_ref, source, emit)
    place = pl.multiple_of(dep_ref[0] * depth, depth)
    edge_row = lax.broadcasted_iota(jnp.int32, (depth, rows, half), 1) == 0
    edge = left_ref[pl.ds(place, depth), :]
    modes = jnp.where(edge_row, edge[:, None, :], solved_ref[...] + stage_ref[pl.ds(place, depth)])
    sine, _ = parts_of(small_ref, depth * rows, depth)
    waves = from_modes(modes, sine)
    cells = dot3(split(waves), table, (((1,), (1,)), ((), ())))
    return cells.reshape(depth, rows, half)


def restore_kernel(
    dep_ref,
    back_ref,
    solved_ref,
    table_ref,
    small_ref,
    weight_ref,
    inverse_ref,
    bins_ref,
    base_ref,
    gain_ref,
    *scratch,
    ends,
    scale,
):
    half = solved_ref.shape[-1]
    sign = jnp.where(dep_ref[0] == 0, -scale, scale).astype(f32)
    gain_ref[:, :, :half] = focusing(bins_ref[:, :, :half]) * scale
    gain_ref[:, :, half:] = focusing(bins_ref[:, :, half:]) * sign
    cells = extend(
        dep_ref,
        back_ref,
        solved_ref,
        (table_ref[0], table_ref[1]),
        small_ref,
        weight_ref,
        inverse_ref,
        *scratch,
        ends,
    )
    base_ref[:, :, :half] = gain_ref[:, :, :half] * cells
    base_ref[:, :, half:] = -(gain_ref[:, :, half:] * cells)


def unfold_kernel(
    dep_ref,
    back_ref,
    solved_ref,
    table_ref,
    small_ref,
    weight_ref,
    inverse_ref,
    base_ref,
    gain_ref,
    out_hbm,
    out_ref,
    sems,
    *scratch,
    ends,
    cuts,
):
    depth, _, half = solved_ref.shape
    size = depth // cuts
    other = 1 - dep_ref[0]
    cells = extend(
        dep_ref,
        back_ref,
        solved_ref,
        (table_ref[other, 0], table_ref[other, 1]),
        small_ref,
        weight_ref,
        inverse_ref,
        *scratch,
        ends,
    )
    copies = []
    for cut in range(cuts):
        part = slice(cut * size, (cut + 1) * size)
        out_ref[part, :, :half] = base_ref[part, :, :half] + gain_ref[part, :, :half] * cells[part]
        out_ref[part, :, half:] = base_ref[part, :, half:] + gain_ref[part, :, half:] * cells[part]
        copy = pltpu.make_async_copy(out_ref.at[part], out_hbm.at[part], sems.at[cut])
        copy.start()
        copies.append(copy)
    for copy in copies:
        copy.wait()


def call(kernel, operands, out_shape, scratch=(), outside=False):
    specs = []
    values = []
    for space, value in operands:
        specs.append(pl.BlockSpec(memory_space=space))
        if space is pltpu.HBM:
            value = pltpu.with_memory_space_constraint(value, pltpu.HBM)
        values.append(value)
    out_space = pltpu.HBM if outside else pltpu.VMEM
    single = not isinstance(out_shape, list)
    out_specs = pl.BlockSpec(memory_space=out_space)
    return pl.pallas_call(
        kernel,
        in_specs=specs,
        out_specs=out_specs if single else [out_specs] * len(out_shape),
        out_shape=out_shape,
        scratch_shapes=list(scratch),
        compiler_params=pltpu.CompilerParams(vmem_limit_bytes=16 * 1024 * 1024),
    )(*values)


def body(residual, focus_bins, layer_class):
    depth, rows, x_cells = residual.shape
    half = x_cells // 2
    layers = layer_class.shape[0]
    hor_count = lax.axis_size("hor")
    y_cells = rows * hor_count
    chunk = half // hor_count
    plane_rows = rows * half // lanes
    dep = lax.axis_index("dep").astype(jnp.int32)
    hor = lax.axis_index("hor").astype(jnp.int32)
    dep_index = dep.reshape(1)
    spot = (hor * 2 + dep).reshape(1)

    table = np.stack(fold_tables(x_cells), axis=1)
    sine = sine_matrix(rows)
    near = np.concatenate([[0.0], sine[1, 1:]])
    far = np.concatenate([[0.0], sine[rows - 1, 1:]])
    lower_row = np.concatenate([[1.0], sine[1, 1:]])
    edge = np.concatenate([np.kron(np.eye(depth), row[None, :]) for row in (lower_row, far)])
    small = np.concatenate(split_table(np.kron(np.eye(depth), sine)) + split_table(edge))
    wave_x = np.stack(
        [symbol_of(2.0 * np.pi * (2 * np.arange(half) + parity) / x_cells) for parity in range(2)]
    )
    mode = symbol_of(np.pi * np.arange(rows) / rows)
    inner = damping + smoothing * (mode[None, :, None] + wave_x[:, None, :])
    lane = np.arange(lanes)
    wave_number = (lane // chunk)[None, :] * plane_rows + np.arange(plane_rows)[:, None]
    wave_y = symbol_of(2.0 * np.pi * wave_number / y_cells)
    spots = np.arange(hor_count)[:, None, None] * chunk + (lane % chunk)[None, None, :]
    spots = 2 * spots + np.arange(2)[None, :, None]
    wave_spots = symbol_of(2.0 * np.pi * spots / x_cells).reshape(2 * hor_count, lanes)
    outer = np.concatenate([wave_y, wave_spots]).astype(np.float32)

    def shape(*dims):
        return jax.ShapeDtypeStruct(dims, f32)

    def constant(value):
        return (pltpu.HBM, jnp.asarray(value))

    def scalar(value):
        return (pltpu.SMEM, value)

    def near_by(value):
        return (pltpu.VMEM, value)

    slab = (depth, rows, half)
    full = (depth, rows, x_cells)
    field = (layers, rows, half)
    packed = (hor_count, layers, lanes)
    plane = (layers, plane_rows, lanes)
    cuts = 4
    own, send, weight, small_here, inner_here, outer_here = call(
        functools.partial(fold_kernel, cuts=cuts // 2),
        [scalar(dep_index)]
        + [(pltpu.HBM, value) for value in (residual, focus_bins, layer_class)]
        + [constant(value) for value in (small, inner.astype(np.float32), outer)],
        [
            shape(*slab),
            shape(*slab),
            shape(layers, 8, lanes),
            jax.ShapeDtypeStruct(small.shape, bf16),
            shape(2, rows, half),
            shape(*outer.shape),
        ],
        [
            pltpu.VMEM(full, f32),
            pltpu.VMEM(full, jnp.int32),
            pltpu.SMEM((layers,), jnp.int32),
            pltpu.SemaphoreType.DMA((2, cuts // 2)),
            pltpu.SemaphoreType.DMA,
            pltpu.SemaphoreType.DMA((3,)),
        ],
    )
    pairs = [(0, 1), (1, 0)]
    recv = lax.ppermute(send, "dep", pairs)
    modes, table_here, inverse, inverse_other, inverse_outer = call(
        prepare_kernel,
        [scalar(dep_index), scalar(spot), near_by(own), near_by(weight), constant(table)]
        + [near_by(value) for value in (small_here, inner_here, outer_here)],
        [
            shape(*slab),
            jax.ShapeDtypeStruct((2, half, half), bf16),
            shape(*field),
            shape(*field),
            shape(*plane),
        ],
        [pltpu.SemaphoreType.DMA((2,))],
    )
    outgoing, keep, give = call(
        interior_kernel,
        [scalar(dep_index)]
        + [near_by(v) for v in (modes, recv, table_here, small_here, weight, inverse)],
        [shape(*packed), shape(*slab), shape(*slab)],
        [pltpu.VMEM(field, f32)] * 4,
    )
    got = lax.ppermute(give, "dep", pairs)
    incoming = lax.all_to_all(outgoing, "hor", split_axis=0, concat_axis=0, tiled=True)
    incoming, got = lax.optimization_barrier((incoming, got))
    answered = call(
        functools.partial(interface_kernel, chunk=chunk),
        [scalar(spot), near_by(incoming), near_by(weight), near_by(inverse_outer)],
        shape(*packed),
        [pltpu.VMEM(packed, f32)] * 3 + [pltpu.VMEM(plane, f32)],
    )
    edges = lax.all_to_all(answered, "hor", split_axis=0, concat_axis=0, tiled=True)
    other_edges = lax.ppermute(edges, "dep", pairs)
    scratch = [pltpu.VMEM((layers, half), f32)] * 2 + [pltpu.VMEM(field, f32)] * 2
    base, gain = call(
        functools.partial(restore_kernel, ends=(near, far), scale=1.0 / x_cells),
        [scalar(dep_index)]
        + [
            near_by(v)
            for v in (edges, keep, table_here, small_here, weight, inverse, focus_bins)
        ],
        [shape(*full)] * 2,
        scratch,
    )
    return call(
        functools.partial(unfold_kernel, ends=(near, far), cuts=cuts),
        [scalar(dep_index)]
        + [
            near_by(v)
            for v in (
                other_edges,
                got,
                jnp.asarray(table),
                small_here,
                weight,
                inverse_other,
                base,
                gain,
            )
        ],
        shape(*full),
        [pltpu.VMEM(full, f32), pltpu.SemaphoreType.DMA((cuts,))] + scratch,
        outside=True,
    )


def solution(mesh):
    return jax.shard_map(
        body,
        mesh=mesh,
        in_specs=(P(("grp", "dep"), "hor", None), P(("grp", "dep"), "hor", None), P("grp")),
        out_specs=P(("grp", "dep"), "hor", None),
        check_vma=False,
    )
```

```python
import functools
import math

import jax
import jax.numpy as jnp
import ml_dtypes
import numpy as np
from jax import lax
from jax.experimental import pallas as pl
from jax.experimental.pallas import tpu as pltpu
from jax.sharding import PartitionSpec as P

damping = 0.01
smoothing = 1.0
coupling_scale = 1.0
weight_base = 0.5
weight_step = 0.2
focus_base = 0.5
focus_step = 0.09242
lanes = 128
f32 = jnp.float32
bf16 = jnp.bfloat16


def cas(angle):
    return np.cos(angle) + np.sin(angle)


def split_table(table):
    table = table.astype(np.float32)
    high = table.astype(ml_dtypes.bfloat16)
    low = (table - high.astype(np.float32)).astype(ml_dtypes.bfloat16)
    return high, low


def fold_tables(length):
    half = length // 2
    cell = np.arange(half)[:, None]
    tables = []
    for parity in range(2):
        wave = 2 * np.arange(half)[None, :] + parity
        tables.append(cas(2.0 * np.pi * (cell * wave % length) / length))
    return split_table(np.stack(tables))


def sine_matrix(rows):
    index = np.arange(1, rows)
    matrix = np.zeros((rows, rows))
    matrix[0, 0] = 1.0
    matrix[1:, 1:] = np.sqrt(2.0 / rows) * np.sin(np.pi * np.outer(index, index) / rows)
    return matrix


def symbol_of(angle):
    return 2.0 - 2.0 * np.cos(angle)


def split(values):
    high = values.astype(bf16)
    low = (values - high.astype(f32)).astype(bf16)
    return high, low


def dot3(left, right, dims=(((1,), (0,)), ((), ()))):
    dot = functools.partial(lax.dot_general, dimension_numbers=dims, preferred_element_type=f32)
    left_high, left_low = left
    right_high, right_low = right
    rows = left_high.shape[0]
    both = dot(jnp.concatenate([left_high, left_low], axis=0), right_high)
    return both[:rows] + (both[rows:] + dot(left_high, right_low))


def focusing(focus_bins):
    return focus_base * jnp.exp(focus_step * focus_bins.astype(f32))


def layer_weights(class_ref, weight_ref):
    for layer in range(weight_ref.shape[0]):
        level = jnp.full(weight_ref.shape[1:], class_ref[layer], jnp.int32).astype(f32)
        weight_ref[layer] = weight_base * jnp.exp(weight_step * level)


def layer_terms(weight_ref, plane_tiles, axis):
    layers = weight_ref.shape[0]
    weights = [weight_ref[layer] for layer in range(layers)]
    couple = [coupling_scale * weights[k] * weights[k + 1] for k in range(layers - 1)]

    def spread(values):
        return [jnp.concatenate([value] * plane_tiles, axis=axis) for value in values]

    return spread(weights), spread(couple)


def row_values(values, shape):
    row = lax.broadcasted_iota(jnp.int32, shape, 0)
    total = jnp.full(shape, float(values[0]), f32)
    for index in range(1, len(values)):
        total = jnp.where(row == index, float(values[index]), total)
    return total


def diagonal(layer, weights, couple, wave):
    total = weights[layer] * wave
    if layer > 0:
        total = total + couple[layer - 1]
    if layer < len(couple):
        total = total + couple[layer]
    return total


def factor(weights, couple, wave, inverse_ref):
    layers = len(weights)
    half = layers // 2
    top = 1.0 / diagonal(0, weights, couple, wave)
    bottom = 1.0 / diagonal(layers - 1, weights, couple, wave)
    inverse_ref[0] = top
    inverse_ref[layers - 1] = bottom
    for step in range(1, half):
        low = step
        link = couple[low - 1]
        top = 1.0 / (diagonal(low, weights, couple, wave) - link * link * top)
        inverse_ref[low] = top
        high = layers - 1 - step
        link = couple[high]
        pivot = diagonal(high, weights, couple, wave) - link * link * bottom
        if step == half - 1:
            link = couple[half - 1]
            pivot = pivot - link * link * top
        bottom = 1.0 / pivot
        inverse_ref[high] = bottom


def substitute(couple, inverse_ref, partial_ref, source, emit):
    layers = len(couple) + 1
    half = layers // 2
    top = source(0)
    bottom = source(layers - 1)
    partial_ref[0] = top
    partial_ref[layers - 1] = bottom
    for step in range(1, half):
        low = step
        top = source(low) + couple[low - 1] * inverse_ref[low - 1] * top
        partial_ref[low] = top
        high = layers - 1 - step
        bottom = source(high) + couple[high] * inverse_ref[high + 1] * bottom
        partial_ref[high] = bottom
    link = couple[half - 1]
    bottom = (bottom + link * inverse_ref[half - 1] * top) * inverse_ref[half]
    top = (top + link * bottom) * inverse_ref[half - 1]
    emit(half, bottom)
    emit(half - 1, top)
    for step in range(1, half):
        low = half - 1 - step
        top = (partial_ref[low] + couple[low] * top) * inverse_ref[low]
        emit(low, top)
        high = half + step
        bottom = (partial_ref[high] + couple[high - 1] * bottom) * inverse_ref[high]
        emit(high, bottom)


def turn(values, shift):
    shift = shift % lanes
    return values if shift == 0 else pltpu.roll(values, shift, values.ndim - 1)


def fold_kernel(
    dep_ref,
    residual_hbm,
    bins_hbm,
    class_hbm,
    small_hbm,
    inner_hbm,
    outer_hbm,
    own_ref,
    send_ref,
    weight_ref,
    small_ref,
    inner_ref,
    outer_ref,
    residual_ref,
    bins_ref,
    class_ref,
    sems,
    class_sem,
    table_sems,
    *,
    cuts,
):
    depth, _, half = own_ref.shape
    size = depth // cuts
    class_copy = pltpu.make_async_copy(class_hbm, class_ref, class_sem)
    class_copy.start()
    copies = []
    for cut in range(cuts):
        part = pl.ds(cut * size, size)
        first = pltpu.make_async_copy(bins_hbm.at[part], bins_ref.at[part], sems.at[0, cut])
        second = pltpu.make_async_copy(
            residual_hbm.at[part], residual_ref.at[part], sems.at[1, cut]
        )
        first.start()
        second.start()
        copies.append((first, second))
    tables = [
        pltpu.make_async_copy(inner_hbm, inner_ref, table_sems.at[0]),
        pltpu.make_async_copy(outer_hbm, outer_ref, table_sems.at[1]),
        pltpu.make_async_copy(small_hbm, small_ref, table_sems.at[2]),
    ]
    for copy in tables:
        copy.start()
    sign = jnp.where(dep_ref[0] == 0, 1.0, -1.0).astype(f32)
    class_copy.wait()
    layer_weights(class_ref, weight_ref)
    for cut in range(cuts):
        part = pl.ds(cut * size, size)
        copies[cut][0].wait()
        focus_map = focusing(bins_ref[part])
        copies[cut][1].wait()
        scaled = focus_map * residual_ref[part]
        left = scaled[..., :half]
        right = sign * scaled[..., half:]
        own_ref[part] = left + right
        send_ref[part] = left - right
    for copy in tables:
        copy.wait()


def dot2(left, right):
    return jnp.dot(left, right, preferred_element_type=f32)


def to_modes(cells, table, sine):
    return dot3(split(from_modes(cells, sine)), table).reshape(cells.shape)


def from_modes(modes, sine):
    depth, rows, half = modes.shape
    high, low = split(modes.reshape(depth * rows, half))
    return dot2(sine, jnp.concatenate([high, low, high], axis=0))


def parts_of(small_ref, block, depth):
    return small_ref[:block], small_ref[block : block + 2 * depth]


def prepare_kernel(
    dep_ref,
    spot_ref,
    own_ref,
    weight_ref,
    table_hbm,
    small_ref,
    inner_ref,
    outer_ref,
    modes_ref,
    table_ref,
    inverse_ref,
    inverse_other_ref,
    inverse_outer_ref,
    sems,
):
    copies = [
        pltpu.make_async_copy(table_hbm.at[dep_ref[0], part], table_ref.at[part], sems.at[part])
        for part in range(2)
    ]
    for copy in copies:
        copy.start()
    depth, rows, half = own_ref.shape
    plane_rows = inverse_outer_ref.shape[1]
    weights, couple = layer_terms(weight_ref, half // lanes, 1)
    factor(weights, couple, inner_ref[dep_ref[0]], inverse_ref)
    factor(weights, couple, inner_ref[1 - dep_ref[0]], inverse_other_ref)
    weights, couple = layer_terms(weight_ref, plane_rows // 8, 0)
    wave = outer_ref[:plane_rows] + outer_ref[pl.ds(plane_rows + spot_ref[0], 1), :]
    factor(weights, couple, damping + smoothing * wave, inverse_outer_ref)
    sine, _ = parts_of(small_ref, depth * rows, depth)
    high, low = split(from_modes(own_ref[...], sine))
    block = depth * rows
    copies[0].wait()
    both = dot2(jnp.concatenate([high, low], axis=0), table_ref[0])
    copies[1].wait()
    total = both[:block] + (both[block:] + dot2(high, table_ref[1]))
    modes_ref[...] = total.reshape(depth, rows, half)


def interior_kernel(
    dep_ref,
    modes_ref,
    recv_ref,
    table_ref,
    small_ref,
    weight_ref,
    inverse_ref,
    packed_ref,
    keep_ref,
    give_ref,
    source_ref,
    solved_ref,
    stage_ref,
    partial_ref,
):
    depth, rows, half = recv_ref.shape
    layers = 2 * depth
    block = depth * rows
    hor_count = packed_ref.shape[0]
    chunk = half // hor_count
    place = dep_ref[0] * depth
    sine, edge = parts_of(small_ref, block, depth)
    source_ref[pl.ds(place, depth)] = modes_ref[...]
    source_ref[pl.ds(depth - place, depth)] = to_modes(
        recv_ref[...], (table_ref[0], table_ref[1]), sine
    )
    weights, couple = layer_terms(weight_ref, half // lanes, 1)
    edge_row = lax.broadcasted_iota(jnp.int32, (rows, half), 0) == 0

    def emit(layer, values):
        solved_ref[layer] = values
        stage_ref[layer] = jnp.where(edge_row, source_ref[layer], weights[layer] * values)

    substitute(couple, inverse_ref, partial_ref, lambda layer: source_ref[layer], emit)
    keep_ref[...] = solved_ref[pl.ds(place, depth)]
    give_ref[...] = solved_ref[pl.ds(depth - place, depth)]
    lower = []
    upper = []
    for part in range(2):
        both = from_modes(stage_ref[part * depth : (part + 1) * depth], edge)
        lower.append(both[:depth])
        upper.append(both[depth:])
    lower = jnp.concatenate(lower, axis=0)
    upper = jnp.concatenate(upper, axis=0)
    lane = lax.broadcasted_iota(jnp.int32, (layers, lanes), 1)
    if 2 * chunk == lanes:
        for tile in range(hor_count // 2):
            here = lower[:, tile * lanes : (tile + 1) * lanes]
            there = turn(upper[:, tile * lanes : (tile + 1) * lanes], chunk)
            packed_ref[2 * tile] = jnp.where(lane < chunk, here, there)
            packed_ref[2 * tile + 1] = jnp.where(lane < chunk, there, here)
        return
    for index in range(hor_count):
        tile = index * chunk // lanes * lanes
        offset = index * chunk % lanes
        packed_ref[index] = jnp.where(
            lane < chunk,
            turn(lower[:, tile : tile + lanes], -offset),
            turn(upper[:, tile : tile + lanes], chunk - offset),
        )


def hartley_8(read, write):
    parts = [read(index) for index in range(8)]
    plus = [parts[index] + parts[index + 4] for index in range(4)]
    minus = [parts[index] - parts[index + 4] for index in range(4)]
    root = math.sqrt(2.0)
    one, three = minus[1] * root, minus[3] * root
    same, cross = plus[0] + plus[2], plus[1] + plus[3]
    write(0, same + cross)
    write(4, same - cross)
    same, cross = plus[0] - plus[2], plus[1] - plus[3]
    write(2, same + cross)
    write(6, same - cross)
    same, cross = minus[0] + minus[2], minus[0] - minus[2]
    write(1, same + one)
    write(5, same - one)
    write(3, cross + three)
    write(7, cross - three)


def small_hartley(count, read, write, shape):
    if count == 8:
        hartley_8(read, write)
        return
    if count <= 8:
        table = cas(2.0 * np.pi * (np.outer(np.arange(count), np.arange(count)) % count) / count)
        parts = [read(index) for index in range(count)]
        for wave in range(count):
            total = None
            for index in range(count):
                value = float(table[wave, index])
                if abs(value) < 1e-12:
                    continue
                if abs(value - 1.0) < 1e-12:
                    term = parts[index]
                elif abs(value + 1.0) < 1e-12:
                    term = -parts[index]
                else:
                    term = parts[index] * value
                total = term if total is None else total + term
            write(wave, total)
        return

    def outer(wave, carry):
        def inner(index, total):
            angle = jnp.full(shape, wave * index % count, jnp.int32).astype(f32)
            angle = angle * (2.0 * math.pi / count)
            return total + read(index) * (jnp.cos(angle) + jnp.sin(angle))

        write(wave, lax.fori_loop(0, count, inner, jnp.zeros(shape, f32)))
        return carry

    lax.fori_loop(0, count, outer, 0)


def interface_kernel(
    spot_ref,
    packed_ref,
    weight_ref,
    inverse_ref,
    back_ref,
    sum_ref,
    wave_ref,
    answer_ref,
    partial_ref,
    *,
    chunk,
):
    hor_count, layers, _ = packed_ref.shape
    rows = inverse_ref.shape[1]
    subsets = lanes // chunk
    classes = max(1, hor_count // rows)
    repeats = max(1, rows // hor_count)
    lane = lax.broadcasted_iota(jnp.int32, (layers, lanes), 1)
    swapped = spot_ref[0] // 2 % 2 if 2 * chunk == lanes else 0
    first = lane // chunk % 2 == swapped

    def halves(index):
        values = packed_ref[index]
        width = 2 * chunk
        while width < lanes:
            values = jnp.where(lane < width, values, turn(values, width))
            width = width * 2
        return values

    def joined(index):
        here = halves(index)
        before = halves((index + hor_count - 1) % hor_count)
        return jnp.where(first, here, turn(here, chunk)) + jnp.where(
            first, turn(before, -chunk), before
        )

    def put_sum(index, values):
        sum_ref[index] = values

    if hor_count <= 8:
        pairs = []
        for index in range(hor_count):
            here = halves(index)
            there = turn(here, chunk)
            back = there if 2 * chunk == lanes else turn(here, -chunk)
            pairs.append((jnp.where(first, here, there), jnp.where(first, back, here)))
        joint = [pairs[index][0] + pairs[index - 1][1] for index in range(hor_count)]
        small_hartley(hor_count, joint.__getitem__, lambda k, v: wave_ref.__setitem__(k, v), (layers, lanes))
    else:
        lax.fori_loop(0, hor_count, lambda k, c: (put_sum(k, joined(k)), c)[1], 0)
        small_hartley(
            hor_count,
            lambda k: sum_ref[k],
            lambda k, v: wave_ref.__setitem__(k, v),
            (layers, lanes),
        )
    weights, couple = layer_terms(weight_ref, rows // 8, 0)
    turned = jnp.swapaxes(wave_ref[...], 0, 1) if classes == 1 else None
    plane_lane = lax.broadcasted_iota(jnp.int32, (rows, lanes), 1)
    group = plane_lane // chunk % classes

    def source(layer):
        if classes == 1:
            return jnp.concatenate([turned[layer]] * repeats, axis=0)
        total = wave_ref[0:rows, layer, :]
        for part in range(1, classes):
            piece = wave_ref[part * rows : (part + 1) * rows, layer, :]
            total = jnp.where(group == part, piece, total)
        return total

    def emit(layer, values):
        if classes == 1:
            total = values[0:hor_count]
            for part in range(1, repeats):
                total = total + values[part * hor_count : (part + 1) * hor_count]
            gathering[layer] = total
            return
        for part in range(classes):
            answer_ref[part * rows : (part + 1) * rows, layer, :] = jnp.where(
                group == part, values, 0.0
            )

    gathering = [None] * layers
    substitute(couple, inverse_ref, partial_ref, source, emit)
    if classes == 1:
        answer_ref[...] = jnp.swapaxes(jnp.stack(gathering), 0, 1)

    def gathered(index):
        values = answer_ref[index]
        shift = chunk
        while shift < lanes:
            values = values + turn(values, shift)
            shift = shift * 2
        return values

    scale = 1.0 / (rows * subsets)

    def put_scaled(index, values):
        sum_ref[index] = values * scale

    if hor_count <= 8:
        small_hartley(hor_count, gathered, put_scaled, (layers, lanes))
    else:
        lax.fori_loop(
            0, hor_count, lambda k, c: (wave_ref.__setitem__(k, gathered(k)), c)[1], 0
        )
        small_hartley(hor_count, lambda k: wave_ref[k], put_scaled, (layers, lanes))
    for index in range(hor_count):
        back_ref[index] = jnp.where(first, sum_ref[index], sum_ref[(index + 1) % hor_count])


def extend(
    dep_ref,
    back_ref,
    solved_ref,
    table,
    small_ref,
    weight_ref,
    inverse_ref,
    left_ref,
    right_ref,
    stage_ref,
    partial_ref,
    ends,
):
    depth, rows, half = solved_ref.shape
    layers = 2 * depth
    hor_count = back_ref.shape[0]
    chunk = half // hor_count
    lane = lax.broadcasted_iota(jnp.int32, (layers, lanes), 1)
    for tile in range(half // lanes if 2 * chunk == lanes else 0):
        even = back_ref[2 * tile]
        odd = back_ref[2 * tile + 1]
        inside = lane < chunk
        left_ref[:, tile * lanes : (tile + 1) * lanes] = jnp.where(inside, even, odd)
        right = turn(jnp.where(inside, odd, even), chunk)
        right_ref[:, tile * lanes : (tile + 1) * lanes] = right
    for tile in range(0 if 2 * chunk == lanes else half // lanes):
        left = None
        right = None
        for index in range(tile * lanes // chunk, (tile + 1) * lanes // chunk):
            offset = index * chunk % lanes
            values = back_ref[index]
            left_part = turn(values, offset)
            right_part = turn(values, offset - chunk)
            inside = lane >= offset
            left = left_part if left is None else jnp.where(inside, left_part, left)
            right = right_part if right is None else jnp.where(inside, right_part, right)
        left_ref[:, tile * lanes : (tile + 1) * lanes] = left
        right_ref[:, tile * lanes : (tile + 1) * lanes] = right
    weights, couple = layer_terms(weight_ref, half // lanes, 1)
    near = row_values(ends[0], (rows, half))
    far = row_values(ends[1], (rows, half))

    def row_of(ref, layer):
        return jnp.broadcast_to(ref[pl.ds(layer, 1), :], (rows, half))

    def source(layer):
        pull = near * row_of(left_ref, layer) + far * row_of(right_ref, layer)
        return weights[layer] * pull

    def emit(layer, values):
        stage_ref[layer] = values

    substitute(couple, inverse_ref, partial_ref, source, emit)
    place = pl.multiple_of(dep_ref[0] * depth, depth)
    edge_row = lax.broadcasted_iota(jnp.int32, (depth, rows, half), 1) == 0
    edge = left_ref[pl.ds(place, depth), :]
    modes = jnp.where(edge_row, edge[:, None, :], solved_ref[...] + stage_ref[pl.ds(place, depth)])
    sine, _ = parts_of(small_ref, depth * rows, depth)
    waves = from_modes(modes, sine)
    cells = dot3(split(waves), table, (((1,), (1,)), ((), ())))
    return cells.reshape(depth, rows, half)


def restore_kernel(
    dep_ref,
    back_ref,
    solved_ref,
    table_ref,
    small_ref,
    weight_ref,
    inverse_ref,
    bins_ref,
    base_ref,
    gain_ref,
    *scratch,
    ends,
    scale,
):
    half = solved_ref.shape[-1]
    sign = jnp.where(dep_ref[0] == 0, -scale, scale).astype(f32)
    gain_ref[:, :, :half] = focusing(bins_ref[:, :, :half]) * scale
    gain_ref[:, :, half:] = focusing(bins_ref[:, :, half:]) * sign
    cells = extend(
        dep_ref,
        back_ref,
        solved_ref,
        (table_ref[0], table_ref[1]),
        small_ref,
        weight_ref,
        inverse_ref,
        *scratch,
        ends,
    )
    base_ref[:, :, :half] = gain_ref[:, :, :half] * cells
    base_ref[:, :, half:] = -(gain_ref[:, :, half:] * cells)


def unfold_kernel(
    dep_ref,
    back_ref,
    solved_ref,
    table_ref,
    small_ref,
    weight_ref,
    inverse_ref,
    base_ref,
    gain_ref,
    out_hbm,
    out_ref,
    sems,
    *scratch,
    ends,
    cuts,
):
    depth, _, half = solved_ref.shape
    size = depth // cuts
    other = 1 - dep_ref[0]
    cells = extend(
        dep_ref,
        back_ref,
        solved_ref,
        (table_ref[other, 0], table_ref[other, 1]),
        small_ref,
        weight_ref,
        inverse_ref,
        *scratch,
        ends,
    )
    copies = []
    for cut in range(cuts):
        part = slice(cut * size, (cut + 1) * size)
        out_ref[part, :, :half] = base_ref[part, :, :half] + gain_ref[part, :, :half] * cells[part]
        out_ref[part, :, half:] = base_ref[part, :, half:] + gain_ref[part, :, half:] * cells[part]
        copy = pltpu.make_async_copy(out_ref.at[part], out_hbm.at[part], sems.at[cut])
        copy.start()
        copies.append(copy)
    for copy in copies:
        copy.wait()


def call(kernel, operands, out_shape, scratch=(), outside=False):
    specs = []
    values = []
    for space, value in operands:
        specs.append(pl.BlockSpec(memory_space=space))
        if space is pltpu.HBM:
            value = pltpu.with_memory_space_constraint(value, pltpu.HBM)
        values.append(value)
    out_space = pltpu.HBM if outside else pltpu.VMEM
    single = not isinstance(out_shape, list)
    out_specs = pl.BlockSpec(memory_space=out_space)
    return pl.pallas_call(
        kernel,
        in_specs=specs,
        out_specs=out_specs if single else [out_specs] * len(out_shape),
        out_shape=out_shape,
        scratch_shapes=list(scratch),
        compiler_params=pltpu.CompilerParams(vmem_limit_bytes=16 * 1024 * 1024),
    )(*values)


def body(residual, focus_bins, layer_class):
    depth, rows, x_cells = residual.shape
    half = x_cells // 2
    layers = layer_class.shape[0]
    hor_count = lax.axis_size("hor")
    y_cells = rows * hor_count
    chunk = half // hor_count
    plane_rows = rows * half // lanes
    dep = lax.axis_index("dep").astype(jnp.int32)
    hor = lax.axis_index("hor").astype(jnp.int32)
    dep_index = dep.reshape(1)
    spot = (hor * 2 + dep).reshape(1)

    table = np.stack(fold_tables(x_cells), axis=1)
    sine = sine_matrix(rows)
    near = np.concatenate([[0.0], sine[1, 1:]])
    far = np.concatenate([[0.0], sine[rows - 1, 1:]])
    lower_row = np.concatenate([[1.0], sine[1, 1:]])
    edge = np.concatenate([np.kron(np.eye(depth), row[None, :]) for row in (lower_row, far)])
    high, low = split_table(np.concatenate([np.kron(np.eye(depth), sine), edge]))
    small = np.concatenate([high, high, low], axis=1)
    wave_x = np.stack(
        [symbol_of(2.0 * np.pi * (2 * np.arange(half) + parity) / x_cells) for parity in range(2)]
    )
    mode = symbol_of(np.pi * np.arange(rows) / rows)
    inner = damping + smoothing * (mode[None, :, None] + wave_x[:, None, :])
    lane = np.arange(lanes)
    wave_number = (lane // chunk)[None, :] * plane_rows + np.arange(plane_rows)[:, None]
    wave_y = symbol_of(2.0 * np.pi * wave_number / y_cells)
    spots = np.arange(hor_count)[:, None, None] * chunk + (lane % chunk)[None, None, :]
    spots = 2 * spots + np.arange(2)[None, :, None]
    wave_spots = symbol_of(2.0 * np.pi * spots / x_cells).reshape(2 * hor_count, lanes)
    outer = np.concatenate([wave_y, wave_spots]).astype(np.float32)

    def shape(*dims):
        return jax.ShapeDtypeStruct(dims, f32)

    def constant(value):
        return (pltpu.HBM, jnp.asarray(value))

    def scalar(value):
        return (pltpu.SMEM, value)

    def near_by(value):
        return (pltpu.VMEM, value)

    slab = (depth, rows, half)
    full = (depth, rows, x_cells)
    field = (layers, rows, half)
    packed = (hor_count, layers, lanes)
    plane = (layers, plane_rows, lanes)
    cuts = 4
    own, send, weight, small_here, inner_here, outer_here = call(
        functools.partial(fold_kernel, cuts=cuts // 2),
        [scalar(dep_index)]
        + [(pltpu.HBM, value) for value in (residual, focus_bins, layer_class)]
        + [constant(value) for value in (small, inner.astype(np.float32), outer)],
        [
            shape(*slab),
            shape(*slab),
            shape(layers, 8, lanes),
            jax.ShapeDtypeStruct(small.shape, bf16),
            shape(2, rows, half),
            shape(*outer.shape),
        ],
        [
            pltpu.VMEM(full, f32),
            pltpu.VMEM(full, jnp.int32),
            pltpu.SMEM((layers,), jnp.int32),
            pltpu.SemaphoreType.DMA((2, cuts // 2)),
            pltpu.SemaphoreType.DMA,
            pltpu.SemaphoreType.DMA((3,)),
        ],
    )
    pairs = [(0, 1), (1, 0)]
    recv = lax.ppermute(send, "dep", pairs)
    modes, table_here, inverse, inverse_other, inverse_outer = call(
        prepare_kernel,
        [scalar(dep_index), scalar(spot), near_by(own), near_by(weight), constant(table)]
        + [near_by(value) for value in (small_here, inner_here, outer_here)],
        [
            shape(*slab),
            jax.ShapeDtypeStruct((2, half, half), bf16),
            shape(*field),
            shape(*field),
            shape(*plane),
        ],
        [pltpu.SemaphoreType.DMA((2,))],
    )
    outgoing, keep, give = call(
        interior_kernel,
        [scalar(dep_index)]
        + [near_by(v) for v in (modes, recv, table_here, small_here, weight, inverse)],
        [shape(*packed), shape(*slab), shape(*slab)],
        [pltpu.VMEM(field, f32)] * 4,
    )
    got = lax.ppermute(give, "dep", pairs)
    incoming = lax.all_to_all(outgoing, "hor", split_axis=0, concat_axis=0, tiled=True)
    incoming, got = lax.optimization_barrier((incoming, got))
    answered = call(
        functools.partial(interface_kernel, chunk=chunk),
        [scalar(spot), near_by(incoming), near_by(weight), near_by(inverse_outer)],
        shape(*packed),
        [pltpu.VMEM(packed, f32)] * 3 + [pltpu.VMEM(plane, f32)],
    )
    edges = lax.all_to_all(answered, "hor", split_axis=0, concat_axis=0, tiled=True)
    other_edges = lax.ppermute(edges, "dep", pairs)
    scratch = [pltpu.VMEM((layers, half), f32)] * 2 + [pltpu.VMEM(field, f32)] * 2
    base, gain = call(
        functools.partial(restore_kernel, ends=(near, far), scale=1.0 / x_cells),
        [scalar(dep_index)]
        + [
            near_by(v)
            for v in (edges, keep, table_here, small_here, weight, inverse, focus_bins)
        ],
        [shape(*full)] * 2,
        scratch,
    )
    return call(
        functools.partial(unfold_kernel, ends=(near, far), cuts=cuts),
        [scalar(dep_index)]
        + [
            near_by(v)
            for v in (
                other_edges,
                got,
                jnp.asarray(table),
                small_here,
                weight,
                inverse_other,
                base,
                gain,
            )
        ],
        shape(*full),
        [pltpu.VMEM(full, f32), pltpu.SemaphoreType.DMA((cuts,))] + scratch,
        outside=True,
    )


def solution(mesh):
    return jax.shard_map(
        body,
        mesh=mesh,
        in_specs=(P(("grp", "dep"), "hor", None), P(("grp", "dep"), "hor", None), P("grp")),
        out_specs=P(("grp", "dep"), "hor", None),
        check_vma=False,
    )
```

```python
import functools
import math

import jax
import jax.numpy as jnp
import ml_dtypes
import numpy as np
from jax import lax
from jax.experimental import pallas as pl
from jax.experimental.pallas import tpu as pltpu
from jax.sharding import PartitionSpec as P

damping = 0.01
smoothing = 1.0
coupling_scale = 1.0
weight_base = 0.5
weight_step = 0.2
focus_base = 0.5
focus_step = 0.09242
lanes = 128
f32 = jnp.float32
bf16 = jnp.bfloat16


def cas(angle):
    return np.cos(angle) + np.sin(angle)


def split_table(table):
    table = table.astype(np.float32)
    high = table.astype(ml_dtypes.bfloat16)
    low = (table - high.astype(np.float32)).astype(ml_dtypes.bfloat16)
    return high, low


def fold_tables(length):
    half = length // 2
    cell = np.arange(half)[:, None]
    tables = []
    for parity in range(2):
        wave = 2 * np.arange(half)[None, :] + parity
        tables.append(cas(2.0 * np.pi * (cell * wave % length) / length))
    return split_table(np.stack(tables))


def sine_matrix(rows):
    index = np.arange(1, rows)
    matrix = np.zeros((rows, rows))
    matrix[0, 0] = 1.0
    matrix[1:, 1:] = np.sqrt(2.0 / rows) * np.sin(np.pi * np.outer(index, index) / rows)
    return matrix


def symbol_of(angle):
    return 2.0 - 2.0 * np.cos(angle)


def split(values):
    high = values.astype(bf16)
    low = (values - high.astype(f32)).astype(bf16)
    return high, low


def dot3(left, right, dims=(((1,), (0,)), ((), ()))):
    dot = functools.partial(lax.dot_general, dimension_numbers=dims, preferred_element_type=f32)
    left_high, left_low = left
    right_high, right_low = right
    rows = left_high.shape[0]
    both = dot(jnp.concatenate([left_high, left_low], axis=0), right_high)
    return both[:rows] + (both[rows:] + dot(left_high, right_low))


def focusing(focus_bins):
    return focus_base * jnp.exp(focus_step * focus_bins.astype(f32))


def layer_weights(class_ref, weight_ref):
    for layer in range(weight_ref.shape[0]):
        level = jnp.full(weight_ref.shape[1:], class_ref[layer], jnp.int32).astype(f32)
        weight_ref[layer] = weight_base * jnp.exp(weight_step * level)


def layer_terms(weight_ref, plane_tiles, axis):
    layers = weight_ref.shape[0]
    weights = [weight_ref[layer] for layer in range(layers)]
    couple = [coupling_scale * weights[k] * weights[k + 1] for k in range(layers - 1)]

    def spread(values):
        return [jnp.concatenate([value] * plane_tiles, axis=axis) for value in values]

    return spread(weights), spread(couple)


def row_values(values, shape):
    row = lax.broadcasted_iota(jnp.int32, shape, 0)
    total = jnp.full(shape, float(values[0]), f32)
    for index in range(1, len(values)):
        total = jnp.where(row == index, float(values[index]), total)
    return total


def diagonal(layer, weights, couple, wave):
    total = weights[layer] * wave
    if layer > 0:
        total = total + couple[layer - 1]
    if layer < len(couple):
        total = total + couple[layer]
    return total


def factor(weights, couple, wave, inverse_ref):
    layers = len(weights)
    half = layers // 2
    top = 1.0 / diagonal(0, weights, couple, wave)
    bottom = 1.0 / diagonal(layers - 1, weights, couple, wave)
    inverse_ref[0] = top
    inverse_ref[layers - 1] = bottom
    for step in range(1, half):
        low = step
        link = couple[low - 1]
        top = 1.0 / (diagonal(low, weights, couple, wave) - link * link * top)
        inverse_ref[low] = top
        high = layers - 1 - step
        link = couple[high]
        pivot = diagonal(high, weights, couple, wave) - link * link * bottom
        if step == half - 1:
            link = couple[half - 1]
            pivot = pivot - link * link * top
        bottom = 1.0 / pivot
        inverse_ref[high] = bottom


def substitute(couple, inverse_ref, partial_ref, source, emit, side=None):
    layers = len(couple) + 1
    half = layers // 2
    top = source(0)
    bottom = source(layers - 1)
    partial_ref[0] = top
    partial_ref[layers - 1] = bottom
    for step in range(1, half):
        low = step
        top = source(low) + couple[low - 1] * inverse_ref[low - 1] * top
        partial_ref[low] = top
        high = layers - 1 - step
        bottom = source(high) + couple[high] * inverse_ref[high + 1] * bottom
        partial_ref[high] = bottom
    link = couple[half - 1]
    bottom = (bottom + link * inverse_ref[half - 1] * top) * inverse_ref[half]
    top = (top + link * bottom) * inverse_ref[half - 1]
    if side != 0:
        emit(half, bottom)
    if side != 1:
        emit(half - 1, top)
    for step in range(1, half):
        if side != 1:
            low = half - 1 - step
            top = (partial_ref[low] + couple[low] * top) * inverse_ref[low]
            emit(low, top)
        if side != 0:
            high = half + step
            bottom = (partial_ref[high] + couple[high - 1] * bottom) * inverse_ref[high]
            emit(high, bottom)


def turn(values, shift):
    shift = shift % lanes
    return values if shift == 0 else pltpu.roll(values, shift, values.ndim - 1)


def fold_kernel(
    dep_ref,
    residual_hbm,
    bins_hbm,
    class_hbm,
    small_hbm,
    inner_hbm,
    outer_hbm,
    own_ref,
    send_ref,
    weight_ref,
    small_ref,
    inner_ref,
    outer_ref,
    residual_ref,
    bins_ref,
    class_ref,
    sems,
    class_sem,
    table_sems,
    *,
    cuts,
):
    depth, _, half = own_ref.shape
    size = depth // cuts
    class_copy = pltpu.make_async_copy(class_hbm, class_ref, class_sem)
    class_copy.start()
    copies = []
    for cut in range(cuts):
        part = pl.ds(cut * size, size)
        first = pltpu.make_async_copy(bins_hbm.at[part], bins_ref.at[part], sems.at[0, cut])
        second = pltpu.make_async_copy(
            residual_hbm.at[part], residual_ref.at[part], sems.at[1, cut]
        )
        first.start()
        second.start()
        copies.append((first, second))
    tables = [
        pltpu.make_async_copy(inner_hbm, inner_ref, table_sems.at[0]),
        pltpu.make_async_copy(outer_hbm, outer_ref, table_sems.at[1]),
        pltpu.make_async_copy(small_hbm, small_ref, table_sems.at[2]),
    ]
    for copy in tables:
        copy.start()
    sign = jnp.where(dep_ref[0] == 0, 1.0, -1.0).astype(f32)
    class_copy.wait()
    layer_weights(class_ref, weight_ref)
    for cut in range(cuts):
        part = pl.ds(cut * size, size)
        copies[cut][0].wait()
        focus_map = focusing(bins_ref[part])
        copies[cut][1].wait()
        scaled = focus_map * residual_ref[part]
        left = scaled[..., :half]
        right = sign * scaled[..., half:]
        own_ref[part] = left + right
        send_ref[part] = left - right
    for copy in tables:
        copy.wait()


def dot2(left, right):
    return jnp.dot(left, right, preferred_element_type=f32)


def to_modes(cells, table, sine):
    return dot3(split(from_modes(cells, sine)), table).reshape(cells.shape)


def from_modes(modes, sine):
    depth, rows, half = modes.shape
    high, low = split(modes.reshape(depth * rows, half))
    return dot2(sine, jnp.concatenate([high, low, high], axis=0))


def parts_of(small_ref, block, depth):
    return small_ref[:block], small_ref[block : block + 2 * depth]


def prepare_kernel(
    dep_ref,
    spot_ref,
    own_ref,
    weight_ref,
    table_hbm,
    small_ref,
    inner_ref,
    outer_ref,
    modes_ref,
    table_ref,
    inverse_ref,
    inverse_other_ref,
    inverse_outer_ref,
    sems,
):
    copies = [
        pltpu.make_async_copy(table_hbm.at[dep_ref[0], part], table_ref.at[part], sems.at[part])
        for part in range(2)
    ]
    for copy in copies:
        copy.start()
    depth, rows, half = own_ref.shape
    plane_rows = inverse_outer_ref.shape[1]
    weights, couple = layer_terms(weight_ref, half // lanes, 1)
    factor(weights, couple, inner_ref[dep_ref[0]], inverse_ref)
    factor(weights, couple, inner_ref[1 - dep_ref[0]], inverse_other_ref)
    weights, couple = layer_terms(weight_ref, plane_rows // 8, 0)
    wave = outer_ref[:plane_rows] + outer_ref[pl.ds(plane_rows + spot_ref[0], 1), :]
    factor(weights, couple, damping + smoothing * wave, inverse_outer_ref)
    sine, _ = parts_of(small_ref, depth * rows, depth)
    high, low = split(from_modes(own_ref[...], sine))
    block = depth * rows
    copies[0].wait()
    both = dot2(jnp.concatenate([high, low], axis=0), table_ref[0])
    copies[1].wait()
    total = both[:block] + (both[block:] + dot2(high, table_ref[1]))
    modes_ref[...] = total.reshape(depth, rows, half)


def interior_kernel(
    dep_ref,
    modes_ref,
    recv_ref,
    table_ref,
    small_ref,
    weight_ref,
    inverse_ref,
    packed_ref,
    keep_ref,
    give_ref,
    source_ref,
    solved_ref,
    stage_ref,
    partial_ref,
):
    depth, rows, half = recv_ref.shape
    layers = 2 * depth
    block = depth * rows
    hor_count = packed_ref.shape[0]
    chunk = half // hor_count
    place = dep_ref[0] * depth
    sine, edge = parts_of(small_ref, block, depth)
    source_ref[pl.ds(place, depth)] = modes_ref[...]
    source_ref[pl.ds(depth - place, depth)] = to_modes(
        recv_ref[...], (table_ref[0], table_ref[1]), sine
    )
    weights, couple = layer_terms(weight_ref, half // lanes, 1)
    edge_row = lax.broadcasted_iota(jnp.int32, (rows, half), 0) == 0

    def emit(layer, values):
        solved_ref[layer] = values
        stage_ref[layer] = jnp.where(edge_row, source_ref[layer], weights[layer] * values)

    substitute(couple, inverse_ref, partial_ref, lambda layer: source_ref[layer], emit)
    keep_ref[...] = solved_ref[pl.ds(place, depth)]
    give_ref[...] = solved_ref[pl.ds(depth - place, depth)]
    lower = []
    upper = []
    for part in range(2):
        both = from_modes(stage_ref[part * depth : (part + 1) * depth], edge)
        lower.append(both[:depth])
        upper.append(both[depth:])
    lower = jnp.concatenate(lower, axis=0)
    upper = jnp.concatenate(upper, axis=0)
    lane = lax.broadcasted_iota(jnp.int32, (layers, lanes), 1)
    if 2 * chunk == lanes:
        for tile in range(hor_count // 2):
            here = lower[:, tile * lanes : (tile + 1) * lanes]
            there = turn(upper[:, tile * lanes : (tile + 1) * lanes], chunk)
            packed_ref[2 * tile] = jnp.where(lane < chunk, here, there)
            packed_ref[2 * tile + 1] = jnp.where(lane < chunk, there, here)
        return
    for index in range(hor_count):
        tile = index * chunk // lanes * lanes
        offset = index * chunk % lanes
        packed_ref[index] = jnp.where(
            lane < chunk,
            turn(lower[:, tile : tile + lanes], -offset),
            turn(upper[:, tile : tile + lanes], chunk - offset),
        )


def hartley_8(read, write):
    parts = [read(index) for index in range(8)]
    plus = [parts[index] + parts[index + 4] for index in range(4)]
    minus = [parts[index] - parts[index + 4] for index in range(4)]
    root = math.sqrt(2.0)
    one, three = minus[1] * root, minus[3] * root
    same, cross = plus[0] + plus[2], plus[1] + plus[3]
    write(0, same + cross)
    write(4, same - cross)
    same, cross = plus[0] - plus[2], plus[1] - plus[3]
    write(2, same + cross)
    write(6, same - cross)
    same, cross = minus[0] + minus[2], minus[0] - minus[2]
    write(1, same + one)
    write(5, same - one)
    write(3, cross + three)
    write(7, cross - three)


def small_hartley(count, read, write, shape):
    if count == 8:
        hartley_8(read, write)
        return
    if count <= 8:
        table = cas(2.0 * np.pi * (np.outer(np.arange(count), np.arange(count)) % count) / count)
        parts = [read(index) for index in range(count)]
        for wave in range(count):
            total = None
            for index in range(count):
                value = float(table[wave, index])
                if abs(value) < 1e-12:
                    continue
                if abs(value - 1.0) < 1e-12:
                    term = parts[index]
                elif abs(value + 1.0) < 1e-12:
                    term = -parts[index]
                else:
                    term = parts[index] * value
                total = term if total is None else total + term
            write(wave, total)
        return

    def outer(wave, carry):
        def inner(index, total):
            angle = jnp.full(shape, wave * index % count, jnp.int32).astype(f32)
            angle = angle * (2.0 * math.pi / count)
            return total + read(index) * (jnp.cos(angle) + jnp.sin(angle))

        write(wave, lax.fori_loop(0, count, inner, jnp.zeros(shape, f32)))
        return carry

    lax.fori_loop(0, count, outer, 0)


def interface_kernel(
    spot_ref,
    packed_ref,
    weight_ref,
    inverse_ref,
    back_ref,
    sum_ref,
    wave_ref,
    answer_ref,
    partial_ref,
    *,
    chunk,
):
    hor_count, layers, _ = packed_ref.shape
    rows = inverse_ref.shape[1]
    subsets = lanes // chunk
    classes = max(1, hor_count // rows)
    repeats = max(1, rows // hor_count)
    lane = lax.broadcasted_iota(jnp.int32, (layers, lanes), 1)
    swapped = spot_ref[0] // 2 % 2 if 2 * chunk == lanes else 0
    first = lane // chunk % 2 == swapped

    def halves(index):
        values = packed_ref[index]
        width = 2 * chunk
        while width < lanes:
            values = jnp.where(lane < width, values, turn(values, width))
            width = width * 2
        return values

    def joined(index):
        here = halves(index)
        before = halves((index + hor_count - 1) % hor_count)
        return jnp.where(first, here, turn(here, chunk)) + jnp.where(
            first, turn(before, -chunk), before
        )

    def put_sum(index, values):
        sum_ref[index] = values

    if hor_count <= 8:
        pairs = []
        for index in range(hor_count):
            here = halves(index)
            there = turn(here, chunk)
            back = there if 2 * chunk == lanes else turn(here, -chunk)
            pairs.append((jnp.where(first, here, there), jnp.where(first, back, here)))
        joint = [pairs[index][0] + pairs[index - 1][1] for index in range(hor_count)]
        small_hartley(hor_count, joint.__getitem__, lambda k, v: wave_ref.__setitem__(k, v), (layers, lanes))
    else:
        lax.fori_loop(0, hor_count, lambda k, c: (put_sum(k, joined(k)), c)[1], 0)
        small_hartley(
            hor_count,
            lambda k: sum_ref[k],
            lambda k, v: wave_ref.__setitem__(k, v),
            (layers, lanes),
        )
    weights, couple = layer_terms(weight_ref, rows // 8, 0)
    turned = jnp.swapaxes(wave_ref[...], 0, 1) if classes == 1 else None
    plane_lane = lax.broadcasted_iota(jnp.int32, (rows, lanes), 1)
    group = plane_lane // chunk % classes

    def source(layer):
        if classes == 1:
            return jnp.concatenate([turned[layer]] * repeats, axis=0)
        total = wave_ref[0:rows, layer, :]
        for part in range(1, classes):
            piece = wave_ref[part * rows : (part + 1) * rows, layer, :]
            total = jnp.where(group == part, piece, total)
        return total

    def emit(layer, values):
        if classes == 1:
            total = values[0:hor_count]
            for part in range(1, repeats):
                total = total + values[part * hor_count : (part + 1) * hor_count]
            gathering[layer] = total
            return
        for part in range(classes):
            answer_ref[part * rows : (part + 1) * rows, layer, :] = jnp.where(
                group == part, values, 0.0
            )

    gathering = [None] * layers
    substitute(couple, inverse_ref, partial_ref, source, emit)
    if classes == 1:
        answer_ref[...] = jnp.swapaxes(jnp.stack(gathering), 0, 1)

    def gathered(index):
        values = answer_ref[index]
        shift = chunk
        while shift < lanes:
            values = values + turn(values, shift)
            shift = shift * 2
        return values

    scale = 1.0 / (rows * subsets)

    def put_scaled(index, values):
        sum_ref[index] = values * scale

    if hor_count <= 8:
        small_hartley(hor_count, gathered, put_scaled, (layers, lanes))
    else:
        lax.fori_loop(
            0, hor_count, lambda k, c: (wave_ref.__setitem__(k, gathered(k)), c)[1], 0
        )
        small_hartley(hor_count, lambda k: wave_ref[k], put_scaled, (layers, lanes))
    for index in range(hor_count):
        back_ref[index] = jnp.where(first, sum_ref[index], sum_ref[(index + 1) % hor_count])


def extend(
    side,
    back_ref,
    solved_ref,
    table,
    small_ref,
    weight_ref,
    inverse_ref,
    left_ref,
    right_ref,
    partial_ref,
    ends,
):
    depth, rows, half = solved_ref.shape
    layers = 2 * depth
    hor_count = back_ref.shape[0]
    chunk = half // hor_count
    lane = lax.broadcasted_iota(jnp.int32, (layers, lanes), 1)
    for tile in range(half // lanes if 2 * chunk == lanes else 0):
        even = back_ref[2 * tile]
        odd = back_ref[2 * tile + 1]
        inside = lane < chunk
        left_ref[:, tile * lanes : (tile + 1) * lanes] = jnp.where(inside, even, odd)
        right = turn(jnp.where(inside, odd, even), chunk)
        right_ref[:, tile * lanes : (tile + 1) * lanes] = right
    for tile in range(0 if 2 * chunk == lanes else half // lanes):
        left = None
        right = None
        for index in range(tile * lanes // chunk, (tile + 1) * lanes // chunk):
            offset = index * chunk % lanes
            values = back_ref[index]
            left_part = turn(values, offset)
            right_part = turn(values, offset - chunk)
            inside = lane >= offset
            left = left_part if left is None else jnp.where(inside, left_part, left)
            right = right_part if right is None else jnp.where(inside, right_part, right)
        left_ref[:, tile * lanes : (tile + 1) * lanes] = left
        right_ref[:, tile * lanes : (tile + 1) * lanes] = right
    weights, couple = layer_terms(weight_ref, half // lanes, 1)
    near = row_values(ends[0], (rows, half))
    far = row_values(ends[1], (rows, half))

    def row_of(ref, layer):
        return jnp.broadcast_to(ref[pl.ds(layer, 1), :], (rows, half))

    def source(layer):
        pull = near * row_of(left_ref, layer) + far * row_of(right_ref, layer)
        return weights[layer] * pull

    edge_row = lax.broadcasted_iota(jnp.int32, (rows, half), 0) == 0
    place = side * depth
    found = [None] * depth

    def emit(layer, values):
        layer_here = layer - place
        total = solved_ref[layer_here] + values
        found[layer_here] = jnp.where(edge_row, row_of(left_ref, layer), total)

    substitute(couple, inverse_ref, partial_ref, source, emit, side)
    modes = jnp.stack(found)
    sine, _ = parts_of(small_ref, depth * rows, depth)
    waves = from_modes(modes, sine)
    cells = dot3(split(waves), table, (((1,), (1,)), ((), ())))
    return cells.reshape(depth, rows, half)


def restore_kernel(
    dep_ref,
    back_ref,
    solved_ref,
    table_ref,
    small_ref,
    weight_ref,
    inverse_ref,
    bins_ref,
    base_ref,
    gain_ref,
    *scratch,
    ends,
    scale,
):
    half = solved_ref.shape[-1]

    def work(side):
        sign = scale if side else -scale
        left = focusing(bins_ref[:, :, :half]) * scale
        right = focusing(bins_ref[:, :, half:]) * sign
        gain_ref[:, :, :half] = left
        gain_ref[:, :, half:] = right
        table = (table_ref[0], table_ref[1])
        cells = extend(
            side, back_ref, solved_ref, table, small_ref, weight_ref, inverse_ref, *scratch, ends
        )
        base_ref[:, :, :half] = gain_ref[:, :, :half] * cells
        base_ref[:, :, half:] = -(gain_ref[:, :, half:] * cells)

    pl.when(dep_ref[0] == 0)(lambda: work(0))
    pl.when(dep_ref[0] == 1)(lambda: work(1))


def unfold_kernel(
    dep_ref,
    back_ref,
    solved_ref,
    table_ref,
    small_ref,
    weight_ref,
    inverse_ref,
    base_ref,
    gain_ref,
    out_hbm,
    out_ref,
    sems,
    *scratch,
    ends,
    cuts,
):
    depth, _, half = solved_ref.shape
    size = depth // cuts

    def work(side):
        table = (table_ref[1 - side, 0], table_ref[1 - side, 1])
        cells = extend(
            side, back_ref, solved_ref, table, small_ref, weight_ref, inverse_ref, *scratch, ends
        )
        copies = []
        for cut in range(cuts):
            part = slice(cut * size, (cut + 1) * size)
            for ends_here in (slice(0, half), slice(half, 2 * half)):
                out_ref[part, :, ends_here] = (
                    base_ref[part, :, ends_here] + gain_ref[part, :, ends_here] * cells[part]
                )
            copy = pltpu.make_async_copy(out_ref.at[part], out_hbm.at[part], sems.at[cut])
            copy.start()
            copies.append(copy)
        for copy in copies:
            copy.wait()

    pl.when(dep_ref[0] == 0)(lambda: work(0))
    pl.when(dep_ref[0] == 1)(lambda: work(1))


def call(kernel, operands, out_shape, scratch=(), outside=False):
    specs = []
    values = []
    for space, value in operands:
        specs.append(pl.BlockSpec(memory_space=space))
        if space is pltpu.HBM:
            value = pltpu.with_memory_space_constraint(value, pltpu.HBM)
        values.append(value)
    out_space = pltpu.HBM if outside else pltpu.VMEM
    single = not isinstance(out_shape, list)
    out_specs = pl.BlockSpec(memory_space=out_space)
    return pl.pallas_call(
        kernel,
        in_specs=specs,
        out_specs=out_specs if single else [out_specs] * len(out_shape),
        out_shape=out_shape,
        scratch_shapes=list(scratch),
        compiler_params=pltpu.CompilerParams(vmem_limit_bytes=16 * 1024 * 1024),
    )(*values)


def body(residual, focus_bins, layer_class):
    depth, rows, x_cells = residual.shape
    half = x_cells // 2
    layers = layer_class.shape[0]
    hor_count = lax.axis_size("hor")
    y_cells = rows * hor_count
    chunk = half // hor_count
    plane_rows = rows * half // lanes
    dep = lax.axis_index("dep").astype(jnp.int32)
    hor = lax.axis_index("hor").astype(jnp.int32)
    dep_index = dep.reshape(1)
    spot = (hor * 2 + dep).reshape(1)

    table = np.stack(fold_tables(x_cells), axis=1)
    sine = sine_matrix(rows)
    near = np.concatenate([[0.0], sine[1, 1:]])
    far = np.concatenate([[0.0], sine[rows - 1, 1:]])
    lower_row = np.concatenate([[1.0], sine[1, 1:]])
    edge = np.concatenate([np.kron(np.eye(depth), row[None, :]) for row in (lower_row, far)])
    high, low = split_table(np.concatenate([np.kron(np.eye(depth), sine), edge]))
    small = np.concatenate([high, high, low], axis=1)
    wave_x = np.stack(
        [symbol_of(2.0 * np.pi * (2 * np.arange(half) + parity) / x_cells) for parity in range(2)]
    )
    mode = symbol_of(np.pi * np.arange(rows) / rows)
    inner = damping + smoothing * (mode[None, :, None] + wave_x[:, None, :])
    lane = np.arange(lanes)
    wave_number = (lane // chunk)[None, :] * plane_rows + np.arange(plane_rows)[:, None]
    wave_y = symbol_of(2.0 * np.pi * wave_number / y_cells)
    spots = np.arange(hor_count)[:, None, None] * chunk + (lane % chunk)[None, None, :]
    spots = 2 * spots + np.arange(2)[None, :, None]
    wave_spots = symbol_of(2.0 * np.pi * spots / x_cells).reshape(2 * hor_count, lanes)
    outer = np.concatenate([wave_y, wave_spots]).astype(np.float32)

    def shape(*dims):
        return jax.ShapeDtypeStruct(dims, f32)

    def constant(value):
        return (pltpu.HBM, jnp.asarray(value))

    def scalar(value):
        return (pltpu.SMEM, value)

    def near_by(value):
        return (pltpu.VMEM, value)

    slab = (depth, rows, half)
    full = (depth, rows, x_cells)
    field = (layers, rows, half)
    packed = (hor_count, layers, lanes)
    plane = (layers, plane_rows, lanes)
    cuts = 4
    own, send, weight, small_here, inner_here, outer_here = call(
        functools.partial(fold_kernel, cuts=cuts // 2),
        [scalar(dep_index)]
        + [(pltpu.HBM, value) for value in (residual, focus_bins, layer_class)]
        + [constant(value) for value in (small, inner.astype(np.float32), outer)],
        [
            shape(*slab),
            shape(*slab),
            shape(layers, 8, lanes),
            jax.ShapeDtypeStruct(small.shape, bf16),
            shape(2, rows, half),
            shape(*outer.shape),
        ],
        [
            pltpu.VMEM(full, f32),
            pltpu.VMEM(full, jnp.int32),
            pltpu.SMEM((layers,), jnp.int32),
            pltpu.SemaphoreType.DMA((2, cuts // 2)),
            pltpu.SemaphoreType.DMA,
            pltpu.SemaphoreType.DMA((3,)),
        ],
    )
    pairs = [(0, 1), (1, 0)]
    recv = lax.ppermute(send, "dep", pairs)
    modes, table_here, inverse, inverse_other, inverse_outer = call(
        prepare_kernel,
        [scalar(dep_index), scalar(spot), near_by(own), near_by(weight), constant(table)]
        + [near_by(value) for value in (small_here, inner_here, outer_here)],
        [
            shape(*slab),
            jax.ShapeDtypeStruct((2, half, half), bf16),
            shape(*field),
            shape(*field),
            shape(*plane),
        ],
        [pltpu.SemaphoreType.DMA((2,))],
    )
    outgoing, keep, give = call(
        interior_kernel,
        [scalar(dep_index)]
        + [near_by(v) for v in (modes, recv, table_here, small_here, weight, inverse)],
        [shape(*packed), shape(*slab), shape(*slab)],
        [pltpu.VMEM(field, f32)] * 4,
    )
    got = lax.ppermute(give, "dep", pairs)
    incoming = lax.all_to_all(outgoing, "hor", split_axis=0, concat_axis=0, tiled=True)
    incoming, got = lax.optimization_barrier((incoming, got))
    answered = call(
        functools.partial(interface_kernel, chunk=chunk),
        [scalar(spot), near_by(incoming), near_by(weight), near_by(inverse_outer)],
        shape(*packed),
        [pltpu.VMEM(packed, f32)] * 3 + [pltpu.VMEM(plane, f32)],
    )
    edges = lax.all_to_all(answered, "hor", split_axis=0, concat_axis=0, tiled=True)
    other_edges = lax.ppermute(edges, "dep", pairs)
    scratch = [pltpu.VMEM((layers, half), f32)] * 2 + [pltpu.VMEM(field, f32)]
    base, gain = call(
        functools.partial(restore_kernel, ends=(near, far), scale=1.0 / x_cells),
        [scalar(dep_index)]
        + [
            near_by(v)
            for v in (edges, keep, table_here, small_here, weight, inverse, focus_bins)
        ],
        [shape(*full)] * 2,
        scratch,
    )
    return call(
        functools.partial(unfold_kernel, ends=(near, far), cuts=cuts),
        [scalar(dep_index)]
        + [
            near_by(v)
            for v in (
                other_edges,
                got,
                jnp.asarray(table),
                small_here,
                weight,
                inverse_other,
                base,
                gain,
            )
        ],
        shape(*full),
        [pltpu.VMEM(full, f32), pltpu.SemaphoreType.DMA((cuts,))] + scratch,
        outside=True,
    )


def solution(mesh):
    return jax.shard_map(
        body,
        mesh=mesh,
        in_specs=(P(("grp", "dep"), "hor", None), P(("grp", "dep"), "hor", None), P("grp")),
        out_specs=P(("grp", "dep"), "hor", None),
        check_vma=False,
    )
```

```python
import functools
import math

import jax
import jax.numpy as jnp
import ml_dtypes
import numpy as np
from jax import lax
from jax.experimental import pallas as pl
from jax.experimental.pallas import tpu as pltpu
from jax.sharding import PartitionSpec as P

damping = 0.01
smoothing = 1.0
coupling_scale = 1.0
weight_base = 0.5
weight_step = 0.2
focus_base = 0.5
focus_step = 0.09242
lanes = 128
f32 = jnp.float32
bf16 = jnp.bfloat16


def cas(angle):
    return np.cos(angle) + np.sin(angle)


def split_table(table):
    table = table.astype(np.float32)
    high = table.astype(ml_dtypes.bfloat16)
    low = (table - high.astype(np.float32)).astype(ml_dtypes.bfloat16)
    return high, low


def fold_tables(length):
    half = length // 2
    cell = np.arange(half)[:, None]
    tables = []
    for parity in range(2):
        wave = 2 * np.arange(half)[None, :] + parity
        tables.append(cas(2.0 * np.pi * (cell * wave % length) / length))
    return split_table(np.stack(tables))


def sine_matrix(rows):
    index = np.arange(1, rows)
    matrix = np.zeros((rows, rows))
    matrix[0, 0] = 1.0
    matrix[1:, 1:] = np.sqrt(2.0 / rows) * np.sin(np.pi * np.outer(index, index) / rows)
    return matrix


def symbol_of(angle):
    return 2.0 - 2.0 * np.cos(angle)


def split(values):
    high = values.astype(bf16)
    low = (values - high.astype(f32)).astype(bf16)
    return high, low


def dot3(left, right, dims=(((1,), (0,)), ((), ()))):
    dot = functools.partial(lax.dot_general, dimension_numbers=dims, preferred_element_type=f32)
    left_high, left_low = left
    right_high, right_low = right
    rows = left_high.shape[0]
    both = dot(jnp.concatenate([left_high, left_low], axis=0), right_high)
    return both[:rows] + (both[rows:] + dot(left_high, right_low))


def focusing(focus_bins):
    return focus_base * jnp.exp(focus_step * focus_bins.astype(f32))


def layer_weights(class_ref, weight_ref):
    for layer in range(weight_ref.shape[0]):
        level = jnp.full(weight_ref.shape[1:], class_ref[layer], jnp.int32).astype(f32)
        weight_ref[layer] = weight_base * jnp.exp(weight_step * level)


def layer_terms(weight_ref, plane_tiles, axis):
    layers = weight_ref.shape[0]
    weights = [weight_ref[layer] for layer in range(layers)]
    couple = [coupling_scale * weights[k] * weights[k + 1] for k in range(layers - 1)]

    def spread(values):
        return [jnp.concatenate([value] * plane_tiles, axis=axis) for value in values]

    return spread(weights), spread(couple)


def row_values(values, shape):
    row = lax.broadcasted_iota(jnp.int32, shape, 0)
    total = jnp.full(shape, float(values[0]), f32)
    for index in range(1, len(values)):
        total = jnp.where(row == index, float(values[index]), total)
    return total


def diagonal(layer, weights, couple, wave):
    total = weights[layer] * wave
    if layer > 0:
        total = total + couple[layer - 1]
    if layer < len(couple):
        total = total + couple[layer]
    return total


def factor(weights, couple, wave, inverse_ref):
    layers = len(weights)
    half = layers // 2
    top = 1.0 / diagonal(0, weights, couple, wave)
    bottom = 1.0 / diagonal(layers - 1, weights, couple, wave)
    inverse_ref[0] = top
    inverse_ref[layers - 1] = bottom
    for step in range(1, half):
        low = step
        link = couple[low - 1]
        top = 1.0 / (diagonal(low, weights, couple, wave) - link * link * top)
        inverse_ref[low] = top
        high = layers - 1 - step
        link = couple[high]
        pivot = diagonal(high, weights, couple, wave) - link * link * bottom
        if step == half - 1:
            link = couple[half - 1]
            pivot = pivot - link * link * top
        bottom = 1.0 / pivot
        inverse_ref[high] = bottom


def substitute(couple, inverse_ref, partial_ref, source, emit, side=None):
    layers = len(couple) + 1
    half = layers // 2
    top = source(0)
    bottom = source(layers - 1)
    partial_ref[0] = top
    partial_ref[layers - 1] = bottom
    for step in range(1, half):
        low = step
        top = source(low) + couple[low - 1] * inverse_ref[low - 1] * top
        partial_ref[low] = top
        high = layers - 1 - step
        bottom = source(high) + couple[high] * inverse_ref[high + 1] * bottom
        partial_ref[high] = bottom
    link = couple[half - 1]
    bottom = (bottom + link * inverse_ref[half - 1] * top) * inverse_ref[half]
    top = (top + link * bottom) * inverse_ref[half - 1]
    if side != 0:
        emit(half, bottom)
    if side != 1:
        emit(half - 1, top)
    for step in range(1, half):
        if side != 1:
            low = half - 1 - step
            top = (partial_ref[low] + couple[low] * top) * inverse_ref[low]
            emit(low, top)
        if side != 0:
            high = half + step
            bottom = (partial_ref[high] + couple[high - 1] * bottom) * inverse_ref[high]
            emit(high, bottom)


def turn(values, shift):
    shift = shift % lanes
    return values if shift == 0 else pltpu.roll(values, shift, values.ndim - 1)


def fold_kernel(
    dep_ref,
    residual_hbm,
    bins_hbm,
    class_hbm,
    small_hbm,
    inner_hbm,
    outer_hbm,
    own_ref,
    send_ref,
    weight_ref,
    small_ref,
    inner_ref,
    outer_ref,
    residual_ref,
    bins_ref,
    class_ref,
    sems,
    class_sem,
    table_sems,
    *,
    cuts,
):
    depth, _, half = own_ref.shape
    size = depth // cuts
    class_copy = pltpu.make_async_copy(class_hbm, class_ref, class_sem)
    class_copy.start()
    copies = []
    for cut in range(cuts):
        part = pl.ds(cut * size, size)
        first = pltpu.make_async_copy(bins_hbm.at[part], bins_ref.at[part], sems.at[0, cut])
        second = pltpu.make_async_copy(
            residual_hbm.at[part], residual_ref.at[part], sems.at[1, cut]
        )
        first.start()
        second.start()
        copies.append((first, second))
    tables = [
        pltpu.make_async_copy(inner_hbm, inner_ref, table_sems.at[0]),
        pltpu.make_async_copy(outer_hbm, outer_ref, table_sems.at[1]),
        pltpu.make_async_copy(small_hbm, small_ref, table_sems.at[2]),
    ]
    for copy in tables:
        copy.start()
    sign = jnp.where(dep_ref[0] == 0, 1.0, -1.0).astype(f32)
    class_copy.wait()
    layer_weights(class_ref, weight_ref)
    for cut in range(cuts):
        part = pl.ds(cut * size, size)
        copies[cut][0].wait()
        focus_map = focusing(bins_ref[part])
        copies[cut][1].wait()
        scaled = focus_map * residual_ref[part]
        left = scaled[..., :half]
        right = sign * scaled[..., half:]
        own_ref[part] = left + right
        send_ref[part] = left - right
    for copy in tables:
        copy.wait()


def dot2(left, right):
    return jnp.dot(left, right, preferred_element_type=f32)


def to_modes(cells, table, sine):
    return dot3(split(from_modes(cells, sine)), table).reshape(cells.shape)


def from_modes(modes, sine):
    depth, rows, half = modes.shape
    high, low = split(modes.reshape(depth * rows, half))
    return dot2(sine, jnp.concatenate([high, low, high], axis=0))


def parts_of(small_ref, block, depth):
    return small_ref[:block], small_ref[block : block + 2 * depth]


def prepare_kernel(
    dep_ref,
    spot_ref,
    own_ref,
    weight_ref,
    table_hbm,
    small_ref,
    inner_ref,
    outer_ref,
    modes_ref,
    table_ref,
    inverse_ref,
    inverse_other_ref,
    inverse_outer_ref,
    sems,
):
    copies = [
        pltpu.make_async_copy(table_hbm.at[dep_ref[0], part], table_ref.at[part], sems.at[part])
        for part in range(2)
    ]
    for copy in copies:
        copy.start()
    depth, rows, half = own_ref.shape
    plane_rows = inverse_outer_ref.shape[1]
    weights, couple = layer_terms(weight_ref, half // lanes, 1)
    factor(weights, couple, inner_ref[dep_ref[0]], inverse_ref)
    factor(weights, couple, inner_ref[1 - dep_ref[0]], inverse_other_ref)
    weights, couple = layer_terms(weight_ref, plane_rows // 8, 0)
    wave = outer_ref[:plane_rows] + outer_ref[pl.ds(plane_rows + spot_ref[0], 1), :]
    factor(weights, couple, damping + smoothing * wave, inverse_outer_ref)
    sine, _ = parts_of(small_ref, depth * rows, depth)
    high, low = split(from_modes(own_ref[...], sine))
    block = depth * rows
    copies[0].wait()
    both = dot2(jnp.concatenate([high, low], axis=0), table_ref[0])
    copies[1].wait()
    total = both[:block] + (both[block:] + dot2(high, table_ref[1]))
    modes_ref[...] = total.reshape(depth, rows, half)


def interior_kernel(
    dep_ref,
    modes_ref,
    recv_ref,
    table_ref,
    small_ref,
    weight_ref,
    inverse_ref,
    packed_ref,
    keep_ref,
    give_ref,
    source_ref,
    solved_ref,
    stage_ref,
    partial_ref,
):
    depth, rows, half = recv_ref.shape
    layers = 2 * depth
    block = depth * rows
    hor_count = packed_ref.shape[0]
    chunk = half // hor_count
    place = dep_ref[0] * depth
    sine, edge = parts_of(small_ref, block, depth)
    source_ref[pl.ds(place, depth)] = modes_ref[...]
    source_ref[pl.ds(depth - place, depth)] = to_modes(
        recv_ref[...], (table_ref[0], table_ref[1]), sine
    )
    weights, couple = layer_terms(weight_ref, half // lanes, 1)
    edge_row = lax.broadcasted_iota(jnp.int32, (rows, half), 0) == 0

    def emit(layer, values):
        solved_ref[layer] = values
        stage_ref[layer] = jnp.where(edge_row, source_ref[layer], weights[layer] * values)

    substitute(couple, inverse_ref, partial_ref, lambda layer: source_ref[layer], emit)
    keep_ref[...] = solved_ref[pl.ds(place, depth)]
    give_ref[...] = solved_ref[pl.ds(depth - place, depth)]
    lower = []
    upper = []
    for part in range(2):
        both = from_modes(stage_ref[part * depth : (part + 1) * depth], edge)
        lower.append(both[:depth])
        upper.append(both[depth:])
    lower = jnp.concatenate(lower, axis=0)
    upper = jnp.concatenate(upper, axis=0)
    lane = lax.broadcasted_iota(jnp.int32, (layers, lanes), 1)
    if 2 * chunk == lanes:
        for tile in range(hor_count // 2):
            here = lower[:, tile * lanes : (tile + 1) * lanes]
            there = turn(upper[:, tile * lanes : (tile + 1) * lanes], chunk)
            packed_ref[2 * tile] = jnp.where(lane < chunk, here, there)
            packed_ref[2 * tile + 1] = jnp.where(lane < chunk, there, here)
        return
    for index in range(hor_count):
        tile = index * chunk // lanes * lanes
        offset = index * chunk % lanes
        packed_ref[index] = jnp.where(
            lane < chunk,
            turn(lower[:, tile : tile + lanes], -offset),
            turn(upper[:, tile : tile + lanes], chunk - offset),
        )


def hartley_8(read, write):
    parts = [read(index) for index in range(8)]
    plus = [parts[index] + parts[index + 4] for index in range(4)]
    minus = [parts[index] - parts[index + 4] for index in range(4)]
    root = math.sqrt(2.0)
    one, three = minus[1] * root, minus[3] * root
    same, cross = plus[0] + plus[2], plus[1] + plus[3]
    write(0, same + cross)
    write(4, same - cross)
    same, cross = plus[0] - plus[2], plus[1] - plus[3]
    write(2, same + cross)
    write(6, same - cross)
    same, cross = minus[0] + minus[2], minus[0] - minus[2]
    write(1, same + one)
    write(5, same - one)
    write(3, cross + three)
    write(7, cross - three)


def small_hartley(count, read, write, shape):
    if count == 8:
        hartley_8(read, write)
        return
    if count <= 8:
        table = cas(2.0 * np.pi * (np.outer(np.arange(count), np.arange(count)) % count) / count)
        parts = [read(index) for index in range(count)]
        for wave in range(count):
            total = None
            for index in range(count):
                value = float(table[wave, index])
                if abs(value) < 1e-12:
                    continue
                if abs(value - 1.0) < 1e-12:
                    term = parts[index]
                elif abs(value + 1.0) < 1e-12:
                    term = -parts[index]
                else:
                    term = parts[index] * value
                total = term if total is None else total + term
            write(wave, total)
        return

    def outer(wave, carry):
        def inner(index, total):
            angle = jnp.full(shape, wave * index % count, jnp.int32).astype(f32)
            angle = angle * (2.0 * math.pi / count)
            return total + read(index) * (jnp.cos(angle) + jnp.sin(angle))

        write(wave, lax.fori_loop(0, count, inner, jnp.zeros(shape, f32)))
        return carry

    lax.fori_loop(0, count, outer, 0)


def interface_kernel(
    spot_ref,
    packed_ref,
    weight_ref,
    inverse_ref,
    back_ref,
    sum_ref,
    wave_ref,
    answer_ref,
    partial_ref,
    *,
    chunk,
):
    hor_count, layers, _ = packed_ref.shape
    rows = inverse_ref.shape[1]
    subsets = lanes // chunk
    classes = max(1, hor_count // rows)
    repeats = max(1, rows // hor_count)
    lane = lax.broadcasted_iota(jnp.int32, (layers, lanes), 1)
    swapped = spot_ref[0] // 2 % 2 if 2 * chunk == lanes else 0
    first = lane // chunk % 2 == swapped

    def halves(index):
        values = packed_ref[index]
        width = 2 * chunk
        while width < lanes:
            values = jnp.where(lane < width, values, turn(values, width))
            width = width * 2
        return values

    def joined(index):
        here = halves(index)
        before = halves((index + hor_count - 1) % hor_count)
        return jnp.where(first, here, turn(here, chunk)) + jnp.where(
            first, turn(before, -chunk), before
        )

    def put_sum(index, values):
        sum_ref[index] = values

    if hor_count <= 8:
        pairs = []
        for index in range(hor_count):
            here = halves(index)
            there = turn(here, chunk)
            back = there if 2 * chunk == lanes else turn(here, -chunk)
            pairs.append((jnp.where(first, here, there), jnp.where(first, back, here)))
        joint = [pairs[index][0] + pairs[index - 1][1] for index in range(hor_count)]
        small_hartley(hor_count, joint.__getitem__, lambda k, v: wave_ref.__setitem__(k, v), (layers, lanes))
    else:
        lax.fori_loop(0, hor_count, lambda k, c: (put_sum(k, joined(k)), c)[1], 0)
        small_hartley(
            hor_count,
            lambda k: sum_ref[k],
            lambda k, v: wave_ref.__setitem__(k, v),
            (layers, lanes),
        )
    weights, couple = layer_terms(weight_ref, rows // 8, 0)
    turned = jnp.swapaxes(wave_ref[...], 0, 1) if classes == 1 else None
    plane_lane = lax.broadcasted_iota(jnp.int32, (rows, lanes), 1)
    group = plane_lane // chunk % classes

    def source(layer):
        if classes == 1:
            return jnp.concatenate([turned[layer]] * repeats, axis=0)
        total = wave_ref[0:rows, layer, :]
        for part in range(1, classes):
            piece = wave_ref[part * rows : (part + 1) * rows, layer, :]
            total = jnp.where(group == part, piece, total)
        return total

    def emit(layer, values):
        if classes == 1:
            total = values[0:hor_count]
            for part in range(1, repeats):
                total = total + values[part * hor_count : (part + 1) * hor_count]
            gathering[layer] = total
            return
        for part in range(classes):
            answer_ref[part * rows : (part + 1) * rows, layer, :] = jnp.where(
                group == part, values, 0.0
            )

    gathering = [None] * layers
    substitute(couple, inverse_ref, partial_ref, source, emit)
    if classes == 1:
        answer_ref[...] = jnp.swapaxes(jnp.stack(gathering), 0, 1)

    def gathered(index):
        values = answer_ref[index]
        shift = chunk
        while shift < lanes:
            values = values + turn(values, shift)
            shift = shift * 2
        return values

    scale = 1.0 / (rows * subsets)

    def put_scaled(index, values):
        sum_ref[index] = values * scale

    if hor_count <= 8:
        small_hartley(hor_count, gathered, put_scaled, (layers, lanes))
    else:
        lax.fori_loop(
            0, hor_count, lambda k, c: (wave_ref.__setitem__(k, gathered(k)), c)[1], 0
        )
        small_hartley(hor_count, lambda k: wave_ref[k], put_scaled, (layers, lanes))
    for index in range(hor_count):
        back_ref[index] = jnp.where(first, sum_ref[index], sum_ref[(index + 1) % hor_count])


def extend(
    side,
    back_ref,
    solved_ref,
    table,
    small_ref,
    weight_ref,
    inverse_ref,
    left_ref,
    right_ref,
    sum_ref,
    partial_ref,
    ends,
):
    depth, rows, half = solved_ref.shape
    layers = 2 * depth
    hor_count = back_ref.shape[0]
    chunk = half // hor_count
    lane = lax.broadcasted_iota(jnp.int32, (layers, lanes), 1)
    for tile in range(half // lanes if 2 * chunk == lanes else 0):
        even = back_ref[2 * tile]
        odd = back_ref[2 * tile + 1]
        inside = lane < chunk
        left_ref[:, tile * lanes : (tile + 1) * lanes] = jnp.where(inside, even, odd)
        right = turn(jnp.where(inside, odd, even), chunk)
        right_ref[:, tile * lanes : (tile + 1) * lanes] = right
    for tile in range(0 if 2 * chunk == lanes else half // lanes):
        left = None
        right = None
        for index in range(tile * lanes // chunk, (tile + 1) * lanes // chunk):
            offset = index * chunk % lanes
            values = back_ref[index]
            left_part = turn(values, offset)
            right_part = turn(values, offset - chunk)
            inside = lane >= offset
            left = left_part if left is None else jnp.where(inside, left_part, left)
            right = right_part if right is None else jnp.where(inside, right_part, right)
        left_ref[:, tile * lanes : (tile + 1) * lanes] = left
        right_ref[:, tile * lanes : (tile + 1) * lanes] = right
    weights, couple = layer_terms(weight_ref, half // lanes, 1)
    near = row_values(ends[0], (rows, lanes))
    odd = lax.broadcasted_iota(jnp.int32, (rows, half), 0) % 2 == 1
    sum_ref[...] = left_ref[...] + right_ref[...]
    right_ref[...] = left_ref[...] - right_ref[...]

    def row_of(ref, layer):
        return jnp.broadcast_to(ref[pl.ds(layer, 1), :], (rows, half))

    def source(layer):
        factors = jnp.concatenate([weight_ref[layer] * near] * (half // lanes), axis=1)
        return factors * jnp.where(odd, row_of(sum_ref, layer), row_of(right_ref, layer))

    edge_row = lax.broadcasted_iota(jnp.int32, (rows, half), 0) == 0
    place = side * depth
    found = [None] * depth

    def emit(layer, values):
        layer_here = layer - place
        total = solved_ref[layer_here] + values
        found[layer_here] = jnp.where(edge_row, row_of(left_ref, layer), total)

    substitute(couple, inverse_ref, partial_ref, source, emit, side)
    modes = jnp.stack(found)
    sine, _ = parts_of(small_ref, depth * rows, depth)
    waves = from_modes(modes, sine)
    cells = dot3(split(waves), table, (((1,), (1,)), ((), ())))
    return cells.reshape(depth, rows, half)


def restore_kernel(
    dep_ref,
    back_ref,
    solved_ref,
    table_ref,
    small_ref,
    weight_ref,
    inverse_ref,
    bins_ref,
    base_ref,
    gain_ref,
    *scratch,
    ends,
    scale,
):
    half = solved_ref.shape[-1]

    def work(side):
        sign = scale if side else -scale
        left = focusing(bins_ref[:, :, :half]) * scale
        right = focusing(bins_ref[:, :, half:]) * sign
        gain_ref[:, :, :half] = left
        gain_ref[:, :, half:] = right
        table = (table_ref[0], table_ref[1])
        cells = extend(
            side, back_ref, solved_ref, table, small_ref, weight_ref, inverse_ref, *scratch, ends
        )
        base_ref[:, :, :half] = gain_ref[:, :, :half] * cells
        base_ref[:, :, half:] = -(gain_ref[:, :, half:] * cells)

    pl.when(dep_ref[0] == 0)(lambda: work(0))
    pl.when(dep_ref[0] == 1)(lambda: work(1))


def unfold_kernel(
    dep_ref,
    back_ref,
    solved_ref,
    table_ref,
    small_ref,
    weight_ref,
    inverse_ref,
    base_ref,
    gain_ref,
    out_hbm,
    out_ref,
    sems,
    *scratch,
    ends,
    cuts,
):
    depth, _, half = solved_ref.shape
    size = depth // cuts

    def work(side):
        table = (table_ref[1 - side, 0], table_ref[1 - side, 1])
        cells = extend(
            side, back_ref, solved_ref, table, small_ref, weight_ref, inverse_ref, *scratch, ends
        )
        copies = []
        for cut in range(cuts):
            part = slice(cut * size, (cut + 1) * size)
            for ends_here in (slice(0, half), slice(half, 2 * half)):
                out_ref[part, :, ends_here] = (
                    base_ref[part, :, ends_here] + gain_ref[part, :, ends_here] * cells[part]
                )
            copy = pltpu.make_async_copy(out_ref.at[part], out_hbm.at[part], sems.at[cut])
            copy.start()
            copies.append(copy)
        for copy in copies:
            copy.wait()

    pl.when(dep_ref[0] == 0)(lambda: work(0))
    pl.when(dep_ref[0] == 1)(lambda: work(1))


def call(kernel, operands, out_shape, scratch=(), outside=False):
    specs = []
    values = []
    for space, value in operands:
        specs.append(pl.BlockSpec(memory_space=space))
        if space is pltpu.HBM:
            value = pltpu.with_memory_space_constraint(value, pltpu.HBM)
        values.append(value)
    out_space = pltpu.HBM if outside else pltpu.VMEM
    single = not isinstance(out_shape, list)
    out_specs = pl.BlockSpec(memory_space=out_space)
    return pl.pallas_call(
        kernel,
        in_specs=specs,
        out_specs=out_specs if single else [out_specs] * len(out_shape),
        out_shape=out_shape,
        scratch_shapes=list(scratch),
        compiler_params=pltpu.CompilerParams(vmem_limit_bytes=16 * 1024 * 1024),
    )(*values)


def body(residual, focus_bins, layer_class):
    depth, rows, x_cells = residual.shape
    half = x_cells // 2
    layers = layer_class.shape[0]
    hor_count = lax.axis_size("hor")
    y_cells = rows * hor_count
    chunk = half // hor_count
    plane_rows = rows * half // lanes
    dep = lax.axis_index("dep").astype(jnp.int32)
    hor = lax.axis_index("hor").astype(jnp.int32)
    dep_index = dep.reshape(1)
    spot = (hor * 2 + dep).reshape(1)

    table = np.stack(fold_tables(x_cells), axis=1)
    sine = sine_matrix(rows)
    near = np.concatenate([[0.0], sine[1, 1:]])
    far = np.concatenate([[0.0], sine[rows - 1, 1:]])
    lower_row = np.concatenate([[1.0], sine[1, 1:]])
    edge = np.concatenate([np.kron(np.eye(depth), row[None, :]) for row in (lower_row, far)])
    high, low = split_table(np.concatenate([np.kron(np.eye(depth), sine), edge]))
    small = np.concatenate([high, high, low], axis=1)
    wave_x = np.stack(
        [symbol_of(2.0 * np.pi * (2 * np.arange(half) + parity) / x_cells) for parity in range(2)]
    )
    mode = symbol_of(np.pi * np.arange(rows) / rows)
    inner = damping + smoothing * (mode[None, :, None] + wave_x[:, None, :])
    lane = np.arange(lanes)
    wave_number = (lane // chunk)[None, :] * plane_rows + np.arange(plane_rows)[:, None]
    wave_y = symbol_of(2.0 * np.pi * wave_number / y_cells)
    spots = np.arange(hor_count)[:, None, None] * chunk + (lane % chunk)[None, None, :]
    spots = 2 * spots + np.arange(2)[None, :, None]
    wave_spots = symbol_of(2.0 * np.pi * spots / x_cells).reshape(2 * hor_count, lanes)
    outer = np.concatenate([wave_y, wave_spots]).astype(np.float32)

    def shape(*dims):
        return jax.ShapeDtypeStruct(dims, f32)

    def constant(value):
        return (pltpu.HBM, jnp.asarray(value))

    def scalar(value):
        return (pltpu.SMEM, value)

    def near_by(value):
        return (pltpu.VMEM, value)

    slab = (depth, rows, half)
    full = (depth, rows, x_cells)
    field = (layers, rows, half)
    packed = (hor_count, layers, lanes)
    plane = (layers, plane_rows, lanes)
    cuts = 4
    own, send, weight, small_here, inner_here, outer_here = call(
        functools.partial(fold_kernel, cuts=cuts // 2),
        [scalar(dep_index)]
        + [(pltpu.HBM, value) for value in (residual, focus_bins, layer_class)]
        + [constant(value) for value in (small, inner.astype(np.float32), outer)],
        [
            shape(*slab),
            shape(*slab),
            shape(layers, 8, lanes),
            jax.ShapeDtypeStruct(small.shape, bf16),
            shape(2, rows, half),
            shape(*outer.shape),
        ],
        [
            pltpu.VMEM(full, f32),
            pltpu.VMEM(full, jnp.int32),
            pltpu.SMEM((layers,), jnp.int32),
            pltpu.SemaphoreType.DMA((2, cuts // 2)),
            pltpu.SemaphoreType.DMA,
            pltpu.SemaphoreType.DMA((3,)),
        ],
    )
    pairs = [(0, 1), (1, 0)]
    recv = lax.ppermute(send, "dep", pairs)
    modes, table_here, inverse, inverse_other, inverse_outer = call(
        prepare_kernel,
        [scalar(dep_index), scalar(spot), near_by(own), near_by(weight), constant(table)]
        + [near_by(value) for value in (small_here, inner_here, outer_here)],
        [
            shape(*slab),
            jax.ShapeDtypeStruct((2, half, half), bf16),
            shape(*field),
            shape(*field),
            shape(*plane),
        ],
        [pltpu.SemaphoreType.DMA((2,))],
    )
    outgoing, keep, give = call(
        interior_kernel,
        [scalar(dep_index)]
        + [near_by(v) for v in (modes, recv, table_here, small_here, weight, inverse)],
        [shape(*packed), shape(*slab), shape(*slab)],
        [pltpu.VMEM(field, f32)] * 4,
    )
    got = lax.ppermute(give, "dep", pairs)
    incoming = lax.all_to_all(outgoing, "hor", split_axis=0, concat_axis=0, tiled=True)
    incoming, got = lax.optimization_barrier((incoming, got))
    answered = call(
        functools.partial(interface_kernel, chunk=chunk),
        [scalar(spot), near_by(incoming), near_by(weight), near_by(inverse_outer)],
        shape(*packed),
        [pltpu.VMEM(packed, f32)] * 3 + [pltpu.VMEM(plane, f32)],
    )
    edges = lax.all_to_all(answered, "hor", split_axis=0, concat_axis=0, tiled=True)
    other_edges = lax.ppermute(edges, "dep", pairs)
    scratch = [pltpu.VMEM((layers, half), f32)] * 3 + [pltpu.VMEM(field, f32)]
    base, gain = call(
        functools.partial(restore_kernel, ends=(near,), scale=1.0 / x_cells),
        [scalar(dep_index)]
        + [
            near_by(v)
            for v in (edges, keep, table_here, small_here, weight, inverse, focus_bins)
        ],
        [shape(*full)] * 2,
        scratch,
    )
    return call(
        functools.partial(unfold_kernel, ends=(near,), cuts=cuts),
        [scalar(dep_index)]
        + [
            near_by(v)
            for v in (
                other_edges,
                got,
                jnp.asarray(table),
                small_here,
                weight,
                inverse_other,
                base,
                gain,
            )
        ],
        shape(*full),
        [pltpu.VMEM(full, f32), pltpu.SemaphoreType.DMA((cuts,))] + scratch,
        outside=True,
    )


def solution(mesh):
    return jax.shard_map(
        body,
        mesh=mesh,
        in_specs=(P(("grp", "dep"), "hor", None), P(("grp", "dep"), "hor", None), P("grp")),
        out_specs=P(("grp", "dep"), "hor", None),
        check_vma=False,
    )
```

```python
import functools
import math

import jax
import jax.numpy as jnp
import ml_dtypes
import numpy as np
from jax import lax
from jax.experimental import pallas as pl
from jax.experimental.pallas import tpu as pltpu
from jax.sharding import PartitionSpec as P

damping = 0.01
smoothing = 1.0
coupling_scale = 1.0
weight_base = 0.5
weight_step = 0.2
focus_base = 0.5
focus_step = 0.09242
lanes = 128
f32 = jnp.float32
bf16 = jnp.bfloat16


def cas(angle):
    return np.cos(angle) + np.sin(angle)


def split_table(table):
    table = table.astype(np.float32)
    high = table.astype(ml_dtypes.bfloat16)
    low = (table - high.astype(np.float32)).astype(ml_dtypes.bfloat16)
    return high, low


def fold_tables(length):
    half = length // 2
    cell = np.arange(half)[:, None]
    tables = []
    for parity in range(2):
        wave = 2 * np.arange(half)[None, :] + parity
        tables.append(cas(2.0 * np.pi * (cell * wave % length) / length))
    return split_table(np.stack(tables))


def sine_matrix(rows):
    index = np.arange(1, rows)
    matrix = np.zeros((rows, rows))
    matrix[0, 0] = 1.0
    matrix[1:, 1:] = np.sqrt(2.0 / rows) * np.sin(np.pi * np.outer(index, index) / rows)
    return matrix


def symbol_of(angle):
    return 2.0 - 2.0 * np.cos(angle)


def split(values):
    high = values.astype(bf16)
    low = (values - high.astype(f32)).astype(bf16)
    return high, low


def dot3(left, right, dims=(((1,), (0,)), ((), ()))):
    dot = functools.partial(lax.dot_general, dimension_numbers=dims, preferred_element_type=f32)
    left_high, left_low = left
    right_high, right_low = right
    rows = left_high.shape[0]
    both = dot(jnp.concatenate([left_high, left_low], axis=0), right_high)
    return both[:rows] + (both[rows:] + dot(left_high, right_low))


def focusing(focus_bins):
    return focus_base * jnp.exp(focus_step * focus_bins.astype(f32))


def layer_weights(class_ref, weight_ref):
    for layer in range(weight_ref.shape[0]):
        level = jnp.full(weight_ref.shape[1:], class_ref[layer], jnp.int32).astype(f32)
        weight_ref[layer] = weight_base * jnp.exp(weight_step * level)


def layer_terms(weight_ref, plane_tiles, axis):
    layers = weight_ref.shape[0]
    weights = [weight_ref[layer] for layer in range(layers)]
    couple = [coupling_scale * weights[k] * weights[k + 1] for k in range(layers - 1)]

    def spread(values):
        return [jnp.concatenate([value] * plane_tiles, axis=axis) for value in values]

    return spread(weights), spread(couple)


def row_values(values, shape):
    row = lax.broadcasted_iota(jnp.int32, shape, 0)
    total = jnp.full(shape, float(values[0]), f32)
    for index in range(1, len(values)):
        total = jnp.where(row == index, float(values[index]), total)
    return total


def diagonal(layer, weights, couple, wave):
    total = weights[layer] * wave
    if layer > 0:
        total = total + couple[layer - 1]
    if layer < len(couple):
        total = total + couple[layer]
    return total


def factor(weights, couple, wave, inverse_ref):
    layers = len(weights)
    half = layers // 2
    top = 1.0 / diagonal(0, weights, couple, wave)
    bottom = 1.0 / diagonal(layers - 1, weights, couple, wave)
    inverse_ref[0] = top
    inverse_ref[layers - 1] = bottom
    for step in range(1, half):
        low = step
        link = couple[low - 1]
        top = 1.0 / (diagonal(low, weights, couple, wave) - link * link * top)
        inverse_ref[low] = top
        high = layers - 1 - step
        link = couple[high]
        pivot = diagonal(high, weights, couple, wave) - link * link * bottom
        if step == half - 1:
            link = couple[half - 1]
            pivot = pivot - link * link * top
        bottom = 1.0 / pivot
        inverse_ref[high] = bottom


def substitute(couple, inverse_ref, partial_ref, source, emit, side=None):
    layers = len(couple) + 1
    half = layers // 2
    top = source(0)
    bottom = source(layers - 1)
    partial_ref[0] = top
    partial_ref[layers - 1] = bottom
    for step in range(1, half):
        low = step
        top = source(low) + couple[low - 1] * inverse_ref[low - 1] * top
        partial_ref[low] = top
        high = layers - 1 - step
        bottom = source(high) + couple[high] * inverse_ref[high + 1] * bottom
        partial_ref[high] = bottom
    link = couple[half - 1]
    bottom = (bottom + link * inverse_ref[half - 1] * top) * inverse_ref[half]
    top = (top + link * bottom) * inverse_ref[half - 1]
    if side != 0:
        emit(half, bottom)
    if side != 1:
        emit(half - 1, top)
    for step in range(1, half):
        if side != 1:
            low = half - 1 - step
            top = (partial_ref[low] + couple[low] * top) * inverse_ref[low]
            emit(low, top)
        if side != 0:
            high = half + step
            bottom = (partial_ref[high] + couple[high - 1] * bottom) * inverse_ref[high]
            emit(high, bottom)


def turn(values, shift):
    shift = shift % lanes
    return values if shift == 0 else pltpu.roll(values, shift, values.ndim - 1)


def fold_kernel(
    dep_ref,
    residual_hbm,
    bins_hbm,
    class_hbm,
    small_hbm,
    inner_hbm,
    outer_hbm,
    own_ref,
    send_ref,
    weight_ref,
    small_ref,
    inner_ref,
    outer_ref,
    residual_ref,
    bins_ref,
    class_ref,
    sems,
    class_sem,
    table_sems,
    *,
    cuts,
):
    depth, _, half = own_ref.shape
    size = depth // cuts
    class_copy = pltpu.make_async_copy(class_hbm, class_ref, class_sem)
    class_copy.start()
    copies = []
    for cut in range(cuts):
        part = pl.ds(cut * size, size)
        first = pltpu.make_async_copy(bins_hbm.at[part], bins_ref.at[part], sems.at[0, cut])
        second = pltpu.make_async_copy(
            residual_hbm.at[part], residual_ref.at[part], sems.at[1, cut]
        )
        first.start()
        second.start()
        copies.append((first, second))
    tables = [
        pltpu.make_async_copy(inner_hbm, inner_ref, table_sems.at[0]),
        pltpu.make_async_copy(outer_hbm, outer_ref, table_sems.at[1]),
        pltpu.make_async_copy(small_hbm, small_ref, table_sems.at[2]),
    ]
    for copy in tables:
        copy.start()
    sign = jnp.where(dep_ref[0] == 0, 1.0, -1.0).astype(f32)
    class_copy.wait()
    layer_weights(class_ref, weight_ref)
    for cut in range(cuts):
        part = pl.ds(cut * size, size)
        copies[cut][0].wait()
        focus_map = focusing(bins_ref[part])
        copies[cut][1].wait()
        scaled = focus_map * residual_ref[part]
        left = scaled[..., :half]
        right = sign * scaled[..., half:]
        own_ref[part] = left + right
        send_ref[part] = left - right
    for copy in tables:
        copy.wait()


def dot2(left, right):
    return jnp.dot(left, right, preferred_element_type=f32)


def to_modes(cells, table, sine):
    return dot3(split(from_modes(cells, sine)), table).reshape(cells.shape)


def from_modes(modes, sine):
    depth, rows, half = modes.shape
    high, low = split(modes.reshape(depth * rows, half))
    return dot2(sine, jnp.concatenate([high, low, high], axis=0))


def parts_of(small_ref, block, depth):
    return small_ref[:block], small_ref[block : block + 2 * depth]


def prepare_kernel(
    dep_ref,
    spot_ref,
    own_ref,
    weight_ref,
    table_hbm,
    small_ref,
    inner_ref,
    outer_ref,
    modes_ref,
    table_ref,
    inverse_ref,
    inverse_other_ref,
    inverse_outer_ref,
    sems,
):
    copies = [
        pltpu.make_async_copy(table_hbm.at[dep_ref[0], part], table_ref.at[part], sems.at[part])
        for part in range(2)
    ]
    for copy in copies:
        copy.start()
    depth, rows, half = own_ref.shape
    plane_rows = inverse_outer_ref.shape[1]
    weights, couple = layer_terms(weight_ref, half // lanes, 1)
    factor(weights, couple, inner_ref[dep_ref[0]], inverse_ref)
    factor(weights, couple, inner_ref[1 - dep_ref[0]], inverse_other_ref)
    weights, couple = layer_terms(weight_ref, plane_rows // 8, 0)
    wave = outer_ref[:plane_rows] + outer_ref[pl.ds(plane_rows + spot_ref[0], 1), :]
    factor(weights, couple, damping + smoothing * wave, inverse_outer_ref)
    sine, _ = parts_of(small_ref, depth * rows, depth)
    high, low = split(from_modes(own_ref[...], sine))
    block = depth * rows
    copies[0].wait()
    both = dot2(jnp.concatenate([high, low], axis=0), table_ref[0])
    copies[1].wait()
    total = both[:block] + (both[block:] + dot2(high, table_ref[1]))
    modes_ref[...] = total.reshape(depth, rows, half)


def interior_kernel(
    dep_ref,
    modes_ref,
    recv_ref,
    table_ref,
    small_ref,
    weight_ref,
    inverse_ref,
    packed_ref,
    keep_ref,
    give_ref,
    source_ref,
    solved_ref,
    stage_ref,
    partial_ref,
):
    depth, rows, half = recv_ref.shape
    layers = 2 * depth
    block = depth * rows
    hor_count = packed_ref.shape[0]
    chunk = half // hor_count
    place = dep_ref[0] * depth
    sine, edge = parts_of(small_ref, block, depth)
    source_ref[pl.ds(place, depth)] = modes_ref[...]
    source_ref[pl.ds(depth - place, depth)] = to_modes(
        recv_ref[...], (table_ref[0], table_ref[1]), sine
    )
    weights, couple = layer_terms(weight_ref, half // lanes, 1)
    edge_row = lax.broadcasted_iota(jnp.int32, (rows, half), 0) == 0

    def emit(layer, values):
        solved_ref[layer] = values
        stage_ref[layer] = jnp.where(edge_row, source_ref[layer], weights[layer] * values)

    substitute(couple, inverse_ref, partial_ref, lambda layer: source_ref[layer], emit)
    keep_ref[...] = solved_ref[pl.ds(place, depth)]
    give_ref[...] = solved_ref[pl.ds(depth - place, depth)]
    lower = []
    upper = []
    for part in range(2):
        both = from_modes(stage_ref[part * depth : (part + 1) * depth], edge)
        lower.append(both[:depth])
        upper.append(both[depth:])
    lower = jnp.concatenate(lower, axis=0)
    upper = jnp.concatenate(upper, axis=0)
    lane = lax.broadcasted_iota(jnp.int32, (layers, lanes), 1)
    if 2 * chunk == lanes:
        for tile in range(hor_count // 2):
            here = lower[:, tile * lanes : (tile + 1) * lanes]
            there = turn(upper[:, tile * lanes : (tile + 1) * lanes], chunk)
            packed_ref[2 * tile] = jnp.where(lane < chunk, here, there)
            packed_ref[2 * tile + 1] = jnp.where(lane < chunk, there, here)
        return
    for index in range(hor_count):
        tile = index * chunk // lanes * lanes
        offset = index * chunk % lanes
        packed_ref[index] = jnp.where(
            lane < chunk,
            turn(lower[:, tile : tile + lanes], -offset),
            turn(upper[:, tile : tile + lanes], chunk - offset),
        )


def hartley_8(read, write):
    parts = [read(index) for index in range(8)]
    plus = [parts[index] + parts[index + 4] for index in range(4)]
    minus = [parts[index] - parts[index + 4] for index in range(4)]
    root = math.sqrt(2.0)
    one, three = minus[1] * root, minus[3] * root
    same, cross = plus[0] + plus[2], plus[1] + plus[3]
    write(0, same + cross)
    write(4, same - cross)
    same, cross = plus[0] - plus[2], plus[1] - plus[3]
    write(2, same + cross)
    write(6, same - cross)
    same, cross = minus[0] + minus[2], minus[0] - minus[2]
    write(1, same + one)
    write(5, same - one)
    write(3, cross + three)
    write(7, cross - three)


def small_hartley(count, read, write, shape):
    if count == 8:
        hartley_8(read, write)
        return
    if count <= 8:
        table = cas(2.0 * np.pi * (np.outer(np.arange(count), np.arange(count)) % count) / count)
        parts = [read(index) for index in range(count)]
        for wave in range(count):
            total = None
            for index in range(count):
                value = float(table[wave, index])
                if abs(value) < 1e-12:
                    continue
                if abs(value - 1.0) < 1e-12:
                    term = parts[index]
                elif abs(value + 1.0) < 1e-12:
                    term = -parts[index]
                else:
                    term = parts[index] * value
                total = term if total is None else total + term
            write(wave, total)
        return

    def outer(wave, carry):
        def inner(index, total):
            angle = jnp.full(shape, wave * index % count, jnp.int32).astype(f32)
            angle = angle * (2.0 * math.pi / count)
            return total + read(index) * (jnp.cos(angle) + jnp.sin(angle))

        write(wave, lax.fori_loop(0, count, inner, jnp.zeros(shape, f32)))
        return carry

    lax.fori_loop(0, count, outer, 0)


def interface_kernel(
    spot_ref,
    packed_ref,
    weight_ref,
    inverse_ref,
    back_ref,
    sum_ref,
    wave_ref,
    answer_ref,
    partial_ref,
    *,
    chunk,
):
    hor_count, layers, _ = packed_ref.shape
    rows = inverse_ref.shape[1]
    subsets = lanes // chunk
    classes = max(1, hor_count // rows)
    repeats = max(1, rows // hor_count)
    lane = lax.broadcasted_iota(jnp.int32, (layers, lanes), 1)
    swapped = spot_ref[0] // 2 % 2 if 2 * chunk == lanes else 0
    first = lane // chunk % 2 == swapped

    def halves(index):
        values = packed_ref[index]
        width = 2 * chunk
        while width < lanes:
            values = jnp.where(lane < width, values, turn(values, width))
            width = width * 2
        return values

    def joined(index):
        here = halves(index)
        before = halves((index + hor_count - 1) % hor_count)
        return jnp.where(first, here, turn(here, chunk)) + jnp.where(
            first, turn(before, -chunk), before
        )

    def put_sum(index, values):
        sum_ref[index] = values

    if hor_count <= 8:
        pairs = []
        for index in range(hor_count):
            here = halves(index)
            there = turn(here, chunk)
            back = there if 2 * chunk == lanes else turn(here, -chunk)
            pairs.append((jnp.where(first, here, there), jnp.where(first, back, here)))
        joint = [pairs[index][0] + pairs[index - 1][1] for index in range(hor_count)]
        small_hartley(hor_count, joint.__getitem__, lambda k, v: wave_ref.__setitem__(k, v), (layers, lanes))
    else:
        lax.fori_loop(0, hor_count, lambda k, c: (put_sum(k, joined(k)), c)[1], 0)
        small_hartley(
            hor_count,
            lambda k: sum_ref[k],
            lambda k, v: wave_ref.__setitem__(k, v),
            (layers, lanes),
        )
    weights, couple = layer_terms(weight_ref, rows // 8, 0)
    turned = jnp.swapaxes(wave_ref[...], 0, 1) if classes == 1 else None
    plane_lane = lax.broadcasted_iota(jnp.int32, (rows, lanes), 1)
    group = plane_lane // chunk % classes

    def source(layer):
        if classes == 1:
            return jnp.concatenate([turned[layer]] * repeats, axis=0)
        total = wave_ref[0:rows, layer, :]
        for part in range(1, classes):
            piece = wave_ref[part * rows : (part + 1) * rows, layer, :]
            total = jnp.where(group == part, piece, total)
        return total

    def emit(layer, values):
        if classes == 1:
            total = values[0:hor_count]
            for part in range(1, repeats):
                total = total + values[part * hor_count : (part + 1) * hor_count]
            gathering[layer] = total
            return
        for part in range(classes):
            answer_ref[part * rows : (part + 1) * rows, layer, :] = jnp.where(
                group == part, values, 0.0
            )

    gathering = [None] * layers
    substitute(couple, inverse_ref, partial_ref, source, emit)
    if classes == 1:
        answer_ref[...] = jnp.swapaxes(jnp.stack(gathering), 0, 1)

    def gathered(index):
        values = answer_ref[index]
        shift = chunk
        while shift < lanes:
            values = values + turn(values, shift)
            shift = shift * 2
        return values

    scale = 1.0 / (rows * subsets)

    def put_scaled(index, values):
        sum_ref[index] = values * scale

    if hor_count <= 8:
        small_hartley(hor_count, gathered, put_scaled, (layers, lanes))
    else:
        lax.fori_loop(
            0, hor_count, lambda k, c: (wave_ref.__setitem__(k, gathered(k)), c)[1], 0
        )
        small_hartley(hor_count, lambda k: wave_ref[k], put_scaled, (layers, lanes))
    for index in range(hor_count):
        back_ref[index] = jnp.where(first, sum_ref[index], sum_ref[(index + 1) % hor_count])


def extend(
    side,
    back_ref,
    solved_ref,
    table,
    small_ref,
    weight_ref,
    inverse_ref,
    left_ref,
    right_ref,
    sum_ref,
    partial_ref,
    ends,
    turned=False,
):
    depth, rows, half = solved_ref.shape
    layers = 2 * depth
    hor_count = back_ref.shape[0]
    chunk = half // hor_count
    lane = lax.broadcasted_iota(jnp.int32, (layers, lanes), 1)
    for tile in range(half // lanes if 2 * chunk == lanes else 0):
        even = back_ref[2 * tile]
        odd = back_ref[2 * tile + 1]
        inside = lane < chunk
        left_ref[:, tile * lanes : (tile + 1) * lanes] = jnp.where(inside, even, odd)
        right = turn(jnp.where(inside, odd, even), chunk)
        right_ref[:, tile * lanes : (tile + 1) * lanes] = right
    for tile in range(0 if 2 * chunk == lanes else half // lanes):
        left = None
        right = None
        for index in range(tile * lanes // chunk, (tile + 1) * lanes // chunk):
            offset = index * chunk % lanes
            values = back_ref[index]
            left_part = turn(values, offset)
            right_part = turn(values, offset - chunk)
            inside = lane >= offset
            left = left_part if left is None else jnp.where(inside, left_part, left)
            right = right_part if right is None else jnp.where(inside, right_part, right)
        left_ref[:, tile * lanes : (tile + 1) * lanes] = left
        right_ref[:, tile * lanes : (tile + 1) * lanes] = right
    weights, couple = layer_terms(weight_ref, half // lanes, 1)
    near = row_values(ends[0], (rows, lanes))
    odd = lax.broadcasted_iota(jnp.int32, (rows, half), 0) % 2 == 1
    sum_ref[...] = left_ref[...] + right_ref[...]
    right_ref[...] = left_ref[...] - right_ref[...]

    def row_of(ref, layer):
        return jnp.broadcast_to(ref[pl.ds(layer, 1), :], (rows, half))

    def source(layer):
        factors = jnp.concatenate([weight_ref[layer] * near] * (half // lanes), axis=1)
        return factors * jnp.where(odd, row_of(sum_ref, layer), row_of(right_ref, layer))

    edge_row = lax.broadcasted_iota(jnp.int32, (rows, half), 0) == 0
    place = side * depth
    found = [None] * depth

    def emit(layer, values):
        layer_here = layer - place
        total = solved_ref[layer_here] + values
        found[layer_here] = jnp.where(edge_row, row_of(left_ref, layer), total)

    substitute(couple, inverse_ref, partial_ref, source, emit, side)
    modes = jnp.stack(found)
    sine, _ = parts_of(small_ref, depth * rows, depth)
    waves = from_modes(modes, sine)
    cells = dot3(split(waves), table, (((1,), (0 if turned else 1,)), ((), ())))
    return cells.reshape(depth, rows, half)


def restore_kernel(
    dep_ref,
    back_ref,
    solved_ref,
    table_ref,
    small_ref,
    weight_ref,
    inverse_ref,
    bins_ref,
    both_ref,
    base_ref,
    gain_ref,
    turned_ref,
    *scratch,
    ends,
    scale,
):
    half = solved_ref.shape[-1]

    def work(side):
        sign = scale if side else -scale
        left = focusing(bins_ref[:, :, :half]) * scale
        right = focusing(bins_ref[:, :, half:]) * sign
        gain_ref[:, :, :half] = left
        gain_ref[:, :, half:] = right
        table = (table_ref[0], table_ref[1])
        cells = extend(
            side, back_ref, solved_ref, table, small_ref, weight_ref, inverse_ref, *scratch, ends
        )
        base_ref[:, :, :half] = gain_ref[:, :, :half] * cells
        base_ref[:, :, half:] = -(gain_ref[:, :, half:] * cells)
        for part in range(2):
            turned_ref[part] = both_ref[1 - side, part].T

    pl.when(dep_ref[0] == 0)(lambda: work(0))
    pl.when(dep_ref[0] == 1)(lambda: work(1))


def unfold_kernel(
    dep_ref,
    back_ref,
    solved_ref,
    table_ref,
    small_ref,
    weight_ref,
    inverse_ref,
    base_ref,
    gain_ref,
    out_hbm,
    out_ref,
    sems,
    *scratch,
    ends,
    cuts,
):
    depth, _, half = solved_ref.shape
    size = depth // cuts

    def work(side):
        table = (table_ref[0], table_ref[1])
        cells = extend(
            side,
            back_ref,
            solved_ref,
            table,
            small_ref,
            weight_ref,
            inverse_ref,
            *scratch,
            ends,
            True,
        )
        copies = []
        for cut in range(cuts):
            part = slice(cut * size, (cut + 1) * size)
            for ends_here in (slice(0, half), slice(half, 2 * half)):
                out_ref[part, :, ends_here] = (
                    base_ref[part, :, ends_here] + gain_ref[part, :, ends_here] * cells[part]
                )
            copy = pltpu.make_async_copy(out_ref.at[part], out_hbm.at[part], sems.at[cut])
            copy.start()
            copies.append(copy)
        for copy in copies:
            copy.wait()

    pl.when(dep_ref[0] == 0)(lambda: work(0))
    pl.when(dep_ref[0] == 1)(lambda: work(1))


def call(kernel, operands, out_shape, scratch=(), outside=False):
    specs = []
    values = []
    for space, value in operands:
        specs.append(pl.BlockSpec(memory_space=space))
        if space is pltpu.HBM:
            value = pltpu.with_memory_space_constraint(value, pltpu.HBM)
        values.append(value)
    out_space = pltpu.HBM if outside else pltpu.VMEM
    single = not isinstance(out_shape, list)
    out_specs = pl.BlockSpec(memory_space=out_space)
    return pl.pallas_call(
        kernel,
        in_specs=specs,
        out_specs=out_specs if single else [out_specs] * len(out_shape),
        out_shape=out_shape,
        scratch_shapes=list(scratch),
        compiler_params=pltpu.CompilerParams(vmem_limit_bytes=16 * 1024 * 1024),
    )(*values)


def body(residual, focus_bins, layer_class):
    depth, rows, x_cells = residual.shape
    half = x_cells // 2
    layers = layer_class.shape[0]
    hor_count = lax.axis_size("hor")
    y_cells = rows * hor_count
    chunk = half // hor_count
    plane_rows = rows * half // lanes
    dep = lax.axis_index("dep").astype(jnp.int32)
    hor = lax.axis_index("hor").astype(jnp.int32)
    dep_index = dep.reshape(1)
    spot = (hor * 2 + dep).reshape(1)

    table = np.stack(fold_tables(x_cells), axis=1)
    sine = sine_matrix(rows)
    near = np.concatenate([[0.0], sine[1, 1:]])
    far = np.concatenate([[0.0], sine[rows - 1, 1:]])
    lower_row = np.concatenate([[1.0], sine[1, 1:]])
    edge = np.concatenate([np.kron(np.eye(depth), row[None, :]) for row in (lower_row, far)])
    high, low = split_table(np.concatenate([np.kron(np.eye(depth), sine), edge]))
    small = np.concatenate([high, high, low], axis=1)
    wave_x = np.stack(
        [symbol_of(2.0 * np.pi * (2 * np.arange(half) + parity) / x_cells) for parity in range(2)]
    )
    mode = symbol_of(np.pi * np.arange(rows) / rows)
    inner = damping + smoothing * (mode[None, :, None] + wave_x[:, None, :])
    lane = np.arange(lanes)
    wave_number = (lane // chunk)[None, :] * plane_rows + np.arange(plane_rows)[:, None]
    wave_y = symbol_of(2.0 * np.pi * wave_number / y_cells)
    spots = np.arange(hor_count)[:, None, None] * chunk + (lane % chunk)[None, None, :]
    spots = 2 * spots + np.arange(2)[None, :, None]
    wave_spots = symbol_of(2.0 * np.pi * spots / x_cells).reshape(2 * hor_count, lanes)
    outer = np.concatenate([wave_y, wave_spots]).astype(np.float32)

    def shape(*dims):
        return jax.ShapeDtypeStruct(dims, f32)

    def constant(value):
        return (pltpu.HBM, jnp.asarray(value))

    def scalar(value):
        return (pltpu.SMEM, value)

    def near_by(value):
        return (pltpu.VMEM, value)

    slab = (depth, rows, half)
    full = (depth, rows, x_cells)
    field = (layers, rows, half)
    packed = (hor_count, layers, lanes)
    plane = (layers, plane_rows, lanes)
    cuts = 4
    own, send, weight, small_here, inner_here, outer_here = call(
        functools.partial(fold_kernel, cuts=cuts // 2),
        [scalar(dep_index)]
        + [(pltpu.HBM, value) for value in (residual, focus_bins, layer_class)]
        + [constant(value) for value in (small, inner.astype(np.float32), outer)],
        [
            shape(*slab),
            shape(*slab),
            shape(layers, 8, lanes),
            jax.ShapeDtypeStruct(small.shape, bf16),
            shape(2, rows, half),
            shape(*outer.shape),
        ],
        [
            pltpu.VMEM(full, f32),
            pltpu.VMEM(full, jnp.int32),
            pltpu.SMEM((layers,), jnp.int32),
            pltpu.SemaphoreType.DMA((2, cuts // 2)),
            pltpu.SemaphoreType.DMA,
            pltpu.SemaphoreType.DMA((3,)),
        ],
    )
    pairs = [(0, 1), (1, 0)]
    recv = lax.ppermute(send, "dep", pairs)
    modes, table_here, inverse, inverse_other, inverse_outer = call(
        prepare_kernel,
        [scalar(dep_index), scalar(spot), near_by(own), near_by(weight), constant(table)]
        + [near_by(value) for value in (small_here, inner_here, outer_here)],
        [
            shape(*slab),
            jax.ShapeDtypeStruct((2, half, half), bf16),
            shape(*field),
            shape(*field),
            shape(*plane),
        ],
        [pltpu.SemaphoreType.DMA((2,))],
    )
    outgoing, keep, give = call(
        interior_kernel,
        [scalar(dep_index)]
        + [near_by(v) for v in (modes, recv, table_here, small_here, weight, inverse)],
        [shape(*packed), shape(*slab), shape(*slab)],
        [pltpu.VMEM(field, f32)] * 4,
    )
    got = lax.ppermute(give, "dep", pairs)
    incoming = lax.all_to_all(outgoing, "hor", split_axis=0, concat_axis=0, tiled=True)
    incoming, got = lax.optimization_barrier((incoming, got))
    answered = call(
        functools.partial(interface_kernel, chunk=chunk),
        [scalar(spot), near_by(incoming), near_by(weight), near_by(inverse_outer)],
        shape(*packed),
        [pltpu.VMEM(packed, f32)] * 3 + [pltpu.VMEM(plane, f32)],
    )
    edges = lax.all_to_all(answered, "hor", split_axis=0, concat_axis=0, tiled=True)
    other_edges = lax.ppermute(edges, "dep", pairs)
    scratch = [pltpu.VMEM((layers, half), f32)] * 3 + [pltpu.VMEM(field, f32)]
    both = jnp.asarray(table)
    base, gain, turned = call(
        functools.partial(restore_kernel, ends=(near,), scale=1.0 / x_cells),
        [scalar(dep_index)]
        + [
            near_by(v)
            for v in (edges, keep, table_here, small_here, weight, inverse, focus_bins, both)
        ],
        [shape(*full)] * 2 + [jax.ShapeDtypeStruct((2, half, half), bf16)],
        scratch,
    )
    return call(
        functools.partial(unfold_kernel, ends=(near,), cuts=cuts),
        [scalar(dep_index)]
        + [
            near_by(v)
            for v in (
                other_edges,
                got,
                turned,
                small_here,
                weight,
                inverse_other,
                base,
                gain,
            )
        ],
        shape(*full),
        [pltpu.VMEM(full, f32), pltpu.SemaphoreType.DMA((cuts,))] + scratch,
        outside=True,
    )


def solution(mesh):
    return jax.shard_map(
        body,
        mesh=mesh,
        in_specs=(P(("grp", "dep"), "hor", None), P(("grp", "dep"), "hor", None), P("grp")),
        out_specs=P(("grp", "dep"), "hor", None),
        check_vma=False,
    )
```

```python
import functools
import math

import jax
import jax.numpy as jnp
import ml_dtypes
import numpy as np
from jax import lax
from jax.experimental import pallas as pl
from jax.experimental.pallas import tpu as pltpu
from jax.sharding import PartitionSpec as P

damping = 0.01
smoothing = 1.0
coupling_scale = 1.0
weight_base = 0.5
weight_step = 0.2
focus_base = 0.5
focus_step = 0.09242
lanes = 128
f32 = jnp.float32
bf16 = jnp.bfloat16


def cas(angle):
    return np.cos(angle) + np.sin(angle)


def split_table(table):
    table = table.astype(np.float32)
    high = table.astype(ml_dtypes.bfloat16)
    low = (table - high.astype(np.float32)).astype(ml_dtypes.bfloat16)
    return high, low


def fold_tables(length):
    half = length // 2
    cell = np.arange(half)[:, None]
    tables = []
    for parity in range(2):
        wave = 2 * np.arange(half)[None, :] + parity
        tables.append(cas(2.0 * np.pi * (cell * wave % length) / length))
    return split_table(np.stack(tables))


def sine_matrix(rows):
    index = np.arange(1, rows)
    matrix = np.zeros((rows, rows))
    matrix[0, 0] = 1.0
    matrix[1:, 1:] = np.sqrt(2.0 / rows) * np.sin(np.pi * np.outer(index, index) / rows)
    return matrix


def symbol_of(angle):
    return 2.0 - 2.0 * np.cos(angle)


def split(values):
    high = values.astype(bf16)
    low = (values - high.astype(f32)).astype(bf16)
    return high, low


def dot3(left, right, dims=(((1,), (0,)), ((), ()))):
    dot = functools.partial(lax.dot_general, dimension_numbers=dims, preferred_element_type=f32)
    left_high, left_low = left
    right_high, right_low = right
    rows = left_high.shape[0]
    both = dot(jnp.concatenate([left_high, left_low], axis=0), right_high)
    return both[:rows] + (both[rows:] + dot(left_high, right_low))


def focusing(focus_bins):
    return focus_base * jnp.exp(focus_step * focus_bins.astype(f32))


def layer_weights(class_ref, weight_ref):
    for layer in range(weight_ref.shape[0]):
        level = jnp.full(weight_ref.shape[1:], class_ref[layer], jnp.int32).astype(f32)
        weight_ref[layer] = weight_base * jnp.exp(weight_step * level)


def layer_terms(weight_ref, plane_tiles, axis):
    layers = weight_ref.shape[0]
    weights = [weight_ref[layer] for layer in range(layers)]
    couple = [coupling_scale * weights[k] * weights[k + 1] for k in range(layers - 1)]

    def spread(values):
        return [jnp.concatenate([value] * plane_tiles, axis=axis) for value in values]

    return spread(weights), spread(couple)


def row_values(values, shape):
    row = lax.broadcasted_iota(jnp.int32, shape, 0)
    total = jnp.full(shape, float(values[0]), f32)
    for index in range(1, len(values)):
        total = jnp.where(row == index, float(values[index]), total)
    return total


def diagonal(layer, weights, couple, wave):
    total = weights[layer] * wave
    if layer > 0:
        total = total + couple[layer - 1]
    if layer < len(couple):
        total = total + couple[layer]
    return total


def factor(weights, couple, wave, inverse_ref):
    layers = len(weights)
    half = layers // 2
    top = 1.0 / diagonal(0, weights, couple, wave)
    bottom = 1.0 / diagonal(layers - 1, weights, couple, wave)
    inverse_ref[0] = top
    inverse_ref[layers - 1] = bottom
    for step in range(1, half):
        low = step
        link = couple[low - 1]
        top = 1.0 / (diagonal(low, weights, couple, wave) - link * link * top)
        inverse_ref[low] = top
        high = layers - 1 - step
        link = couple[high]
        pivot = diagonal(high, weights, couple, wave) - link * link * bottom
        if step == half - 1:
            link = couple[half - 1]
            pivot = pivot - link * link * top
        bottom = 1.0 / pivot
        inverse_ref[high] = bottom


def substitute(couple, inverse_ref, partial_ref, source, emit, side=None):
    layers = len(couple) + 1
    half = layers // 2
    top = source(0)
    bottom = source(layers - 1)
    partial_ref[0] = top
    partial_ref[layers - 1] = bottom
    for step in range(1, half):
        low = step
        top = source(low) + couple[low - 1] * inverse_ref[low - 1] * top
        partial_ref[low] = top
        high = layers - 1 - step
        bottom = source(high) + couple[high] * inverse_ref[high + 1] * bottom
        partial_ref[high] = bottom
    link = couple[half - 1]
    bottom = (bottom + link * inverse_ref[half - 1] * top) * inverse_ref[half]
    top = (top + link * bottom) * inverse_ref[half - 1]
    if side != 0:
        emit(half, bottom)
    if side != 1:
        emit(half - 1, top)
    for step in range(1, half):
        if side != 1:
            low = half - 1 - step
            top = (partial_ref[low] + couple[low] * top) * inverse_ref[low]
            emit(low, top)
        if side != 0:
            high = half + step
            bottom = (partial_ref[high] + couple[high - 1] * bottom) * inverse_ref[high]
            emit(high, bottom)


def turn(values, shift):
    shift = shift % lanes
    return values if shift == 0 else pltpu.roll(values, shift, values.ndim - 1)


def fold_kernel(
    dep_ref,
    residual_hbm,
    bins_hbm,
    class_hbm,
    small_hbm,
    inner_hbm,
    outer_hbm,
    own_ref,
    send_ref,
    weight_ref,
    small_ref,
    inner_ref,
    outer_ref,
    residual_ref,
    bins_ref,
    class_ref,
    sems,
    class_sem,
    table_sems,
    *,
    cuts,
):
    depth, _, half = own_ref.shape
    size = depth // cuts
    class_copy = pltpu.make_async_copy(class_hbm, class_ref, class_sem)
    class_copy.start()
    copies = []
    for cut in range(cuts):
        part = pl.ds(cut * size, size)
        first = pltpu.make_async_copy(bins_hbm.at[part], bins_ref.at[part], sems.at[0, cut])
        second = pltpu.make_async_copy(
            residual_hbm.at[part], residual_ref.at[part], sems.at[1, cut]
        )
        first.start()
        second.start()
        copies.append((first, second))
    tables = [
        pltpu.make_async_copy(inner_hbm, inner_ref, table_sems.at[0]),
        pltpu.make_async_copy(outer_hbm, outer_ref, table_sems.at[1]),
        pltpu.make_async_copy(small_hbm, small_ref, table_sems.at[2]),
    ]
    for copy in tables:
        copy.start()
    sign = jnp.where(dep_ref[0] == 0, 1.0, -1.0).astype(f32)
    class_copy.wait()
    layer_weights(class_ref, weight_ref)
    for cut in range(cuts):
        part = pl.ds(cut * size, size)
        copies[cut][0].wait()
        focus_map = focusing(bins_ref[part])
        copies[cut][1].wait()
        scaled = focus_map * residual_ref[part]
        left = scaled[..., :half]
        right = sign * scaled[..., half:]
        own_ref[part] = left + right
        send_ref[part] = left - right
    for copy in tables:
        copy.wait()


def dot2(left, right):
    return jnp.dot(left, right, preferred_element_type=f32)


def to_modes(cells, table, sine):
    return dot3(split(from_modes(cells, sine)), table).reshape(cells.shape)


def from_modes(modes, sine):
    depth, rows, half = modes.shape
    high, low = split(modes.reshape(depth * rows, half))
    return dot2(sine, jnp.concatenate([high, low, high], axis=0))


def parts_of(small_ref, block, depth):
    return small_ref[:block], small_ref[block : block + 2 * depth]


def prepare_kernel(
    dep_ref,
    spot_ref,
    own_ref,
    weight_ref,
    table_hbm,
    small_ref,
    inner_ref,
    outer_ref,
    modes_ref,
    table_ref,
    inverse_ref,
    inverse_other_ref,
    inverse_outer_ref,
    sems,
):
    copies = [
        pltpu.make_async_copy(table_hbm.at[dep_ref[0], part], table_ref.at[part], sems.at[part])
        for part in range(2)
    ]
    for copy in copies:
        copy.start()
    depth, rows, half = own_ref.shape
    plane_rows = inverse_outer_ref.shape[1]
    weights, couple = layer_terms(weight_ref, half // lanes, 1)
    factor(weights, couple, inner_ref[dep_ref[0]], inverse_ref)
    factor(weights, couple, inner_ref[1 - dep_ref[0]], inverse_other_ref)
    weights, couple = layer_terms(weight_ref, plane_rows // 8, 0)
    wave = outer_ref[:plane_rows] + outer_ref[pl.ds(plane_rows + spot_ref[0], 1), :]
    factor(weights, couple, damping + smoothing * wave, inverse_outer_ref)
    sine, _ = parts_of(small_ref, depth * rows, depth)
    high, low = split(from_modes(own_ref[...], sine))
    block = depth * rows
    copies[0].wait()
    both = dot2(jnp.concatenate([high, low], axis=0), table_ref[0])
    copies[1].wait()
    total = both[:block] + (both[block:] + dot2(high, table_ref[1]))
    modes_ref[...] = total.reshape(depth, rows, half)


def interior_kernel(
    dep_ref,
    modes_ref,
    recv_ref,
    table_ref,
    small_ref,
    weight_ref,
    inverse_ref,
    packed_ref,
    keep_ref,
    give_ref,
    partial_ref,
):
    depth, rows, half = recv_ref.shape
    layers = 2 * depth
    block = depth * rows
    hor_count = packed_ref.shape[0]
    chunk = half // hor_count

    def work(side):
        sine, edge = parts_of(small_ref, block, depth)
        modes = to_modes(recv_ref[...], (table_ref[0], table_ref[1]), sine)
        weights, couple = layer_terms(weight_ref, half // lanes, 1)
        edge_row = lax.broadcasted_iota(jnp.int32, (rows, half), 0) == 0
        staged = [None] * layers

        def source(layer):
            if layer // depth == side:
                return modes_ref[layer - side * depth]
            return modes[layer - (1 - side) * depth]

        def emit(layer, values):
            if layer // depth == side:
                keep_ref[layer - side * depth] = values
            else:
                give_ref[layer - (1 - side) * depth] = values
            staged[layer] = jnp.where(edge_row, source(layer), weights[layer] * values)

        substitute(couple, inverse_ref, partial_ref, source, emit)
        lower = []
        upper = []
        for part in range(2):
            both = from_modes(jnp.stack(staged[part * depth : (part + 1) * depth]), edge)
            lower.append(both[:depth])
            upper.append(both[depth:])
        pack(jnp.concatenate(lower, axis=0), jnp.concatenate(upper, axis=0), packed_ref)

    pl.when(dep_ref[0] == 0)(lambda: work(0))
    pl.when(dep_ref[0] == 1)(lambda: work(1))


def pack(lower, upper, packed_ref):
    hor_count, layers, _ = packed_ref.shape
    chunk = lower.shape[1] // hor_count
    lane = lax.broadcasted_iota(jnp.int32, (layers, lanes), 1)
    if 2 * chunk == lanes:
        for tile in range(hor_count // 2):
            here = lower[:, tile * lanes : (tile + 1) * lanes]
            there = turn(upper[:, tile * lanes : (tile + 1) * lanes], chunk)
            packed_ref[2 * tile] = jnp.where(lane < chunk, here, there)
            packed_ref[2 * tile + 1] = jnp.where(lane < chunk, there, here)
        return
    for index in range(hor_count):
        tile = index * chunk // lanes * lanes
        offset = index * chunk % lanes
        packed_ref[index] = jnp.where(
            lane < chunk,
            turn(lower[:, tile : tile + lanes], -offset),
            turn(upper[:, tile : tile + lanes], chunk - offset),
        )


def hartley_8(read, write):
    parts = [read(index) for index in range(8)]
    plus = [parts[index] + parts[index + 4] for index in range(4)]
    minus = [parts[index] - parts[index + 4] for index in range(4)]
    root = math.sqrt(2.0)
    one, three = minus[1] * root, minus[3] * root
    same, cross = plus[0] + plus[2], plus[1] + plus[3]
    write(0, same + cross)
    write(4, same - cross)
    same, cross = plus[0] - plus[2], plus[1] - plus[3]
    write(2, same + cross)
    write(6, same - cross)
    same, cross = minus[0] + minus[2], minus[0] - minus[2]
    write(1, same + one)
    write(5, same - one)
    write(3, cross + three)
    write(7, cross - three)


def small_hartley(count, read, write, shape):
    if count == 8:
        hartley_8(read, write)
        return
    if count <= 8:
        table = cas(2.0 * np.pi * (np.outer(np.arange(count), np.arange(count)) % count) / count)
        parts = [read(index) for index in range(count)]
        for wave in range(count):
            total = None
            for index in range(count):
                value = float(table[wave, index])
                if abs(value) < 1e-12:
                    continue
                if abs(value - 1.0) < 1e-12:
                    term = parts[index]
                elif abs(value + 1.0) < 1e-12:
                    term = -parts[index]
                else:
                    term = parts[index] * value
                total = term if total is None else total + term
            write(wave, total)
        return

    def outer(wave, carry):
        def inner(index, total):
            angle = jnp.full(shape, wave * index % count, jnp.int32).astype(f32)
            angle = angle * (2.0 * math.pi / count)
            return total + read(index) * (jnp.cos(angle) + jnp.sin(angle))

        write(wave, lax.fori_loop(0, count, inner, jnp.zeros(shape, f32)))
        return carry

    lax.fori_loop(0, count, outer, 0)


def interface_kernel(
    spot_ref,
    packed_ref,
    weight_ref,
    inverse_ref,
    back_ref,
    sum_ref,
    wave_ref,
    answer_ref,
    partial_ref,
    *,
    chunk,
):
    hor_count, layers, _ = packed_ref.shape
    rows = inverse_ref.shape[1]
    subsets = lanes // chunk
    classes = max(1, hor_count // rows)
    repeats = max(1, rows // hor_count)
    lane = lax.broadcasted_iota(jnp.int32, (layers, lanes), 1)
    swapped = spot_ref[0] // 2 % 2 if 2 * chunk == lanes else 0
    first = lane // chunk % 2 == swapped

    def halves(index):
        values = packed_ref[index]
        width = 2 * chunk
        while width < lanes:
            values = jnp.where(lane < width, values, turn(values, width))
            width = width * 2
        return values

    def joined(index):
        here = halves(index)
        before = halves((index + hor_count - 1) % hor_count)
        return jnp.where(first, here, turn(here, chunk)) + jnp.where(
            first, turn(before, -chunk), before
        )

    def put_sum(index, values):
        sum_ref[index] = values

    if hor_count <= 8:
        pairs = []
        for index in range(hor_count):
            here = halves(index)
            there = turn(here, chunk)
            back = there if 2 * chunk == lanes else turn(here, -chunk)
            pairs.append((jnp.where(first, here, there), jnp.where(first, back, here)))
        joint = [pairs[index][0] + pairs[index - 1][1] for index in range(hor_count)]
        small_hartley(hor_count, joint.__getitem__, lambda k, v: wave_ref.__setitem__(k, v), (layers, lanes))
    else:
        lax.fori_loop(0, hor_count, lambda k, c: (put_sum(k, joined(k)), c)[1], 0)
        small_hartley(
            hor_count,
            lambda k: sum_ref[k],
            lambda k, v: wave_ref.__setitem__(k, v),
            (layers, lanes),
        )
    weights, couple = layer_terms(weight_ref, rows // 8, 0)
    turned = jnp.swapaxes(wave_ref[...], 0, 1) if classes == 1 else None
    plane_lane = lax.broadcasted_iota(jnp.int32, (rows, lanes), 1)
    group = plane_lane // chunk % classes

    def source(layer):
        if classes == 1:
            return jnp.concatenate([turned[layer]] * repeats, axis=0)
        total = wave_ref[0:rows, layer, :]
        for part in range(1, classes):
            piece = wave_ref[part * rows : (part + 1) * rows, layer, :]
            total = jnp.where(group == part, piece, total)
        return total

    def emit(layer, values):
        if classes == 1:
            total = values[0:hor_count]
            for part in range(1, repeats):
                total = total + values[part * hor_count : (part + 1) * hor_count]
            gathering[layer] = total
            return
        for part in range(classes):
            answer_ref[part * rows : (part + 1) * rows, layer, :] = jnp.where(
                group == part, values, 0.0
            )

    gathering = [None] * layers
    substitute(couple, inverse_ref, partial_ref, source, emit)
    if classes == 1:
        answer_ref[...] = jnp.swapaxes(jnp.stack(gathering), 0, 1)

    def gathered(index):
        values = answer_ref[index]
        shift = chunk
        while shift < lanes:
            values = values + turn(values, shift)
            shift = shift * 2
        return values

    scale = 1.0 / (rows * subsets)

    def put_scaled(index, values):
        sum_ref[index] = values * scale

    if hor_count <= 8:
        small_hartley(hor_count, gathered, put_scaled, (layers, lanes))
    else:
        lax.fori_loop(
            0, hor_count, lambda k, c: (wave_ref.__setitem__(k, gathered(k)), c)[1], 0
        )
        small_hartley(hor_count, lambda k: wave_ref[k], put_scaled, (layers, lanes))
    for index in range(hor_count):
        back_ref[index] = jnp.where(first, sum_ref[index], sum_ref[(index + 1) % hor_count])


def extend(
    side,
    back_ref,
    solved_ref,
    table,
    small_ref,
    weight_ref,
    inverse_ref,
    left_ref,
    right_ref,
    sum_ref,
    partial_ref,
    ends,
    turned=False,
):
    depth, rows, half = solved_ref.shape
    layers = 2 * depth
    hor_count = back_ref.shape[0]
    chunk = half // hor_count
    lane = lax.broadcasted_iota(jnp.int32, (layers, lanes), 1)
    for tile in range(half // lanes if 2 * chunk == lanes else 0):
        even = back_ref[2 * tile]
        odd = back_ref[2 * tile + 1]
        inside = lane < chunk
        left_ref[:, tile * lanes : (tile + 1) * lanes] = jnp.where(inside, even, odd)
        right = turn(jnp.where(inside, odd, even), chunk)
        right_ref[:, tile * lanes : (tile + 1) * lanes] = right
    for tile in range(0 if 2 * chunk == lanes else half // lanes):
        left = None
        right = None
        for index in range(tile * lanes // chunk, (tile + 1) * lanes // chunk):
            offset = index * chunk % lanes
            values = back_ref[index]
            left_part = turn(values, offset)
            right_part = turn(values, offset - chunk)
            inside = lane >= offset
            left = left_part if left is None else jnp.where(inside, left_part, left)
            right = right_part if right is None else jnp.where(inside, right_part, right)
        left_ref[:, tile * lanes : (tile + 1) * lanes] = left
        right_ref[:, tile * lanes : (tile + 1) * lanes] = right
    weights, couple = layer_terms(weight_ref, half // lanes, 1)
    near = row_values(ends[0], (rows, lanes))
    odd = lax.broadcasted_iota(jnp.int32, (rows, half), 0) % 2 == 1
    sum_ref[...] = left_ref[...] + right_ref[...]
    right_ref[...] = left_ref[...] - right_ref[...]

    def row_of(ref, layer):
        return jnp.broadcast_to(ref[pl.ds(layer, 1), :], (rows, half))

    def source(layer):
        factors = jnp.concatenate([weight_ref[layer] * near] * (half // lanes), axis=1)
        return factors * jnp.where(odd, row_of(sum_ref, layer), row_of(right_ref, layer))

    edge_row = lax.broadcasted_iota(jnp.int32, (rows, half), 0) == 0
    place = side * depth
    found = [None] * depth

    def emit(layer, values):
        layer_here = layer - place
        total = solved_ref[layer_here] + values
        found[layer_here] = jnp.where(edge_row, row_of(left_ref, layer), total)

    substitute(couple, inverse_ref, partial_ref, source, emit, side)
    modes = jnp.stack(found)
    sine, _ = parts_of(small_ref, depth * rows, depth)
    waves = from_modes(modes, sine)
    cells = dot3(split(waves), table, (((1,), (0 if turned else 1,)), ((), ())))
    return cells.reshape(depth, rows, half)


def restore_kernel(
    dep_ref,
    back_ref,
    solved_ref,
    table_ref,
    small_ref,
    weight_ref,
    inverse_ref,
    bins_ref,
    both_ref,
    base_ref,
    gain_ref,
    turned_ref,
    *scratch,
    ends,
    scale,
):
    half = solved_ref.shape[-1]

    def work(side):
        sign = scale if side else -scale
        left = focusing(bins_ref[:, :, :half]) * scale
        right = focusing(bins_ref[:, :, half:]) * sign
        gain_ref[:, :, :half] = left
        gain_ref[:, :, half:] = right
        table = (table_ref[0], table_ref[1])
        cells = extend(
            side, back_ref, solved_ref, table, small_ref, weight_ref, inverse_ref, *scratch, ends
        )
        base_ref[:, :, :half] = gain_ref[:, :, :half] * cells
        base_ref[:, :, half:] = -(gain_ref[:, :, half:] * cells)
        for part in range(2):
            turned_ref[part] = both_ref[1 - side, part].T

    pl.when(dep_ref[0] == 0)(lambda: work(0))
    pl.when(dep_ref[0] == 1)(lambda: work(1))


def unfold_kernel(
    dep_ref,
    back_ref,
    solved_ref,
    table_ref,
    small_ref,
    weight_ref,
    inverse_ref,
    base_ref,
    gain_ref,
    out_hbm,
    out_ref,
    sems,
    *scratch,
    ends,
    cuts,
):
    depth, _, half = solved_ref.shape
    size = depth // cuts

    def work(side):
        table = (table_ref[0], table_ref[1])
        cells = extend(
            side,
            back_ref,
            solved_ref,
            table,
            small_ref,
            weight_ref,
            inverse_ref,
            *scratch,
            ends,
            True,
        )
        copies = []
        for cut in range(cuts):
            part = slice(cut * size, (cut + 1) * size)
            for ends_here in (slice(0, half), slice(half, 2 * half)):
                out_ref[part, :, ends_here] = (
                    base_ref[part, :, ends_here] + gain_ref[part, :, ends_here] * cells[part]
                )
            copy = pltpu.make_async_copy(out_ref.at[part], out_hbm.at[part], sems.at[cut])
            copy.start()
            copies.append(copy)
        for copy in copies:
            copy.wait()

    pl.when(dep_ref[0] == 0)(lambda: work(0))
    pl.when(dep_ref[0] == 1)(lambda: work(1))


def call(kernel, operands, out_shape, scratch=(), outside=False):
    specs = []
    values = []
    for space, value in operands:
        specs.append(pl.BlockSpec(memory_space=space))
        if space is pltpu.HBM:
            value = pltpu.with_memory_space_constraint(value, pltpu.HBM)
        values.append(value)
    out_space = pltpu.HBM if outside else pltpu.VMEM
    single = not isinstance(out_shape, list)
    out_specs = pl.BlockSpec(memory_space=out_space)
    return pl.pallas_call(
        kernel,
        in_specs=specs,
        out_specs=out_specs if single else [out_specs] * len(out_shape),
        out_shape=out_shape,
        scratch_shapes=list(scratch),
        compiler_params=pltpu.CompilerParams(vmem_limit_bytes=16 * 1024 * 1024),
    )(*values)


def body(residual, focus_bins, layer_class):
    depth, rows, x_cells = residual.shape
    half = x_cells // 2
    layers = layer_class.shape[0]
    hor_count = lax.axis_size("hor")
    y_cells = rows * hor_count
    chunk = half // hor_count
    plane_rows = rows * half // lanes
    dep = lax.axis_index("dep").astype(jnp.int32)
    hor = lax.axis_index("hor").astype(jnp.int32)
    dep_index = dep.reshape(1)
    spot = (hor * 2 + dep).reshape(1)

    table = np.stack(fold_tables(x_cells), axis=1)
    sine = sine_matrix(rows)
    near = np.concatenate([[0.0], sine[1, 1:]])
    far = np.concatenate([[0.0], sine[rows - 1, 1:]])
    lower_row = np.concatenate([[1.0], sine[1, 1:]])
    edge = np.concatenate([np.kron(np.eye(depth), row[None, :]) for row in (lower_row, far)])
    high, low = split_table(np.concatenate([np.kron(np.eye(depth), sine), edge]))
    small = np.concatenate([high, high, low], axis=1)
    wave_x = np.stack(
        [symbol_of(2.0 * np.pi * (2 * np.arange(half) + parity) / x_cells) for parity in range(2)]
    )
    mode = symbol_of(np.pi * np.arange(rows) / rows)
    inner = damping + smoothing * (mode[None, :, None] + wave_x[:, None, :])
    lane = np.arange(lanes)
    wave_number = (lane // chunk)[None, :] * plane_rows + np.arange(plane_rows)[:, None]
    wave_y = symbol_of(2.0 * np.pi * wave_number / y_cells)
    spots = np.arange(hor_count)[:, None, None] * chunk + (lane % chunk)[None, None, :]
    spots = 2 * spots + np.arange(2)[None, :, None]
    wave_spots = symbol_of(2.0 * np.pi * spots / x_cells).reshape(2 * hor_count, lanes)
    outer = np.concatenate([wave_y, wave_spots]).astype(np.float32)

    def shape(*dims):
        return jax.ShapeDtypeStruct(dims, f32)

    def constant(value):
        return (pltpu.HBM, jnp.asarray(value))

    def scalar(value):
        return (pltpu.SMEM, value)

    def near_by(value):
        return (pltpu.VMEM, value)

    slab = (depth, rows, half)
    full = (depth, rows, x_cells)
    field = (layers, rows, half)
    packed = (hor_count, layers, lanes)
    plane = (layers, plane_rows, lanes)
    cuts = 4
    own, send, weight, small_here, inner_here, outer_here = call(
        functools.partial(fold_kernel, cuts=cuts // 2),
        [scalar(dep_index)]
        + [(pltpu.HBM, value) for value in (residual, focus_bins, layer_class)]
        + [constant(value) for value in (small, inner.astype(np.float32), outer)],
        [
            shape(*slab),
            shape(*slab),
            shape(layers, 8, lanes),
            jax.ShapeDtypeStruct(small.shape, bf16),
            shape(2, rows, half),
            shape(*outer.shape),
        ],
        [
            pltpu.VMEM(full, f32),
            pltpu.VMEM(full, jnp.int32),
            pltpu.SMEM((layers,), jnp.int32),
            pltpu.SemaphoreType.DMA((2, cuts // 2)),
            pltpu.SemaphoreType.DMA,
            pltpu.SemaphoreType.DMA((3,)),
        ],
    )
    pairs = [(0, 1), (1, 0)]
    recv = lax.ppermute(send, "dep", pairs)
    modes, table_here, inverse, inverse_other, inverse_outer = call(
        prepare_kernel,
        [scalar(dep_index), scalar(spot), near_by(own), near_by(weight), constant(table)]
        + [near_by(value) for value in (small_here, inner_here, outer_here)],
        [
            shape(*slab),
            jax.ShapeDtypeStruct((2, half, half), bf16),
            shape(*field),
            shape(*field),
            shape(*plane),
        ],
        [pltpu.SemaphoreType.DMA((2,))],
    )
    outgoing, keep, give = call(
        interior_kernel,
        [scalar(dep_index)]
        + [near_by(v) for v in (modes, recv, table_here, small_here, weight, inverse)],
        [shape(*packed), shape(*slab), shape(*slab)],
        [pltpu.VMEM(field, f32)],
    )
    got = lax.ppermute(give, "dep", pairs)
    incoming = lax.all_to_all(outgoing, "hor", split_axis=0, concat_axis=0, tiled=True)
    incoming, got = lax.optimization_barrier((incoming, got))
    answered = call(
        functools.partial(interface_kernel, chunk=chunk),
        [scalar(spot), near_by(incoming), near_by(weight), near_by(inverse_outer)],
        shape(*packed),
        [pltpu.VMEM(packed, f32)] * 3 + [pltpu.VMEM(plane, f32)],
    )
    edges = lax.all_to_all(answered, "hor", split_axis=0, concat_axis=0, tiled=True)
    other_edges = lax.ppermute(edges, "dep", pairs)
    scratch = [pltpu.VMEM((layers, half), f32)] * 3 + [pltpu.VMEM(field, f32)]
    both = jnp.asarray(table)
    base, gain, turned = call(
        functools.partial(restore_kernel, ends=(near,), scale=1.0 / x_cells),
        [scalar(dep_index)]
        + [
            near_by(v)
            for v in (edges, keep, table_here, small_here, weight, inverse, focus_bins, both)
        ],
        [shape(*full)] * 2 + [jax.ShapeDtypeStruct((2, half, half), bf16)],
        scratch,
    )
    return call(
        functools.partial(unfold_kernel, ends=(near,), cuts=cuts),
        [scalar(dep_index)]
        + [
            near_by(v)
            for v in (
                other_edges,
                got,
                turned,
                small_here,
                weight,
                inverse_other,
                base,
                gain,
            )
        ],
        shape(*full),
        [pltpu.VMEM(full, f32), pltpu.SemaphoreType.DMA((cuts,))] + scratch,
        outside=True,
    )


def solution(mesh):
    return jax.shard_map(
        body,
        mesh=mesh,
        in_specs=(P(("grp", "dep"), "hor", None), P(("grp", "dep"), "hor", None), P("grp")),
        out_specs=P(("grp", "dep"), "hor", None),
        check_vma=False,
    )
```
